32 devices in a mesh: row: 4 (over y, core), col: 8 (over z, x).
Axes of the slice: x: 2, y: 2, z: 4, core: 2. Of those that a mesh axis runs over, the one named last changes fastest.
Arguments:
- support_views: float32 [256, 4, 3, 1024], P(('row', 'col')), may hold values from -6 to 6
- support_pick: int32 [256], P(('row', 'col')), may hold values from 0 to 3
- target_views: float32 [256, 4, 3, 1024], P(('row', 'col')), may hold values from -6 to 6
- target_pick: int32 [256], P(('row', 'col')), may hold values from 0 to 3
- support_labels: float32 [256, 10], P(('row', 'col')), may hold values from -6 to 6
- target_labels: int32 [256], replicated, may hold values from 0 to 9
Outputs:
- support_grad: float32 [256, 3, 1024], P(('row', 'col'))
- label_grad: float32 [256, 10], P(('row', 'col'))
- loss: float32 [], replicated
The draws below stay inside these ranges and needn't reach their ends.
All inputs are finite; a program needn't handle non-finite values.
Results may differ from the reference program's by a relative error of at most 0.00055.
Values sent between devices are 32-bit elements; how exact they have to be, the bound alone decides.
No kernel may reach another device: no remote copies, remote signals or barrier semaphores. Data moves between devices by JAX's collectives and lax.ppermute only.
A program may use at most 64 MiB of HBM per device.

```python
import jax
import jax.numpy as jnp
from jax import lax

SIDE = 32
PIX = 1024
CHANNELS = 3
LAYERS = 3
CLASSES = 10
VIEWS = 4
SUPPORT = 256
TARGETS = 256


def set_ends(array, key, least, largest):
    index_at = [jax.random.randint(jax.random.fold_in(key, axis), (), 0, length) for axis, length in enumerate(array.shape)]
    longest = array.shape.index(max(array.shape))
    beside = index_at[:longest] + [(index_at[longest] + 1) % array.shape[longest]] + index_at[longest + 1:]
    return array.at[tuple(index_at)].set(least).at[tuple(beside)].set(largest)


def shard_levels(own_key, shape, cuts, low, largest):
    def one(dim, parts):
        heights = jax.random.uniform(jax.random.fold_in(jax.random.fold_in(own_key, 6), dim), (parts,), jnp.float32, low / len(cuts), largest / len(cuts))
        return jnp.repeat(jnp.exp(heights), shape[dim] // parts).reshape((-1,) + (1,) * (len(shape) - dim - 1))

    gain = one(*cuts[0])
    for cut in cuts[1:]:
        gain = gain * one(*cut)
    return gain


def scatter_about(rng, shape, width, bound, cuts=(), kind=jnp.bfloat16):
    loudness = shard_levels(rng, shape, cuts, -0.22, 0.18) if cuts else 1.0
    array = jax.random.normal(rng, shape, jnp.float32) * width * loudness
    return jnp.minimum(jnp.maximum(array, -bound), bound).astype(kind)


def setup_inputs(seed: int = 0) -> dict:
    keys = jax.random.split(jax.random.key(seed), 7)
    return {
        "support_views": scatter_about(keys[0], (SUPPORT, VIEWS, CHANNELS, PIX), 1.0, 6.0, ((0, 32),), jnp.float32),
        "support_pick": set_ends(jax.random.randint(keys[1], (SUPPORT,), 0, VIEWS), jax.random.fold_in(keys[1], 1), 0, VIEWS - 1).astype(jnp.int32),
        "target_views": scatter_about(keys[2], (TARGETS, VIEWS, CHANNELS, PIX), 1.0, 6.0, ((0, 32),), jnp.float32),
        "target_pick": set_ends(jax.random.randint(keys[3], (TARGETS,), 0, VIEWS), jax.random.fold_in(keys[3], 1), 0, VIEWS - 1).astype(jnp.int32),
        "support_labels": scatter_about(keys[4], (SUPPORT, CLASSES), 1.0, 6.0, ((0, 32),), jnp.float32),
        "target_labels": set_ends(jax.random.randint(keys[5], (TARGETS,), 0, CLASSES), jax.random.fold_in(keys[5], 1), 0, CLASSES - 1).astype(jnp.int32),
    }


bias_variance = 0.1
ridge_scale = 0.1
highest = lax.Precision.HIGHEST

def shifted(surface, offset):
    extent = surface.shape[-1]
    padding = jnp.zeros(surface.shape[:-1] + (abs(offset),), surface.dtype)
    if offset > 0:
        return jnp.concatenate([surface[..., offset:], padding], axis=-1)
    return jnp.concatenate([padding, surface[..., :extent + offset]], axis=-1)

def average(surface):
    column = jnp.arange(surface.shape[-1], dtype=jnp.int32) % SIDE
    rightward = jnp.where(column < SIDE - 1, shifted(surface, 1), 0.0)
    leftward = jnp.where(column > 0, shifted(surface, -1), 0.0)
    across = surface + leftward + rightward
    return (across + shifted(across, SIDE) + shifted(across, -SIDE)) / 9.0

def choose_view(views, picked):
    options = jnp.arange(views.shape[1], dtype=jnp.int32)
    selector = (picked[:, None] == options[None, :]).astype(jnp.float32)
    return lax.optimization_barrier(jnp.sum(selector[:, :, None, None] * views, axis=1))

def self_maps(images):
    energy = lax.optimization_barrier(jnp.sum(images * images, axis=1)) / images.shape[1]
    current = average(energy) + bias_variance
    stacked = [current]
    for layer in range(1, LAYERS):
        current = average(current) + bias_variance
        stacked.append(current)
    return jnp.stack(stacked, axis=1)

def self_back(images, grad_maps):
    carry = grad_maps[:, -1]
    for layer in range(grad_maps.shape[1] - 2, -1, -1):
        carry = grad_maps[:, layer] + average(carry)
    return average(carry)[:, None, :] * images * (2.0 / images.shape[1])

def arc(kernel_map, first_diag, second_diag):
    scale_map = jnp.sqrt(first_diag * second_diag)
    cosine = jnp.clip(kernel_map / scale_map, -1.0, 1.0)
    sine = jnp.sqrt(1.0 - cosine * cosine)
    angle = jnp.arccos(cosine)
    value = scale_map * (sine + (jnp.pi - angle) * cosine) / jnp.pi
    slope = (jnp.pi - angle) / jnp.pi
    spread = scale_map * sine / (2.0 * jnp.pi)
    return (value, slope, spread)

def pair_forward(first, first_maps, second, second_maps):
    product = first[:, None, 0] * second[None, :, 0]
    for channel in range(1, first.shape[1]):
        product = product + first[:, None, channel] * second[None, :, channel]
    current = average(product / first.shape[1]) + bias_variance
    slopes = []
    spreads = []
    depth = first_maps.shape[1]
    for layer in range(depth):
        value, slope, spread = arc(current, first_maps[:, None, layer], second_maps[None, :, layer])
        slopes.append(slope)
        spreads.append(spread)
        if layer + 1 < depth:
            current = average(value) + bias_variance
    return (lax.optimization_barrier(jnp.mean(value, axis=-1)), slopes, spreads)

def pair_backward(first, first_maps, second, second_maps, weights, want_second):
    kernel, slopes, spreads = pair_forward(first, first_maps, second, second_maps)
    depth = first_maps.shape[1]
    grad = jnp.broadcast_to(weights[:, :, None] / first.shape[-1], slopes[0].shape)
    first_parts = []
    second_parts = []
    for layer in range(depth - 1, -1, -1):
        scaled = grad * spreads[layer]
        first_parts.insert(0, lax.optimization_barrier(jnp.sum(scaled, axis=1)) / first_maps[:, layer])
        if want_second:
            second_parts.insert(0, lax.optimization_barrier(jnp.sum(scaled, axis=0)) / second_maps[:, layer])
        grad = average(grad * slopes[layer])
    first_image = jnp.stack([lax.optimization_barrier(jnp.sum(grad * second[None, :, channel], axis=1)) for channel in range(first.shape[1])], axis=1) / first.shape[1]
    if not want_second:
        return (first_image, jnp.stack(first_parts, axis=1), None, None)
    second_image = jnp.stack([lax.optimization_barrier(jnp.sum(grad * first[:, None, channel], axis=0)) for channel in range(first.shape[1])], axis=1) / first.shape[1]
    return (first_image, jnp.stack(first_parts, axis=1), second_image, jnp.stack(second_parts, axis=1))

def solve_with(factor, rhs):
    halfway = lax.linalg.triangular_solve(factor, rhs, left_side=True, lower=True)
    return lax.linalg.triangular_solve(factor, halfway, left_side=True, lower=True, transpose_a=True)

def reference(support_views, support_pick, target_views, target_pick, support_labels, target_labels):
    support = choose_view(support_views, support_pick)
    targets = choose_view(target_views, target_pick)
    support_maps = self_maps(support)
    target_maps = self_maps(targets)
    block_rows = 8
    block_count = SUPPORT // block_rows
    support_blocks = support.reshape(block_count, block_rows, CHANNELS, PIX)
    map_blocks = support_maps.reshape(block_count, block_rows, LAYERS, PIX)

    def forward_block(inputs):
        block, block_maps = inputs
        inner, _, _ = pair_forward(block, block_maps, support, support_maps)
        outer, _, _ = pair_forward(block, block_maps, targets, target_maps)
        return (inner, outer)
    inner, outer = lax.map(forward_block, (support_blocks, map_blocks))
    support_kernel = inner.reshape(SUPPORT, SUPPORT)
    cross_kernel = outer.reshape(SUPPORT, TARGETS)
    identity = jnp.eye(SUPPORT, dtype=jnp.float32)
    trace_mean = jnp.trace(support_kernel) / SUPPORT
    system = support_kernel + ridge_scale * trace_mean * identity
    factor = jnp.linalg.cholesky(system)
    alpha = solve_with(factor, support_labels)
    onehot = (target_labels[:, None] == jnp.arange(CLASSES, dtype=jnp.int32)[None, :]).astype(jnp.float32) - 1.0 / CLASSES
    predicted = jnp.dot(cross_kernel.T, alpha, precision=highest)
    error = predicted - onehot
    loss = 0.5 * jnp.sum(error * error)
    adjoint = jnp.dot(cross_kernel, error, precision=highest)
    gamma = solve_with(factor, adjoint)
    intersection = jnp.sum(gamma * alpha)
    cross_weights = jnp.dot(alpha, error.T, precision=highest)
    support_weights = -jnp.dot(gamma, alpha.T, precision=highest) - ridge_scale * intersection / SUPPORT * identity

    def backward_block(carry, inputs):
        block, block_maps, inner_weights, outer_weights = inputs
        grad_one, maps_one, grad_two, maps_two = pair_backward(block, block_maps, support, support_maps, inner_weights, True)
        grad_three, maps_three, _, _ = pair_backward(block, block_maps, targets, target_maps, outer_weights, False)
        column_images, column_maps = carry
        return ((column_images + grad_two, column_maps + maps_two), (grad_one + grad_three, maps_one + maps_three))
    start = (jnp.zeros((SUPPORT, CHANNELS, PIX), jnp.float32), jnp.zeros((SUPPORT, LAYERS, PIX), jnp.float32))
    (column_images, column_maps), (row_images, row_maps) = lax.scan(backward_block, start, (support_blocks, map_blocks, support_weights.reshape(block_count, block_rows, SUPPORT), cross_weights.reshape(block_count, block_rows, TARGETS)))
    image_grad = row_images.reshape(SUPPORT, CHANNELS, PIX) + column_images
    map_grad = row_maps.reshape(SUPPORT, LAYERS, PIX) + column_maps
    support_grad = image_grad + self_back(support, map_grad)
    return (support_grad, gamma, loss)
```

```python
import math

import jax
import jax.numpy as jnp
from jax import lax
from jax.experimental import pallas as pl
from jax.experimental.pallas import tpu as pltpu
from jax.sharding import PartitionSpec as P

LAYERS = 3
LANES = 128
SUBLANES = 8
BATCHES = 4
ROWS = 1
RING = 4

bias_variance = 0.1
ridge_scale = 0.1
highest = lax.Precision.HIGHEST
tiny = 1e-30
PI = math.pi

ACOS = (
    1.4142137164552202,
    0.11783707507052552,
    0.026725055357041356,
    0.00674552756719407,
    0.005608499939250727,
    -0.0026297111285195295,
    0.002296009448189848,
)
SINE = (
    0.31830981148327425,
    0.032252498831491,
    0.001158328114192081,
    2.2834735017183973e-05,
)
AXES = ("row", "col")


def horner(coefficients, x):
    total = coefficients[-1] * x + coefficients[-2]
    for coefficient in coefficients[-3::-1]:
        total = total * x + coefficient
    return total


def choose_view(views, picked):
    options = jnp.arange(views.shape[1], dtype=jnp.int32)
    selector = (picked[:, None] == options[None, :]).astype(jnp.float32)
    return jnp.sum(selector[:, :, None, None] * views, axis=1)


def edges(side, shape):
    x = lax.broadcasted_iota(jnp.int32, shape, len(shape) - 1) % side
    return x > 0, x < side - 1


def across(surface, masks):
    axis = surface.ndim - 1
    left = jnp.where(masks[0], pltpu.roll(surface, 1, axis), 0.0)
    right = jnp.where(masks[1], pltpu.roll(surface, LANES - 1, axis), 0.0)
    return surface + left + right


def map_scale(channels, layer):
    return 9.0 * channels if layer == 0 else 9.0


def prepare_kernel(side, channels, image_ref, *refs):
    outs = refs[:LAYERS]
    sums_ref = refs[LAYERS]
    masks = edges(side, image_ref.shape[3:])
    groups = image_ref.shape[2]
    blank = jnp.zeros(sums_ref.shape[2:], jnp.float32)
    for layer in range(LAYERS):
        sums_ref[layer, 0] = blank
        sums_ref[layer, side + 1] = blank

    def energy(y, carry):
        for g in range(groups):
            total = None
            for c in range(channels):
                plane = image_ref[c, y, g]
                total = plane * plane if total is None else total + plane * plane
            sums_ref[0, y + 1, g] = across(total, masks)
        return carry

    lax.fori_loop(0, side, energy, 0)
    for layer in range(LAYERS):
        scale = map_scale(channels, layer)

        def one_row(y, carry, layer=layer, scale=scale):
            for g in range(groups):
                total = sums_ref[layer, y, g] + sums_ref[layer, y + 1, g] + sums_ref[layer, y + 2, g]
                current = total * (1.0 / scale) + bias_variance
                inverse = lax.rsqrt(current)
                outs[layer][y, 0, g] = inverse * (1.0 / scale)
                outs[layer][y, 1, g] = current * inverse * (1.0 / PI)
                if layer + 1 < LAYERS:
                    sums_ref[layer + 1, y + 1, g] = across(current, masks)
            return carry

        lax.fori_loop(0, side, one_row, 0)


def prepare_rows(u_images):
    channels, side, groups, _, _ = u_images.shape
    f32 = jnp.float32
    shape = jax.ShapeDtypeStruct((side, 2, groups, SUBLANES, LANES), f32)
    return pl.pallas_call(
        lambda *refs: prepare_kernel(side, channels, *refs),
        out_shape=[shape] * LAYERS,
        scratch_shapes=[pltpu.VMEM((LAYERS, side + 2, groups, SUBLANES, LANES), f32)],
        name="prepare_rows",
    )(u_images)


def forward_kernel(side, channels, groups, packs, *refs):
    u_ref, v_ref = refs[0], refs[1]
    u_map_refs = refs[2 : 2 + LAYERS]
    outs = refs[2 + LAYERS :]
    angle_refs = outs[:LAYERS]
    root_refs = outs[LAYERS : 2 * LAYERS]
    tile_ref = outs[2 * LAYERS]
    sums_ref, own_sums_ref, total_ref = outs[2 * LAYERS + 1 :]
    step = pl.program_id(0)
    steps = side // ROWS
    masks = edges(side, (SUBLANES, LANES))
    own_masks = edges(side, (packs, LANES))

    def slot(row):
        return row & (RING - 1)

    def spread(line):
        return jnp.broadcast_to(line, (SUBLANES, LANES))

    @pl.when(step == 0)
    def _():
        total_ref[...] = jnp.zeros(total_ref.shape, jnp.float32)
        for layer in range(LAYERS):
            sums_ref[layer, RING - 1] = jnp.zeros(sums_ref.shape[2:], jnp.float32)
            own_sums_ref[layer, RING - 1] = jnp.zeros(own_sums_ref.shape[2:], jnp.float32)

    for layer in range(LAYERS):

        @pl.when(step == steps + layer)
        def _(layer=layer):
            sums_ref[layer, slot(side)] = jnp.zeros(sums_ref.shape[2:], jnp.float32)
            own_sums_ref[layer, slot(side)] = jnp.zeros(own_sums_ref.shape[2:], jnp.float32)

    @pl.when(step < steps)
    def _():
        for r in range(ROWS):
            where = slot(step * ROWS + r)
            energy = None
            for c in range(channels):
                plane = v_ref[c, r]
                energy = plane * plane if energy is None else energy + plane * plane
            own_sums_ref[0, where] = across(energy, own_masks)
            for pack in range(packs):
                lines = [spread(v_ref[c, r, pack : pack + 1, :]) for c in range(channels)]
                for g in range(groups):
                    product = None
                    for c in range(channels):
                        part = u_ref[c, r, g] * lines[c]
                        product = part if product is None else product + part
                    sums_ref[0, where, pack * groups + g] = across(product, masks)

    def arc_stage(layer):
        scale = map_scale(channels, layer)
        offset = scale * bias_variance
        for r in range(ROWS):
            row = (step - 1 - layer) * ROWS + r
            near = [slot(row - 1), slot(row), slot(row + 1)]
            own_total = own_sums_ref[layer, near[0]] + own_sums_ref[layer, near[1]] + own_sums_ref[layer, near[2]]
            own_map = own_total * (1.0 / scale) + bias_variance
            inverse = lax.rsqrt(own_map)
            root_of = own_map * inverse
            root_refs[layer][r] = root_of
            if layer + 1 < LAYERS:
                own_sums_ref[layer + 1, near[1]] = across(own_map, own_masks)
            for pack in range(packs):
                right_inverse = spread(inverse[pack : pack + 1, :])
                right_root = spread(root_of[pack : pack + 1, :])
                for g in range(groups):
                    at = pack * groups + g
                    summed = sums_ref[layer, near[0], at] + sums_ref[layer, near[1], at] + sums_ref[layer, near[2], at]
                    cosine = (summed + offset) * u_map_refs[layer][r, 0, g] * right_inverse
                    gap = 1.0 - (jnp.abs(cosine) if layer == 0 else cosine)
                    gap = jnp.maximum(gap, tiny)
                    theta = gap * lax.rsqrt(gap)
                    rest = 2.0 - gap
                    sine = theta * (rest * lax.rsqrt(rest))
                    theta = theta * horner(ACOS, gap)
                    angle = PI - theta
                    if layer == 0:
                        angle = jnp.where(cosine >= 0.0, angle, theta)
                    angle_refs[layer][r, at] = angle
                    value = (cosine * angle + sine) * u_map_refs[layer][r, 1, g] * right_root
                    if layer + 1 < LAYERS:
                        sums_ref[layer + 1, near[1], at] = across(value, masks)
                    else:
                        total_ref[at] += value

    for layer in range(LAYERS):
        pl.when((step > layer) & (step <= steps + layer))(lambda layer=layer: arc_stage(layer))

    @pl.when(step == steps + LAYERS - 1)
    def _():
        tile_ref[...] = total_ref[...]


def pair_forward(u_images, u_maps, v_rows):
    channels, side, groups, _, _ = u_images.shape
    packs = v_rows.shape[2]
    steps = side // ROWS
    f32 = jnp.float32

    def lag(layer, trailing):
        return lambda i: (jnp.clip(i - 1 - layer, 0, steps - 1),) + (0,) * trailing

    count = packs * groups
    return pl.pallas_call(
        lambda *refs: forward_kernel(side, channels, groups, packs, *refs),
        out_shape=[jax.ShapeDtypeStruct((side, count, SUBLANES, LANES), f32)] * LAYERS
        + [jax.ShapeDtypeStruct((side, packs, LANES), f32)] * LAYERS
        + [jax.ShapeDtypeStruct((count, SUBLANES, LANES), f32)],
        grid=(steps + LAYERS,),
        in_specs=[
            pl.BlockSpec(
                (channels, ROWS, groups, SUBLANES, LANES),
                lambda i: (0, jnp.minimum(i, steps - 1), 0, 0, 0),
            ),
            pl.BlockSpec((channels, ROWS, packs, LANES), lambda i: (0, jnp.minimum(i, steps - 1), 0, 0)),
        ]
        + [
            pl.BlockSpec((ROWS, 2, groups, SUBLANES, LANES), lag(layer, 4)) for layer in range(LAYERS)
        ],
        out_specs=[
            pl.BlockSpec((ROWS, count, SUBLANES, LANES), lag(layer, 3)) for layer in range(LAYERS)
        ]
        + [pl.BlockSpec((ROWS, packs, LANES), lag(layer, 2)) for layer in range(LAYERS)]
        + [pl.BlockSpec((count, SUBLANES, LANES), lambda i: (0, 0, 0))],
        scratch_shapes=[
            pltpu.VMEM((LAYERS, RING, count, SUBLANES, LANES), f32),
            pltpu.VMEM((LAYERS, RING, packs, LANES), f32),
            pltpu.VMEM((count, SUBLANES, LANES), f32),
        ],
        name="pair_forward",
    )(u_images, v_rows, *u_maps)


def backward_kernel(side, channels, groups, packs, batches, *refs):
    weight_ref, u_ref = refs[0], refs[1]
    u_map_refs = refs[2 : 2 + LAYERS]
    taken = 2 + LAYERS
    angle_refs, root_refs, image_refs = [], [], []
    for batch in range(batches):
        angle_refs.append(refs[taken : taken + LAYERS])
        root_refs.append(refs[taken + LAYERS : taken + 2 * LAYERS])
        image_refs.append(refs[taken + 2 * LAYERS])
        taken += 2 * LAYERS + 1
    grad_ref, sums_ref, own_sums_ref = refs[taken:]
    ring = sums_ref.shape[1]
    step = pl.program_id(0)
    masks = edges(side, (SUBLANES, LANES))
    shrink = 1.0 / (9.0 * PI)
    pixels = side * side

    def slot(row):
        return row & (ring - 1)

    def fold(total):
        total = total + pltpu.roll(total, 2 * side, 1)
        return total + pltpu.roll(total, side, 1)

    def spread(line):
        return jnp.broadcast_to(line, (SUBLANES, LANES))

    def summed(ref, depth, row, at):
        return ref[depth, slot(row - 1), at] + ref[depth, slot(row), at] + ref[depth, slot(row + 1), at]

    @pl.when(step == 0)
    def _():
        for depth in range(LAYERS):
            sums_ref[depth, ring - 1] = jnp.zeros(sums_ref.shape[2:], jnp.float32)
            own_sums_ref[depth, ring - 1] = jnp.zeros(own_sums_ref.shape[2:], jnp.float32)

    for depth in range(LAYERS):

        @pl.when(step == side + depth)
        def _(depth=depth):
            sums_ref[depth, slot(side)] = jnp.zeros(sums_ref.shape[2:], jnp.float32)
            own_sums_ref[depth, slot(side)] = jnp.zeros(own_sums_ref.shape[2:], jnp.float32)

    def layer_stage(depth):
        layer = LAYERS - 1 - depth
        row = step - depth
        totals = [None] * groups
        for batch in range(batches):
            for pack in range(packs):
                root = spread(root_refs[batch][layer][0, pack : pack + 1, :])
                for g in range(groups):
                    inner = pack * groups + g
                    at = batch * packs * groups + inner
                    grad = weight_ref[at] if depth == 0 else summed(sums_ref, depth - 1, row, at)
                    angle = angle_refs[batch][layer][0, inner]
                    product = angle * (PI - angle)
                    part = grad * root * (product * horner(SINE, product))
                    totals[g] = part if totals[g] is None else totals[g] + part
                    sums_ref[depth, slot(row), at] = across(grad * angle, masks)
        factor = shrink**depth / (pixels * 2.0 * PI * PI)
        for g in range(groups):
            carry = fold(totals[g]) * (factor / u_map_refs[layer][0, 1, g])
            if depth > 0:
                carry = carry + summed(own_sums_ref, depth - 1, row, g) * (1.0 / 9.0)
            own_sums_ref[depth, slot(row), g] = across(carry, masks)

    def image_stage():
        row = step - LAYERS
        totals = [[None] * groups for _ in range(channels)]
        for batch in range(batches):
            for pack in range(packs):
                lines = [spread(image_refs[batch][c, 0, pack : pack + 1, :]) for c in range(channels)]
                for g in range(groups):
                    at = (batch * packs + pack) * groups + g
                    grad = summed(sums_ref, LAYERS - 1, row, at)
                    for c in range(channels):
                        part = grad * lines[c]
                        totals[c][g] = part if totals[c][g] is None else totals[c][g] + part
        for g in range(groups):
            carry = summed(own_sums_ref, LAYERS - 1, row, g) * (2.0 / (9.0 * channels))
            for c in range(channels):
                full = fold(totals[c][g]) * (shrink**LAYERS / (pixels * channels)) + carry * u_ref[c, 0, g]
                grad_ref[0, c, g] = full[:, :side]

    for depth in range(LAYERS):
        pl.when((step >= depth) & (step < side + depth))(lambda depth=depth: layer_stage(depth))
    pl.when(step >= LAYERS)(image_stage)


def pair_backward(weights, u_images, u_maps, batches):
    channels, side, groups, _, _ = u_images.shape
    packs = batches[0][2].shape[2]
    count = packs * groups
    f32 = jnp.float32

    def rows(lag, trailing):
        return lambda i: (jnp.clip(i - lag, 0, side - 1),) + (0,) * trailing

    def image_rows(trailing):
        return lambda i: (0, jnp.clip(i - LAYERS, 0, side - 1)) + (0,) * trailing

    operands = [weights, u_images, *u_maps]
    in_specs = [
        pl.BlockSpec(weights.shape, lambda i: (0, 0, 0)),
        pl.BlockSpec((channels, 1, groups, SUBLANES, LANES), image_rows(3)),
    ] + [
        pl.BlockSpec((1, 2, groups, SUBLANES, LANES), rows(LAYERS - 1 - layer, 4))
        for layer in range(LAYERS)
    ]
    for angles, roots, images in batches:
        for layer in range(LAYERS):
            operands.append(angles[layer])
            in_specs.append(pl.BlockSpec((1, count, SUBLANES, LANES), rows(LAYERS - 1 - layer, 3)))
        for layer in range(LAYERS):
            operands.append(roots[layer])
            in_specs.append(pl.BlockSpec((1, packs, LANES), rows(LAYERS - 1 - layer, 2)))
        operands.append(images)
        in_specs.append(pl.BlockSpec((channels, 1, packs, LANES), image_rows(2)))
    return pl.pallas_call(
        lambda *refs: backward_kernel(side, channels, groups, packs, len(batches), *refs),
        out_shape=jax.ShapeDtypeStruct((side, channels, groups, SUBLANES, side), f32),
        grid=(side + LAYERS,),
        in_specs=in_specs,
        out_specs=pl.BlockSpec((1, channels, groups, SUBLANES, side), rows(LAYERS, 4)),
        scratch_shapes=[
            pltpu.VMEM((LAYERS, 4, count * len(batches), SUBLANES, LANES), f32),
            pltpu.VMEM((LAYERS, 4, groups, SUBLANES, LANES), f32),
        ],
        name="pair_backward",
    )(*operands)


def solve_with(factor, rhs):
    halfway = lax.linalg.triangular_solve(factor, rhs, left_side=True, lower=True)
    return lax.linalg.triangular_solve(factor, halfway, left_side=True, lower=True, transpose_a=True)


def body(support_views, support_pick, target_views, target_pick, support_labels, target_labels):
    own, _, channels, pixels = support_views.shape
    side = math.isqrt(pixels)
    copies = LANES // side
    classes = support_labels.shape[1]
    row_count = lax.axis_size("row")
    col_count = lax.axis_size("col")
    row_index = lax.axis_index("row")
    col_index = lax.axis_index("col")
    own_support = choose_view(support_views, support_pick)
    own_target = choose_view(target_views, target_pick)

    both = jnp.stack([own_support, own_target]).reshape(2 * own, channels, side, side)
    chunk = jnp.transpose(both, (1, 2, 0, 3)).reshape(channels, side, 2 * own * side)
    chunks = [chunk]
    for d in range(1, col_count):
        pairs = [((i + d) % col_count, i) for i in range(col_count)]
        chunks.append(lax.ppermute(chunk, "col", pairs))
    per_batch = col_count // BATCHES
    v_rows = []
    for batch in range(BATCHES):
        taken = jnp.concatenate(chunks[batch * per_batch : (batch + 1) * per_batch], axis=-1)
        v_rows.append(taken.reshape(channels, side, -1, LANES))
    packs = v_rows[0].shape[2]

    row_images = lax.all_gather(own_support, "row", axis=0, tiled=True)
    groups = row_images.shape[0] // SUBLANES
    u_images = jnp.transpose(
        row_images.reshape(groups, SUBLANES, channels, side, side), (2, 3, 0, 1, 4)
    )
    u_images = jnp.tile(u_images, (1, 1, 1, 1, copies))
    u_maps = prepare_rows(u_images)
    batches = []
    tiles = []
    for batch in range(BATCHES):
        results = pair_forward(u_images, u_maps, v_rows[batch])
        batches.append((results[:LAYERS], results[LAYERS : 2 * LAYERS], v_rows[batch]))
        tiles.append(results[-1])
    lane_group = (
        jnp.arange(LANES, dtype=jnp.int32)[:, None] // side == jnp.arange(copies, dtype=jnp.int32)
    ).astype(jnp.float32)
    tile = jnp.dot(
        jnp.stack(tiles).reshape(-1, LANES), lane_group * (1.0 / pixels), precision=highest
    )
    tile = tile.reshape(BATCHES * packs, groups * SUBLANES, copies)
    tile = jnp.transpose(tile, (0, 2, 1)).reshape(col_count, 2, own, groups * SUBLANES)
    tile = lax.dynamic_slice_in_dim(
        jnp.concatenate([tile, tile], axis=0), (col_count - col_index) % col_count, col_count, 0
    )
    everywhere = row_count * col_count
    count = everywhere * own
    kernels = lax.all_gather(tile.reshape(1, -1, groups * SUBLANES), AXES, axis=0, tiled=True)
    kernels = kernels.reshape(row_count, col_count, col_count, 2, own, row_count * own)
    kernels = jnp.transpose(kernels, (3, 2, 0, 4, 1, 5)).reshape(2, count, count)
    labels = lax.all_gather(support_labels, ("col", "row"), axis=0, tiled=True)
    support_kernel, cross_kernel = kernels[0], kernels[1].T
    classes_of = jnp.transpose(target_labels.reshape(row_count, col_count, own), (1, 0, 2)).reshape(-1)
    identity = jnp.eye(count, dtype=jnp.float32)
    trace_mean = jnp.trace(support_kernel) / count
    factor = jnp.linalg.cholesky(support_kernel + ridge_scale * trace_mean * identity)
    alpha = solve_with(factor, labels)
    onehot = (classes_of[:, None] == jnp.arange(classes, dtype=jnp.int32)[None, :]).astype(
        jnp.float32
    ) - 1.0 / classes
    error = jnp.dot(cross_kernel.T, alpha, precision=highest) - onehot
    loss = 0.5 * jnp.sum(error * error)
    gamma = solve_with(factor, jnp.dot(cross_kernel, error, precision=highest))
    intersection = jnp.sum(gamma * alpha)

    def rows_here(matrix):
        return lax.dynamic_slice_in_dim(matrix, col_index * row_count * own, row_count * own, 0)

    def columns_here(matrix):
        shaped = matrix.reshape(col_count, row_count, own, -1)
        shaped = lax.dynamic_index_in_dim(shaped, row_index, 1, keepdims=False)
        return lax.dynamic_slice_in_dim(
            jnp.concatenate([shaped, shaped], axis=0), col_index, col_count, 0
        )

    alpha_rows, gamma_rows = rows_here(alpha), rows_here(gamma)
    left = jnp.concatenate([columns_here(gamma), columns_here(alpha)], axis=-1).reshape(-1, 2 * classes)
    right = jnp.concatenate([alpha_rows, gamma_rows], axis=-1)
    pair_weights = -jnp.dot(left, right.T, precision=highest).reshape(col_count, own, row_count, own)
    same = (
        (jnp.arange(col_count)[:, None, None, None] == 0)
        & (jnp.arange(row_count)[None, None, :, None] == row_index)
        & (jnp.arange(own)[None, :, None, None] == jnp.arange(own)[None, None, None, :])
    )
    pair_weights = pair_weights - jnp.where(same, 2.0 * ridge_scale * intersection / count, 0.0)
    cross_weights = jnp.dot(
        columns_here(error).reshape(-1, classes), alpha_rows.T, precision=highest
    ).reshape(col_count, own, row_count, own)
    weights = jnp.stack([pair_weights, cross_weights], axis=1)
    weights = weights.reshape(BATCHES * packs, copies, groups, SUBLANES)
    weights = jnp.dot(
        jnp.transpose(weights, (0, 2, 3, 1)).reshape(-1, copies), lane_group.T, precision=highest
    ).reshape(-1, SUBLANES, LANES)
    grads = pair_backward(weights, u_images, u_maps, batches)
    grads = jnp.transpose(grads, (2, 3, 1, 0, 4)).reshape(row_count * own, channels, pixels)
    support_grad = lax.psum_scatter(grads, "row", scatter_dimension=0, tiled=True)
    start = (col_index * row_count + row_index) * own
    return (support_grad, lax.dynamic_slice_in_dim(gamma, start, own, 0), loss)


def solution(mesh):
    return jax.shard_map(
        body,
        mesh=mesh,
        in_specs=(
            P(AXES, None, None, None),
            P(AXES),
            P(AXES, None, None, None),
            P(AXES),
            P(AXES, None),
            P(),
        ),
        out_specs=(P(AXES, None, None), P(AXES, None), P()),
        check_vma=False,
    )
```

```python
import math

import jax
import jax.numpy as jnp
from jax import lax
from jax.experimental import pallas as pl
from jax.experimental.pallas import tpu as pltpu
from jax.sharding import PartitionSpec as P

LAYERS = 3
LANES = 128
SUBLANES = 8
BATCHES = 4
UNROLL = 8
BLOCK = 32
ROWS = 1
RING = 4

bias_variance = 0.1
ridge_scale = 0.1
highest = lax.Precision.HIGHEST
tiny = 1e-30
PI = math.pi

ACOS = (
    1.4142137164552202,
    0.11783707507052552,
    0.026725055357041356,
    0.00674552756719407,
    0.005608499939250727,
    -0.0026297111285195295,
    0.002296009448189848,
)
SINE = (
    0.31830981148327425,
    0.032252498831491,
    0.001158328114192081,
    2.2834735017183973e-05,
)
AXES = ("row", "col")


def horner(coefficients, x):
    total = coefficients[-1] * x + coefficients[-2]
    for coefficient in coefficients[-3::-1]:
        total = total * x + coefficient
    return total


def choose_view(views, picked):
    options = jnp.arange(views.shape[1], dtype=jnp.int32)
    selector = (picked[:, None] == options[None, :]).astype(jnp.float32)
    return jnp.sum(selector[:, :, None, None] * views, axis=1)


def edges(side, shape):
    x = lax.broadcasted_iota(jnp.int32, shape, len(shape) - 1) % side
    return x > 0, x < side - 1


def across(surface, masks):
    axis = surface.ndim - 1
    left = jnp.where(masks[0], pltpu.roll(surface, 1, axis), 0.0)
    right = jnp.where(masks[1], pltpu.roll(surface, LANES - 1, axis), 0.0)
    return surface + left + right


def map_scale(channels, layer):
    return 9.0 * channels if layer == 0 else 9.0


def prepare_kernel(side, channels, image_ref, *refs):
    wide_ref = refs[0]
    outs = refs[1 : 1 + LAYERS]
    sums_ref = refs[1 + LAYERS]
    groups = image_ref.shape[2]
    masks = edges(side, (SUBLANES, LANES))
    blank = jnp.zeros(sums_ref.shape[2:], jnp.float32)
    for layer in range(LAYERS):
        sums_ref[layer, 0] = blank
        sums_ref[layer, side + 1] = blank

    def energy(y):
        for g in range(groups):
            total = None
            for c in range(channels):
                narrow = image_ref[c, y, g]
                plane = jnp.concatenate([narrow] * (LANES // side), axis=-1)
                wide_ref[c, y, g] = plane
                total = plane * plane if total is None else total + plane * plane
            sums_ref[0, y + 1, g] = across(total, masks)

    def one_row(layer, y):
        scale = map_scale(channels, layer)
        for g in range(groups):
            total = sums_ref[layer, y, g] + sums_ref[layer, y + 1, g] + sums_ref[layer, y + 2, g]
            current = total * (1.0 / scale) + bias_variance
            inverse = lax.rsqrt(current)
            outs[layer][y, 0, g] = inverse * (1.0 / scale)
            outs[layer][y, 1, g] = current * inverse * (1.0 / PI)
            if layer + 1 < LAYERS:
                sums_ref[layer + 1, y + 1, g] = across(current, masks)

    def sweep(action):
        def some_rows(i, carry):
            for r in range(UNROLL):
                action(i * UNROLL + r)
            return carry

        lax.fori_loop(0, side // UNROLL, some_rows, 0)

    sweep(energy)
    for layer in range(LAYERS):
        sweep(lambda y, layer=layer: one_row(layer, y))


def prepare_rows(images):
    channels, side, groups, _, _ = images.shape
    f32 = jnp.float32
    shape = jax.ShapeDtypeStruct((side, 2, groups, SUBLANES, LANES), f32)
    return pl.pallas_call(
        lambda *refs: prepare_kernel(side, channels, *refs),
        out_shape=[jax.ShapeDtypeStruct((channels, side, groups, SUBLANES, LANES), f32)]
        + [shape] * LAYERS,
        scratch_shapes=[pltpu.VMEM((LAYERS, side + 2, groups, SUBLANES, LANES), f32)],
        name="prepare_rows",
    )(images)


def forward_kernel(side, channels, groups, packs, first, *refs):
    u_ref, v_ref = refs[0], refs[1]
    u_map_refs = refs[2 : 2 + LAYERS]
    past_ref = refs[2 + LAYERS]
    outs = refs[3 + LAYERS :]
    angle_refs = outs[:LAYERS]
    root_refs = outs[LAYERS : 2 * LAYERS]
    tile_ref = outs[2 * LAYERS]
    sums_ref, own_sums_ref, total_ref = outs[2 * LAYERS + 1 :]
    step = pl.program_id(0)
    steps = side // ROWS
    masks = edges(side, (SUBLANES, LANES))
    own_masks = edges(side, (packs, LANES))

    def slot(row):
        return row & (RING - 1)

    def spread(line):
        return jnp.broadcast_to(line, (SUBLANES, LANES))

    @pl.when(step == 0)
    def _():
        total_ref[...] = jnp.zeros(total_ref.shape, jnp.float32)
        for layer in range(LAYERS):
            sums_ref[layer, RING - 1] = jnp.zeros(sums_ref.shape[2:], jnp.float32)
            own_sums_ref[layer, RING - 1] = jnp.zeros(own_sums_ref.shape[2:], jnp.float32)

    for layer in range(LAYERS):

        @pl.when(step == steps + layer)
        def _(layer=layer):
            sums_ref[layer, slot(side)] = jnp.zeros(sums_ref.shape[2:], jnp.float32)
            own_sums_ref[layer, slot(side)] = jnp.zeros(own_sums_ref.shape[2:], jnp.float32)

    @pl.when(step < steps)
    def _():
        for r in range(ROWS):
            where = slot(step * ROWS + r)
            energy = None
            for c in range(channels):
                plane = v_ref[c, r]
                energy = plane * plane if energy is None else energy + plane * plane
            own_sums_ref[0, where] = across(energy, own_masks)
            for pack in range(packs):
                lines = [spread(v_ref[c, r, pack : pack + 1, :]) for c in range(channels)]
                for g in range(groups):
                    product = None
                    for c in range(channels):
                        part = u_ref[c, r, g] * lines[c]
                        product = part if product is None else product + part
                    sums_ref[0, where, pack * groups + g] = across(product, masks)

    def arc_stage(layer):
        scale = map_scale(channels, layer)
        offset = scale * bias_variance
        for r in range(ROWS):
            row = (step - 1 - layer) * ROWS + r
            near = [slot(row - 1), slot(row), slot(row + 1)]
            own_total = own_sums_ref[layer, near[0]] + own_sums_ref[layer, near[1]] + own_sums_ref[layer, near[2]]
            own_map = own_total * (1.0 / scale) + bias_variance
            inverse = lax.rsqrt(own_map)
            root_of = own_map * inverse
            root_refs[layer][r] = root_of
            if layer + 1 < LAYERS:
                own_sums_ref[layer + 1, near[1]] = across(own_map, own_masks)
            for pack in range(packs):
                right_inverse = spread(inverse[pack : pack + 1, :])
                right_root = spread(root_of[pack : pack + 1, :])
                for g in range(groups):
                    at = pack * groups + g
                    summed = sums_ref[layer, near[0], at] + sums_ref[layer, near[1], at] + sums_ref[layer, near[2], at]
                    cosine = (summed + offset) * u_map_refs[layer][r, 0, g] * right_inverse
                    gap = 1.0 - (jnp.abs(cosine) if layer == 0 else cosine)
                    gap = jnp.maximum(gap, tiny)
                    theta = gap * lax.rsqrt(gap)
                    rest = 2.0 - gap
                    sine = theta * (rest * lax.rsqrt(rest))
                    theta = theta * horner(ACOS, gap)
                    angle = PI - theta
                    if layer == 0:
                        angle = jnp.where(cosine >= 0.0, angle, theta)
                    angle_refs[layer][r, at] = angle
                    value = (cosine * angle + sine) * u_map_refs[layer][r, 1, g] * right_root
                    if layer + 1 < LAYERS:
                        sums_ref[layer + 1, near[1], at] = across(value, masks)
                    else:
                        total_ref[at] += value

    for layer in range(LAYERS):
        pl.when((step > layer) & (step <= steps + layer))(lambda layer=layer: arc_stage(layer))

    @pl.when(step == steps + LAYERS - 1)
    def _():
        lane = lax.broadcasted_iota(jnp.int32, (LANES, LANES), 1)
        from_lane = lax.broadcasted_iota(jnp.int32, (LANES, LANES), 0)
        copies = LANES // side
        folding = jnp.where(lane % copies == from_lane // side, 1.0 / (side * side), 0.0)
        means = jnp.dot(total_ref[...].reshape(-1, LANES), folding, precision=highest)
        place = lax.broadcasted_iota(jnp.int32, (SUBLANES, LANES), 1) // copies
        for g in range(groups):
            line = past_ref[g * SUBLANES : (g + 1) * SUBLANES, :]
            for pack in range(packs):
                at = (pack * groups + g) * SUBLANES
                line = jnp.where(place == first + pack, means[at : at + SUBLANES], line)
            tile_ref[g * SUBLANES : (g + 1) * SUBLANES, :] = line


def pair_forward(u_images, u_maps, v_rows, first, tile):
    channels, side, groups, _, _ = u_images.shape
    packs = v_rows.shape[2]
    steps = side // ROWS
    f32 = jnp.float32

    def lag(layer, trailing):
        return lambda i: (jnp.clip(i - 1 - layer, 0, steps - 1),) + (0,) * trailing

    count = packs * groups
    return pl.pallas_call(
        lambda *refs: forward_kernel(side, channels, groups, packs, first, *refs),
        out_shape=[jax.ShapeDtypeStruct((side, count, SUBLANES, LANES), f32)] * LAYERS
        + [jax.ShapeDtypeStruct((side, packs, LANES), f32)] * LAYERS
        + [jax.ShapeDtypeStruct(tile.shape, f32)],
        grid=(steps + LAYERS,),
        in_specs=[
            pl.BlockSpec(
                (channels, ROWS, groups, SUBLANES, LANES),
                lambda i: (0, jnp.minimum(i, steps - 1), 0, 0, 0),
            ),
            pl.BlockSpec((channels, ROWS, packs, LANES), lambda i: (0, jnp.minimum(i, steps - 1), 0, 0)),
        ]
        + [
            pl.BlockSpec((ROWS, 2, groups, SUBLANES, LANES), lag(layer, 4)) for layer in range(LAYERS)
        ]
        + [pl.BlockSpec(tile.shape, lambda i: (0, 0))],
        out_specs=[
            pl.BlockSpec((ROWS, count, SUBLANES, LANES), lag(layer, 3)) for layer in range(LAYERS)
        ]
        + [pl.BlockSpec((ROWS, packs, LANES), lag(layer, 2)) for layer in range(LAYERS)]
        + [pl.BlockSpec(tile.shape, lambda i: (0, 0))],
        scratch_shapes=[
            pltpu.VMEM((LAYERS, RING, count, SUBLANES, LANES), f32),
            pltpu.VMEM((LAYERS, RING, packs, LANES), f32),
            pltpu.VMEM((count, SUBLANES, LANES), f32),
        ],
        name="pair_forward",
    )(u_images, v_rows, *u_maps, tile)


def backward_kernel(side, channels, groups, packs, batches, *refs):
    weight_ref, u_ref = refs[0], refs[1]
    u_map_refs = refs[2 : 2 + LAYERS]
    taken = 2 + LAYERS
    angle_refs, root_refs, image_refs = [], [], []
    for batch in range(batches):
        angle_refs.append(refs[taken : taken + LAYERS])
        root_refs.append(refs[taken + LAYERS : taken + 2 * LAYERS])
        image_refs.append(refs[taken + 2 * LAYERS])
        taken += 2 * LAYERS + 1
    grad_ref, sums_ref, own_sums_ref, wide_ref = refs[taken:]
    ring = sums_ref.shape[1]
    step = pl.program_id(0)
    masks = edges(side, (SUBLANES, LANES))
    shrink = 1.0 / (9.0 * PI)
    pixels = side * side

    def slot(row):
        return row & (ring - 1)

    def fold(total):
        total = total + pltpu.roll(total, 2 * side, 1)
        return total + pltpu.roll(total, side, 1)

    def spread(line):
        return jnp.broadcast_to(line, (SUBLANES, LANES))

    def summed(ref, depth, row, at):
        return ref[depth, slot(row - 1), at] + ref[depth, slot(row), at] + ref[depth, slot(row + 1), at]

    @pl.when(step == 0)
    def _():
        lane = lax.broadcasted_iota(jnp.int32, (SUBLANES, LANES), 1)
        for pack in range(batches * packs):
            index = lane // side + pack * (LANES // side)
            for g in range(groups):
                line = weight_ref[g * SUBLANES : (g + 1) * SUBLANES, :]
                wide_ref[pack * groups + g] = jnp.take_along_axis(line, index, axis=1)
        for depth in range(LAYERS):
            sums_ref[depth, ring - 1] = jnp.zeros(sums_ref.shape[2:], jnp.float32)
            own_sums_ref[depth, ring - 1] = jnp.zeros(own_sums_ref.shape[2:], jnp.float32)

    for depth in range(LAYERS):

        @pl.when(step == side + depth)
        def _(depth=depth):
            sums_ref[depth, slot(side)] = jnp.zeros(sums_ref.shape[2:], jnp.float32)
            own_sums_ref[depth, slot(side)] = jnp.zeros(own_sums_ref.shape[2:], jnp.float32)

    def layer_stage(depth):
        layer = LAYERS - 1 - depth
        row = step - depth
        totals = [None] * groups
        for batch in range(batches):
            for pack in range(packs):
                root = spread(root_refs[batch][layer][0, pack : pack + 1, :])
                for g in range(groups):
                    inner = pack * groups + g
                    at = batch * packs * groups + inner
                    grad = wide_ref[at] if depth == 0 else summed(sums_ref, depth - 1, row, at)
                    angle = angle_refs[batch][layer][0, inner]
                    product = angle * (PI - angle)
                    part = grad * root * (product * horner(SINE, product))
                    totals[g] = part if totals[g] is None else totals[g] + part
                    sums_ref[depth, slot(row), at] = across(grad * angle, masks)
        factor = shrink**depth / (pixels * 2.0 * PI * PI)
        for g in range(groups):
            carry = fold(totals[g]) * (factor / u_map_refs[layer][0, 1, g])
            if depth > 0:
                carry = carry + summed(own_sums_ref, depth - 1, row, g) * (1.0 / 9.0)
            own_sums_ref[depth, slot(row), g] = across(carry, masks)

    def image_stage():
        row = step - LAYERS
        totals = [[None] * groups for _ in range(channels)]
        for batch in range(batches):
            for pack in range(packs):
                lines = [spread(image_refs[batch][c, 0, pack : pack + 1, :]) for c in range(channels)]
                for g in range(groups):
                    at = (batch * packs + pack) * groups + g
                    grad = summed(sums_ref, LAYERS - 1, row, at)
                    for c in range(channels):
                        part = grad * lines[c]
                        totals[c][g] = part if totals[c][g] is None else totals[c][g] + part
        for g in range(groups):
            carry = summed(own_sums_ref, LAYERS - 1, row, g) * (2.0 / (9.0 * channels))
            for c in range(channels):
                full = fold(totals[c][g]) * (shrink**LAYERS / (pixels * channels)) + carry * u_ref[c, 0, g]
                grad_ref[0, c, g] = full[:, :side]

    for depth in range(LAYERS):
        pl.when((step >= depth) & (step < side + depth))(lambda depth=depth: layer_stage(depth))
    pl.when(step >= LAYERS)(image_stage)


def pair_backward(weights, u_images, u_maps, batches):
    channels, side, groups, _, _ = u_images.shape
    packs = batches[0][2].shape[2]
    count = packs * groups
    f32 = jnp.float32

    def rows(lag, trailing):
        return lambda i: (jnp.clip(i - lag, 0, side - 1),) + (0,) * trailing

    def image_rows(trailing):
        return lambda i: (0, jnp.clip(i - LAYERS, 0, side - 1)) + (0,) * trailing

    operands = [weights, u_images, *u_maps]
    in_specs = [
        pl.BlockSpec(weights.shape, lambda i: (0, 0)),
        pl.BlockSpec((channels, 1, groups, SUBLANES, LANES), image_rows(3)),
    ] + [
        pl.BlockSpec((1, 2, groups, SUBLANES, LANES), rows(LAYERS - 1 - layer, 4))
        for layer in range(LAYERS)
    ]
    for angles, roots, images in batches:
        for layer in range(LAYERS):
            operands.append(angles[layer])
            in_specs.append(pl.BlockSpec((1, count, SUBLANES, LANES), rows(LAYERS - 1 - layer, 3)))
        for layer in range(LAYERS):
            operands.append(roots[layer])
            in_specs.append(pl.BlockSpec((1, packs, LANES), rows(LAYERS - 1 - layer, 2)))
        operands.append(images)
        in_specs.append(pl.BlockSpec((channels, 1, packs, LANES), image_rows(2)))
    return pl.pallas_call(
        lambda *refs: backward_kernel(side, channels, groups, packs, len(batches), *refs),
        out_shape=jax.ShapeDtypeStruct((side, channels, groups, SUBLANES, side), f32),
        grid=(side + LAYERS,),
        in_specs=in_specs,
        out_specs=pl.BlockSpec((1, channels, groups, SUBLANES, side), rows(LAYERS, 4)),
        scratch_shapes=[
            pltpu.VMEM((LAYERS, 4, count * len(batches), SUBLANES, LANES), f32),
            pltpu.VMEM((LAYERS, 4, groups, SUBLANES, LANES), f32),
            pltpu.VMEM((count * len(batches), SUBLANES, LANES), f32),
        ],
        name="pair_backward",
    )(*operands)


def eliminate(panel):
    height = panel.shape[0]
    lane = lax.broadcasted_iota(jnp.int32, panel.shape, 1)
    row = lax.broadcasted_iota(jnp.int32, panel.shape, 0)
    for j in range(height):
        column = panel[:, j : j + 1]
        line = panel[j : j + 1, :]
        inverse = 1.0 / panel[j : j + 1, j : j + 1]
        line = jnp.where(lane[:1] == j, 1.0, line) * inverse
        panel = jnp.where(row == j, line, jnp.where(lane == j, 0.0, panel) - column * line)
    return panel


def solve_kernel(row_count, col_count, own, place_ref, gathered_ref, onehot_ref, *refs):
    weight_ref, gamma_ref, loss_ref, big_ref, label_ref, system_ref, inverse_ref, row_ref = refs
    f32 = jnp.float32
    row_index, col_index = place_ref[0], place_ref[1]
    count = row_count * col_count * own
    rows = row_count * own
    block = col_count * own
    half = LANES // 2

    def dot(a, b, da=1, db=0):
        return lax.dot_general(a, b, (((da,), (db,)), ((), ())), precision=highest, preferred_element_type=f32)

    for r in range(row_count):
        for c in range(col_count):
            source = r * col_count + c
            tile = pltpu.roll(gathered_ref[source, :rows, :], 2 * own * c, 1) if c else gathered_ref[source, :rows, :]
            for r2 in range(row_count):
                big_ref[r, pl.ds((r2 * col_count + c) * own, own), :] = tile[r2 * own : (r2 + 1) * own]
            label_ref[pl.ds(source * own, own), :] = gathered_ref[source, rows : rows + own, :]
    i = lax.broadcasted_iota(jnp.int32, (LANES, LANES), 0)
    j = lax.broadcasted_iota(jnp.int32, (LANES, LANES), 1)
    target = (i // own) % 2 * half + i // (2 * own) * own + i % own
    sorting = (target == j).astype(f32)
    parts = dot(big_ref[...].reshape(row_count * count, LANES), sorting).reshape(row_count, count, LANES)
    lane = lax.broadcasted_iota(jnp.int32, (count, LANES), 1)
    inner, outer = [], []
    for t in range(row_count // 2):
        even, odd = parts[2 * t], parts[2 * t + 1]
        inner.append(jnp.where(lane < half, even, pltpu.roll(odd, half, 1)))
        outer.append(jnp.where(lane < half, pltpu.roll(even, half, 1), odd))
    support = jnp.concatenate(inner, axis=1)
    cross = jnp.concatenate(outer, axis=1)
    wide_lane = lax.broadcasted_iota(jnp.int32, (count, count), 1)
    wide_row = lax.broadcasted_iota(jnp.int32, (count, count), 0)
    diagonal = jnp.where(wide_lane == wide_row, support, 0.0)
    ridge = jnp.sum(diagonal) * (ridge_scale / count)
    system = support + jnp.where(wide_lane == wide_row, ridge, 0.0)
    system_ref[...] = system
    inverse_ref[...] = system
    rest_lane = lax.broadcasted_iota(jnp.int32, (count - BLOCK, count), 1)

    def one_block(step, carry):
        reduced = eliminate(inverse_ref[:BLOCK, :])
        below = inverse_ref[BLOCK:, :]
        below = jnp.where(rest_lane < BLOCK, 0.0, below) - dot(below[:, :BLOCK], reduced)
        inverse_ref[: count - BLOCK, :] = pltpu.roll(below, count - BLOCK, 1)
        inverse_ref[count - BLOCK :, :] = pltpu.roll(reduced, count - BLOCK, 1)
        return carry

    lax.fori_loop(0, count // BLOCK, one_block, 0)

    def solve(right):
        first = dot(inverse_ref[...], right)
        return first + dot(inverse_ref[...], right - dot(system_ref[...], first))

    alpha = solve(label_ref[...])
    error = dot(cross, alpha, 0, 0) - onehot_ref[...]
    loss_ref[...] = jnp.broadcast_to(0.5 * jnp.sum(error * error), loss_ref.shape)
    gamma = solve(dot(cross, error))
    intersection = jnp.sum(gamma * alpha)
    row_ref[0] = alpha
    row_ref[1] = gamma
    row_ref[2] = error
    mine = pl.multiple_of((row_index * col_count + col_index) * own, own)
    gamma_ref[...] = row_ref[1, pl.ds(mine, own), :]

    def rows_here(which):
        starts = [pl.multiple_of((r2 * col_count + col_index) * own, own) for r2 in range(row_count)]
        return jnp.concatenate([row_ref[which, pl.ds(start, own), :] for start in starts], axis=0)

    def columns_here(which):
        return row_ref[which, pl.ds(pl.multiple_of(row_index * block, block), block), :]

    left = jnp.concatenate([rows_here(1), rows_here(0)], axis=1)
    right = jnp.concatenate(
        [
            jnp.concatenate([-columns_here(0), -columns_here(1)], axis=1),
            jnp.concatenate([jnp.zeros((block, LANES), f32), columns_here(2)], axis=1),
        ],
        axis=0,
    )
    weights = dot(left, right, 1, 1)
    u = lax.broadcasted_iota(jnp.int32, weights.shape, 0)
    v = lax.broadcasted_iota(jnp.int32, weights.shape, 1)
    same = (u // own == row_index) & (v == col_index * own + u % own)
    weights = weights - jnp.where(same, intersection * (2.0 * ridge_scale / count), 0.0)
    weights = dot(weights, sorting, 1, 1)
    weight_ref[...] = pltpu.roll(weights, (LANES - 2 * own * col_index) % LANES, 1)


def solve_in_kernel(gathered, onehot, row_index, col_index, row_count, col_count, own):
    f32 = jnp.float32
    count = row_count * col_count * own
    vmem = pl.BlockSpec(memory_space=pltpu.VMEM)
    return pl.pallas_call(
        lambda *refs: solve_kernel(row_count, col_count, own, *refs),
        out_shape=[
            jax.ShapeDtypeStruct((row_count * own, LANES), f32),
            jax.ShapeDtypeStruct((own, LANES), f32),
            jax.ShapeDtypeStruct((SUBLANES, LANES), f32),
        ],
        in_specs=[pl.BlockSpec(memory_space=pltpu.SMEM), vmem, vmem],
        out_specs=[vmem] * 3,
        scratch_shapes=[
            pltpu.VMEM((row_count, count, LANES), f32),
            pltpu.VMEM((count, LANES), f32),
            pltpu.VMEM((count, count), f32),
            pltpu.VMEM((count, count), f32),
            pltpu.VMEM((3, count, LANES), f32),
        ],
        name="solve",
    )(jnp.stack([row_index, col_index]).astype(jnp.int32), gathered, onehot)


def solve_with(factor, rhs):
    halfway = lax.linalg.triangular_solve(factor, rhs, left_side=True, lower=True)
    return lax.linalg.triangular_solve(factor, halfway, left_side=True, lower=True, transpose_a=True)


def solve_plainly(gathered, onehot, row_index, col_index, row_count, col_count, own):
    count = row_count * col_count * own
    rows = row_count * own
    block = 2 * col_count * own
    labels = gathered[:, rows : rows + own].reshape(count, LANES)
    kernels = []
    for kind in range(2):
        picked = gathered[:, :rows, :block].reshape(-1, rows, col_count, 2 * own)
        picked = picked[..., kind * own : (kind + 1) * own]
        picked = picked.reshape(row_count, col_count, row_count, own, block // 2)
        picked = jnp.stack(
            [jnp.roll(picked[:, c], c * own, axis=-1) for c in range(col_count)], axis=1
        )
        kernels.append(jnp.transpose(picked, (2, 1, 3, 0, 4)).reshape(count, count))
    identity = jnp.eye(count, dtype=jnp.float32)
    ridge = jnp.trace(kernels[0]) * (ridge_scale / count)
    factor = jnp.linalg.cholesky(kernels[0] + ridge * identity)
    alpha = solve_with(factor, labels)
    error = jnp.dot(kernels[1].T, alpha, precision=highest) - onehot
    gamma = solve_with(factor, jnp.dot(kernels[1], error, precision=highest))
    intersection = jnp.sum(gamma * alpha)
    values = jnp.stack([alpha, gamma, error]).reshape(3, row_count, col_count, own, LANES)
    here = lax.dynamic_index_in_dim(values, col_index, 2, keepdims=False).reshape(3, rows, LANES)
    there = lax.dynamic_index_in_dim(values, row_index, 1, keepdims=False)
    there = lax.dynamic_slice_in_dim(
        jnp.concatenate([there, there], axis=1), col_index, col_count, 1
    ).reshape(3, -1, LANES)

    def outer(a, b):
        return jnp.dot(a, b.T, precision=highest)

    pair = -outer(here[1], there[0]) - outer(here[0], there[1])
    u, v = jnp.arange(rows)[:, None], jnp.arange(block // 2)[None, :]
    same = (u // own == row_index) & (v == u % own)
    pair = pair - jnp.where(same, intersection * (2.0 * ridge_scale / count), 0.0)
    weights = jnp.stack([pair, outer(here[0], there[2])]).reshape(2, rows, col_count, own)
    weights = jnp.transpose(weights, (1, 2, 0, 3)).reshape(rows, block)
    weights = jnp.pad(weights, ((0, 0), (0, LANES - block)))
    mine = (row_index * col_count + col_index) * own
    return (
        weights,
        lax.dynamic_slice_in_dim(gamma, mine, own, 0),
        jnp.full((SUBLANES, LANES), 0.5 * jnp.sum(error * error)),
    )


def body(support_views, support_pick, target_views, target_pick, support_labels, target_labels):
    own, _, channels, pixels = support_views.shape
    side = math.isqrt(pixels)
    classes = support_labels.shape[1]
    row_count = lax.axis_size("row")
    col_count = lax.axis_size("col")
    row_index = lax.axis_index("row")
    col_index = lax.axis_index("col")
    own_support = choose_view(support_views, support_pick)
    own_target = choose_view(target_views, target_pick)

    both = jnp.stack([own_support, own_target]).reshape(2 * own, channels, side, side)
    chunk = jnp.transpose(both, (1, 2, 0, 3)).reshape(channels, side, 2 * own * side)
    chunks = [chunk]
    for d in range(1, col_count):
        pairs = [((i + d) % col_count, i) for i in range(col_count)]
        chunks.append(lax.ppermute(chunk, "col", pairs))
    per_batch = col_count // BATCHES
    v_rows = []
    for batch in range(BATCHES):
        taken = jnp.concatenate(chunks[batch * per_batch : (batch + 1) * per_batch], axis=-1)
        v_rows.append(taken.reshape(channels, side, -1, LANES))
    packs = v_rows[0].shape[2]

    row_images = lax.all_gather(own_support, "row", axis=0, tiled=True)
    groups = row_images.shape[0] // SUBLANES
    narrow = jnp.transpose(
        row_images.reshape(groups, SUBLANES, channels, side, side), (2, 3, 0, 1, 4)
    )
    u_images, *u_maps = prepare_rows(narrow)
    batches = []
    tile = jnp.zeros((groups * SUBLANES, LANES), jnp.float32)
    for batch in range(BATCHES):
        results = pair_forward(u_images, u_maps, v_rows[batch], batch * packs, tile)
        batches.append((results[:LAYERS], results[LAYERS : 2 * LAYERS], v_rows[batch]))
        tile = results[-1]
    devices = row_count * col_count
    labels = jnp.pad(support_labels, ((0, 0), (0, LANES - classes)))
    parcel = jnp.concatenate([tile, labels], axis=0)
    gathered = lax.all_to_all(
        jnp.broadcast_to(parcel[None], (devices,) + parcel.shape), AXES, 0, 0, tiled=True
    )
    lanes = jnp.arange(LANES, dtype=jnp.int32)[None, :]
    onehot = jnp.where(
        lanes < classes, (target_labels[:, None] == lanes).astype(jnp.float32) - 1.0 / classes, 0.0
    )
    fits = own == SUBLANES and 2 * col_count * own == LANES and row_count % 2 == 0
    solve = solve_in_kernel if fits else solve_plainly
    weights, gamma_own, loss = solve(
        gathered, onehot, row_index, col_index, row_count, col_count, own
    )
    grads = pair_backward(weights, u_images, u_maps, batches)
    grads = jnp.transpose(grads, (2, 3, 1, 0, 4)).reshape(row_count * own, channels, pixels)
    support_grad = lax.psum_scatter(grads, "row", scatter_dimension=0, tiled=True)
    return (support_grad, gamma_own[:, :classes], loss[0, 0])


def solution(mesh):
    return jax.shard_map(
        body,
        mesh=mesh,
        in_specs=(
            P(AXES, None, None, None),
            P(AXES),
            P(AXES, None, None, None),
            P(AXES),
            P(AXES, None),
            P(),
        ),
        out_specs=(P(AXES, None, None), P(AXES, None), P()),
        check_vma=False,
    )
```

```python
import math

import jax
import jax.numpy as jnp
from jax import lax
from jax.experimental import pallas as pl
from jax.experimental.pallas import tpu as pltpu
from jax.sharding import PartitionSpec as P

LAYERS = 3
LANES = 128
SUBLANES = 8
SHARES = (1, 1, 2, 2, 2)
PART = 8
BLOCK = 64
ROWS = 2
RING = 8

bias_variance = 0.1
ridge_scale = 0.1
highest = lax.Precision.HIGHEST
tiny = 1e-30
PI = math.pi

ACOS = (
    1.4142137164552202,
    0.11783707507052552,
    0.026725055357041356,
    0.00674552756719407,
    0.005608499939250727,
    -0.0026297111285195295,
    0.002296009448189848,
)
SINE = (
    0.31830981148327425,
    0.032252498831491,
    0.001158328114192081,
    2.2834735017183973e-05,
)
AXES = ("row", "col")


def horner(coefficients, x):
    total = coefficients[-1] * x + coefficients[-2]
    for coefficient in coefficients[-3::-1]:
        total = total * x + coefficient
    return total


def choose_view(views, picked):
    options = jnp.arange(views.shape[1], dtype=jnp.int32)
    selector = (picked[:, None] == options[None, :]).astype(jnp.float32)
    return jnp.sum(selector[:, :, None, None] * views, axis=1)


def edges(side, shape):
    x = lax.broadcasted_iota(jnp.int32, shape, len(shape) - 1) % side
    return x > 0, x < side - 1


def across(surface, masks):
    axis = surface.ndim - 1
    left = jnp.where(masks[0], pltpu.roll(surface, 1, axis), 0.0)
    right = jnp.where(masks[1], pltpu.roll(surface, LANES - 1, axis), 0.0)
    return surface + left + right


def map_scale(channels, layer):
    return 9.0 * channels if layer == 0 else 9.0


def forward_kernel(side, channels, groups, packs, first, *refs):
    if first == 0:
        narrow_ref, v_ref = refs[:2]
        u_ref, *u_map_refs = refs[2 : 3 + LAYERS]
        u_sums_ref = refs[-1]
        outs = refs[3 + LAYERS : -1]
    else:
        u_ref, v_ref = refs[:2]
        u_map_refs = refs[2 : 2 + LAYERS]
        past_ref = refs[2 + LAYERS]
        outs = refs[3 + LAYERS :]
    angle_refs = outs[:LAYERS]
    root_refs = outs[LAYERS : 2 * LAYERS]
    tile_ref = outs[2 * LAYERS]
    sums_ref, own_sums_ref, total_ref = outs[2 * LAYERS + 1 :]
    step = pl.program_id(0)
    steps = side // ROWS
    masks = edges(side, (SUBLANES, LANES))
    own_masks = edges(side, (packs, LANES))

    def slot(row):
        return row & (RING - 1)

    def spread(line):
        return jnp.broadcast_to(line, (SUBLANES, LANES))

    if first == 0:

        @pl.when(step == 0)
        def _():
            for layer in range(LAYERS):
                u_sums_ref[layer, RING - 1] = jnp.zeros(u_sums_ref.shape[2:], jnp.float32)

        for layer in range(LAYERS):

            @pl.when(step == steps + layer)
            def _(layer=layer):
                u_sums_ref[layer, slot(side)] = jnp.zeros(u_sums_ref.shape[2:], jnp.float32)

        @pl.when(step < steps)
        def _():
            for r in range(ROWS):
                for g in range(groups):
                    energy = None
                    for c in range(channels):
                        plane = jnp.concatenate([narrow_ref[c, r, g]] * (LANES // side), axis=-1)
                        u_ref[c, r, g] = plane
                        energy = plane * plane if energy is None else energy + plane * plane
                    u_sums_ref[0, slot(step * ROWS + r), g] = across(energy, masks)

    def row_maps(layer):
        scale = map_scale(channels, layer)
        for r in range(ROWS):
            row = (step - 1 - layer) * ROWS + r
            for g in range(groups):
                total = (
                    u_sums_ref[layer, slot(row - 1), g]
                    + u_sums_ref[layer, slot(row), g]
                    + u_sums_ref[layer, slot(row + 1), g]
                )
                current = total * (1.0 / scale) + bias_variance
                inverse = lax.rsqrt(current)
                u_map_refs[layer][r, 0, g] = inverse * (1.0 / scale)
                u_map_refs[layer][r, 1, g] = current * inverse * (1.0 / PI)
                if layer + 1 < LAYERS:
                    u_sums_ref[layer + 1, slot(row), g] = across(current, masks)

    @pl.when(step == 0)
    def _():
        total_ref[...] = jnp.zeros(total_ref.shape, jnp.float32)
        for layer in range(LAYERS):
            sums_ref[layer, RING - 1] = jnp.zeros(sums_ref.shape[2:], jnp.float32)
            own_sums_ref[layer, RING - 1] = jnp.zeros(own_sums_ref.shape[2:], jnp.float32)

    for layer in range(LAYERS):

        @pl.when(step == steps + layer)
        def _(layer=layer):
            sums_ref[layer, slot(side)] = jnp.zeros(sums_ref.shape[2:], jnp.float32)
            own_sums_ref[layer, slot(side)] = jnp.zeros(own_sums_ref.shape[2:], jnp.float32)

    @pl.when(step < steps)
    def _():
        for r in range(ROWS):
            where = slot(step * ROWS + r)
            energy = None
            for c in range(channels):
                plane = v_ref[c, r]
                energy = plane * plane if energy is None else energy + plane * plane
            own_sums_ref[0, where] = across(energy, own_masks)
            for pack in range(packs):
                lines = [spread(v_ref[c, r, pack : pack + 1, :]) for c in range(channels)]
                for g in range(groups):
                    product = None
                    for c in range(channels):
                        part = u_ref[c, r, g] * lines[c]
                        product = part if product is None else product + part
                    sums_ref[0, where, pack * groups + g] = across(product, masks)

    def arc_stage(layer):
        if first == 0:
            row_maps(layer)
        scale = map_scale(channels, layer)
        offset = scale * bias_variance
        rows = [(step - 1 - layer) * ROWS + r for r in range(ROWS)]
        near = [slot(rows[0] + r) for r in range(-1, ROWS + 1)]
        inverses, roots = [], []
        for r in range(ROWS):
            own_total = own_sums_ref[layer, near[r]] + own_sums_ref[layer, near[r + 1]] + own_sums_ref[layer, near[r + 2]]
            own_map = own_total * (1.0 / scale) + bias_variance
            inverse = lax.rsqrt(own_map)
            inverses.append(inverse)
            roots.append(own_map * inverse)
            root_refs[layer][r] = roots[r]
            if layer + 1 < LAYERS:
                own_sums_ref[layer + 1, near[r + 1]] = across(own_map, own_masks)
        for pack in range(packs):
            for g in range(groups):
                at = pack * groups + g
                for r in range(0, ROWS, 2):
                    lines = [sums_ref[layer, near[r + k], at] for k in range(4)]
                    middle = (lines[1] + lines[2]) + offset
                    for k, summed in enumerate((lines[0] + middle, middle + lines[3])):
                        right_inverse = spread(inverses[r + k][pack : pack + 1, :])
                        right_root = spread(roots[r + k][pack : pack + 1, :])
                        cosine = summed * u_map_refs[layer][r + k, 0, g] * right_inverse
                        gap = 1.0 - (jnp.abs(cosine) if layer == 0 else cosine)
                        gap = jnp.maximum(gap, tiny)
                        theta = gap * lax.rsqrt(gap)
                        rest = 2.0 - gap
                        sine = theta * (rest * lax.rsqrt(rest))
                        theta = theta * horner(ACOS, gap)
                        angle = PI - theta
                        if layer == 0:
                            angle = jnp.where(cosine >= 0.0, angle, theta)
                        angle_refs[layer][r + k, at] = angle
                        value = (cosine * angle + sine) * u_map_refs[layer][r + k, 1, g] * right_root
                        if layer + 1 < LAYERS:
                            sums_ref[layer + 1, near[r + k + 1], at] = across(value, masks)
                        else:
                            total_ref[at] += value

    for layer in range(LAYERS):
        pl.when((step > layer) & (step <= steps + layer))(lambda layer=layer: arc_stage(layer))

    @pl.when(step == steps + LAYERS - 1)
    def _():
        lane = lax.broadcasted_iota(jnp.int32, (LANES, LANES), 1)
        from_lane = lax.broadcasted_iota(jnp.int32, (LANES, LANES), 0)
        copies = LANES // side
        folding = jnp.where(lane % copies == from_lane // side, 1.0 / (side * side), 0.0)
        means = jnp.dot(total_ref[...].reshape(-1, LANES), folding, precision=highest)
        place = lax.broadcasted_iota(jnp.int32, (SUBLANES, LANES), 1) // copies
        for g in range(groups):
            mine = slice(g * SUBLANES, (g + 1) * SUBLANES)
            line = jnp.zeros((SUBLANES, LANES), jnp.float32) if first == 0 else past_ref[mine, :]
            for pack in range(packs):
                at = (pack * groups + g) * SUBLANES
                line = jnp.where(place == first + pack, means[at : at + SUBLANES], line)
            tile_ref[mine, :] = line


def pair_forward(rows, v_rows, first, tile):
    channels, side, groups = (rows if first == 0 else rows[0]).shape[:3]
    packs = v_rows.shape[2]
    steps = side // ROWS
    count = packs * groups
    f32 = jnp.float32

    def lag(layer, trailing):
        return lambda i: (jnp.clip(i - 1 - layer, 0, steps - 1),) + (0,) * trailing

    def now(trailing):
        return lambda i: (0, jnp.minimum(i, steps - 1)) + (0,) * trailing

    image = pl.BlockSpec((channels, ROWS, groups, SUBLANES, LANES), now(3))
    maps = [pl.BlockSpec((ROWS, 2, groups, SUBLANES, LANES), lag(layer, 4)) for layer in range(LAYERS)]
    column = pl.BlockSpec((channels, ROWS, packs, LANES), now(2))
    whole = pl.BlockSpec((groups * SUBLANES, LANES), lambda i: (0, 0))
    out_shape = (
        [jax.ShapeDtypeStruct((side, count, SUBLANES, LANES), f32)] * LAYERS
        + [jax.ShapeDtypeStruct((side, packs, LANES), f32)] * LAYERS
        + [jax.ShapeDtypeStruct((groups * SUBLANES, LANES), f32)]
    )
    out_specs = (
        [pl.BlockSpec((ROWS, count, SUBLANES, LANES), lag(layer, 3)) for layer in range(LAYERS)]
        + [pl.BlockSpec((ROWS, packs, LANES), lag(layer, 2)) for layer in range(LAYERS)]
        + [whole]
    )
    scratch_shapes = [
        pltpu.VMEM((LAYERS, RING, count, SUBLANES, LANES), f32),
        pltpu.VMEM((LAYERS, RING, packs, LANES), f32),
        pltpu.VMEM((count, SUBLANES, LANES), f32),
    ]
    if first == 0:
        operands = [rows, v_rows]
        in_specs = [pl.BlockSpec((channels, ROWS, groups, SUBLANES, side), now(3)), column]
        out_shape = (
            [jax.ShapeDtypeStruct((channels, side, groups, SUBLANES, LANES), f32)]
            + [jax.ShapeDtypeStruct((side, 2, groups, SUBLANES, LANES), f32)] * LAYERS
            + out_shape
        )
        out_specs = [image] + maps + out_specs
        scratch_shapes = scratch_shapes + [pltpu.VMEM((LAYERS, RING, groups, SUBLANES, LANES), f32)]
    else:
        operands = [rows[0], v_rows, *rows[1:], tile]
        in_specs = [image, column] + maps + [whole]
    results = pl.pallas_call(
        lambda *refs: forward_kernel(side, channels, groups, packs, first, *refs),
        out_shape=out_shape,
        grid=(steps + LAYERS,),
        in_specs=in_specs,
        out_specs=out_specs,
        scratch_shapes=scratch_shapes,
        name="pair_forward",
    )(*operands)
    if first == 0:
        rows, results = results[: 1 + LAYERS], results[1 + LAYERS :]
    return rows, results[-1], results[:LAYERS], results[LAYERS : 2 * LAYERS]


def backward_kernel(side, channels, groups, packs, *refs):
    weight_ref, u_ref = refs[0], refs[1]
    u_map_refs = refs[2 : 2 + LAYERS]
    taken = 2 + LAYERS
    angle_refs, root_refs, image_refs = [], [], []
    for batch in range(len(packs)):
        angle_refs.append(refs[taken : taken + LAYERS])
        root_refs.append(refs[taken + LAYERS : taken + 2 * LAYERS])
        image_refs.append(refs[taken + 2 * LAYERS])
        taken += 2 * LAYERS + 1
    grad_ref, sums_ref, own_sums_ref, wide_ref, total_ref = refs[taken:]
    parts = [(batch, pack) for batch in range(len(packs)) for pack in range(packs[batch])]
    blocks = [
        list(enumerate(parts))[start : start + PART] for start in range(0, len(parts), PART)
    ]
    step = pl.program_id(0)
    steps = side // ROWS
    masks = edges(side, (SUBLANES, LANES))
    shrink = 1.0 / (9.0 * PI)
    pixels = side * side

    def slot(row):
        return row & (RING - 1)

    def fold(total):
        total = total + pltpu.roll(total, 2 * side, 1)
        return total + pltpu.roll(total, side, 1)

    def spread(line):
        return jnp.broadcast_to(line, (SUBLANES, LANES))

    def summed(ref, depth, row, at):
        lines = [ref[depth, slot(row + k), at] for k in range(-1, ROWS + 1)]
        totals = []
        for r in range(0, ROWS, 2):
            middle = lines[r + 1] + lines[r + 2]
            totals += [lines[r] + middle, middle + lines[r + 3]]
        return totals

    def add(total, part):
        return part if total is None else total + part

    @pl.when(step == 0)
    def _():
        lane = lax.broadcasted_iota(jnp.int32, (SUBLANES, LANES), 1)
        for pack in range(len(parts)):
            index = lane // side + pack * (LANES // side)
            for g in range(groups):
                line = weight_ref[g * SUBLANES : (g + 1) * SUBLANES, :]
                wide_ref[pack * groups + g] = jnp.take_along_axis(line, index, axis=1)
        for depth in range(LAYERS):
            sums_ref[depth, RING - 1] = jnp.zeros(sums_ref.shape[2:], jnp.float32)
            own_sums_ref[depth, RING - 1] = jnp.zeros(own_sums_ref.shape[2:], jnp.float32)

    for depth in range(LAYERS):

        @pl.when(step == steps + depth)
        def _(depth=depth):
            sums_ref[depth, slot(side)] = jnp.zeros(sums_ref.shape[2:], jnp.float32)
            own_sums_ref[depth, slot(side)] = jnp.zeros(own_sums_ref.shape[2:], jnp.float32)

    def layer_block(depth, block):
        layer = LAYERS - 1 - depth
        row = (step - depth) * ROWS
        totals = [[None] * groups for _ in range(ROWS)]
        for part, (batch, pack) in blocks[block]:
            for g in range(groups):
                inner = pack * groups + g
                at = part * groups + g
                if depth == 0:
                    grads = [wide_ref[at]] * ROWS
                else:
                    grads = summed(sums_ref, depth - 1, row, at)
                for r, grad in enumerate(grads):
                    angle = angle_refs[batch][layer][r, inner]
                    sums_ref[depth, slot(row + r), at] = across(grad * angle, masks)
                    product = angle * (PI - angle)
                    root = spread(root_refs[batch][layer][r, pack : pack + 1, :])
                    totals[r][g] = add(totals[r][g], grad * root * (product * horner(SINE, product)))
        for r in range(ROWS):
            for g in range(groups):
                total = totals[r][g]
                total_ref[depth, r, g] = total if block == 0 else total_ref[depth, r, g] + total

    def layer_end(depth):
        layer = LAYERS - 1 - depth
        row = (step - depth) * ROWS
        factor = shrink**depth / (pixels * 2.0 * PI * PI)
        for g in range(groups):
            above = summed(own_sums_ref, depth - 1, row, g) if depth > 0 else None
            for r in range(ROWS):
                carry = fold(total_ref[depth, r, g]) * (factor / u_map_refs[layer][r, 1, g])
                if depth > 0:
                    carry = carry + above[r] * (1.0 / 9.0)
                own_sums_ref[depth, slot(row + r), g] = across(carry, masks)

    def image_block(block):
        row = (step - LAYERS) * ROWS
        totals = [[[None] * groups for _ in range(channels)] for _ in range(ROWS)]
        for part, (batch, pack) in blocks[block]:
            for g in range(groups):
                at = part * groups + g
                for r, grad in enumerate(summed(sums_ref, LAYERS - 1, row, at)):
                    for c in range(channels):
                        line = spread(image_refs[batch][c, r, pack : pack + 1, :])
                        totals[r][c][g] = add(totals[r][c][g], grad * line)
        for r in range(ROWS):
            for c in range(channels):
                for g in range(groups):
                    total, at = totals[r][c][g], LAYERS + c
                    total_ref[at, r, g] = total if block == 0 else total_ref[at, r, g] + total

    def image_end():
        row = (step - LAYERS) * ROWS
        copies = LANES // side
        lane = lax.broadcasted_iota(jnp.int32, (SUBLANES, LANES), 1)
        for g in range(groups):
            above = summed(own_sums_ref, LAYERS - 1, row, g)
            for r in range(ROWS):
                carry = above[r] * (2.0 / (9.0 * channels))
                for c in range(channels):
                    image = fold(total_ref[LAYERS + c, r, g]) * (shrink**LAYERS / (pixels * channels))
                    image = image + carry * u_ref[c, r, g]
                    lines = grad_ref[g, 0, c]
                    grad_ref[g, 0, c] = jnp.where(lane // side == (row + r) % copies, image, lines)

    for depth in range(LAYERS):
        for block in range(len(blocks)):
            pl.when((step >= depth) & (step < steps + depth))(
                lambda depth=depth, block=block: layer_block(depth, block)
            )
        pl.when((step >= depth) & (step < steps + depth))(lambda depth=depth: layer_end(depth))
    for block in range(len(blocks)):
        pl.when(step >= LAYERS)(lambda block=block: image_block(block))
    pl.when(step >= LAYERS)(image_end)


def pair_backward(weights, rows, batches):
    channels, side, groups = rows[0].shape[:3]
    packs = [images.shape[2] for _, _, images in batches]
    steps = side // ROWS
    copies = LANES // side
    f32 = jnp.float32

    def at_lag(lag, trailing):
        return lambda i: (jnp.clip(i - lag, 0, steps - 1),) + (0,) * trailing

    def image_rows(trailing):
        return lambda i: (0, jnp.clip(i - LAYERS, 0, steps - 1)) + (0,) * trailing

    operands = [weights, *rows]
    in_specs = [
        pl.BlockSpec(weights.shape, lambda i: (0, 0)),
        pl.BlockSpec((channels, ROWS, groups, SUBLANES, LANES), image_rows(3)),
    ] + [
        pl.BlockSpec((ROWS, 2, groups, SUBLANES, LANES), at_lag(LAYERS - 1 - layer, 4))
        for layer in range(LAYERS)
    ]
    for (angles, roots, images), width in zip(batches, packs):
        for layer in range(LAYERS):
            operands.append(angles[layer])
            in_specs.append(
                pl.BlockSpec((ROWS, width * groups, SUBLANES, LANES), at_lag(LAYERS - 1 - layer, 3))
            )
        for layer in range(LAYERS):
            operands.append(roots[layer])
            in_specs.append(pl.BlockSpec((ROWS, width, LANES), at_lag(LAYERS - 1 - layer, 2)))
        operands.append(images)
        in_specs.append(pl.BlockSpec((channels, ROWS, width, LANES), image_rows(2)))
    count = sum(packs) * groups
    return pl.pallas_call(
        lambda *refs: backward_kernel(side, channels, groups, packs, *refs),
        out_shape=jax.ShapeDtypeStruct((groups, side // copies, channels, SUBLANES, LANES), f32),
        grid=(steps + LAYERS,),
        in_specs=in_specs,
        out_specs=pl.BlockSpec(
            (groups, 1, channels, SUBLANES, LANES),
            lambda i: (0, jnp.clip(i - LAYERS, 0, steps - 1) * ROWS // copies, 0, 0, 0),
        ),
        scratch_shapes=[
            pltpu.VMEM((LAYERS, RING, count, SUBLANES, LANES), f32),
            pltpu.VMEM((LAYERS, RING, groups, SUBLANES, LANES), f32),
            pltpu.VMEM((count, SUBLANES, LANES), f32),
            pltpu.VMEM((LAYERS + channels, ROWS, groups, SUBLANES, LANES), f32),
        ],
        name="pair_backward",
    )(*operands)


def eliminate(panel):
    height, width = panel.shape
    tiles = [panel[:, start : start + LANES] for start in range(0, width, LANES)]
    lane = lax.broadcasted_iota(jnp.int32, tiles[0].shape, 1)
    row = lax.broadcasted_iota(jnp.int32, tiles[0].shape, 0)
    for j in range(0, height, 2):
        k = j + 1
        first = jnp.broadcast_to(tiles[0][:, j : j + 1], tiles[0].shape)
        second = jnp.broadcast_to(tiles[0][:, k : k + 1], tiles[0].shape)
        a, b, d = first[j : j + 1], first[k : k + 1], second[k : k + 1]
        scale = 1.0 / (a * d - b * b)
        a, b, d = a * scale, b * scale, d * scale
        for t, tile in enumerate(tiles):
            upper, lower = tile[j : j + 1], tile[k : k + 1]
            if t == 0:
                upper = jnp.where(lane[:1] == j, 1.0, jnp.where(lane[:1] == k, 0.0, upper))
                lower = jnp.where(lane[:1] == k, 1.0, jnp.where(lane[:1] == j, 0.0, lower))
                tile = jnp.where((lane == j) | (lane == k), 0.0, tile)
            upper, lower = d * upper - b * lower, a * lower - b * upper
            rest = tile - first * upper - second * lower
            tiles[t] = jnp.where(row == j, upper, jnp.where(row == k, lower, rest))
    return jnp.concatenate(tiles, axis=1)


def solve_kernel(row_count, col_count, own, place_ref, gathered_ref, onehot_ref, *refs):
    weight_ref, gamma_ref, loss_ref, big_ref, label_ref, system_ref, inverse_ref, row_ref = refs
    f32 = jnp.float32
    row_index, col_index = place_ref[0], place_ref[1]
    count = row_count * col_count * own
    rows = row_count * own
    block = col_count * own
    half = LANES // 2

    def dot(a, b, da=1, db=0):
        return lax.dot_general(a, b, (((da,), (db,)), ((), ())), precision=highest, preferred_element_type=f32)

    for r in range(row_count):
        for c in range(col_count):
            source = r * col_count + c
            tile = pltpu.roll(gathered_ref[source, :rows, :], 2 * own * c, 1) if c else gathered_ref[source, :rows, :]
            for r2 in range(row_count):
                big_ref[r, pl.ds((r2 * col_count + c) * own, own), :] = tile[r2 * own : (r2 + 1) * own]
            label_ref[pl.ds(source * own, own), :] = gathered_ref[source, rows : rows + own, :]
    i = lax.broadcasted_iota(jnp.int32, (LANES, LANES), 0)
    j = lax.broadcasted_iota(jnp.int32, (LANES, LANES), 1)
    target = (i // own) % 2 * half + i // (2 * own) * own + i % own
    sorting = (target == j).astype(f32)
    parts = dot(big_ref[...].reshape(row_count * count, LANES), sorting).reshape(row_count, count, LANES)
    lane = lax.broadcasted_iota(jnp.int32, (count, LANES), 1)
    inner, outer = [], []
    for t in range(row_count // 2):
        even, odd = parts[2 * t], parts[2 * t + 1]
        inner.append(jnp.where(lane < half, even, pltpu.roll(odd, half, 1)))
        outer.append(jnp.where(lane < half, pltpu.roll(even, half, 1), odd))
    support = jnp.concatenate(inner, axis=1)
    cross = jnp.concatenate(outer, axis=1)
    wide_lane = lax.broadcasted_iota(jnp.int32, (count, count), 1)
    wide_row = lax.broadcasted_iota(jnp.int32, (count, count), 0)
    diagonal = jnp.where(wide_lane == wide_row, support, 0.0)
    ridge = jnp.sum(diagonal) * (ridge_scale / count)
    system = support + jnp.where(wide_lane == wide_row, ridge, 0.0)
    system_ref[...] = system
    inverse_ref[...] = system
    rest_lane = lax.broadcasted_iota(jnp.int32, (count - BLOCK, count), 1)

    def one_block(step, carry):
        reduced = eliminate(inverse_ref[:BLOCK, :])
        below = inverse_ref[BLOCK:, :]
        below = jnp.where(rest_lane < BLOCK, 0.0, below) - dot(below[:, :BLOCK], reduced)
        inverse_ref[: count - BLOCK, :] = pltpu.roll(below, count - BLOCK, 1)
        inverse_ref[count - BLOCK :, :] = pltpu.roll(reduced, count - BLOCK, 1)
        return carry

    lax.fori_loop(0, count // BLOCK, one_block, 0)

    def solve(right):
        first = dot(inverse_ref[...], right)
        return first + dot(inverse_ref[...], right - dot(system_ref[...], first))

    alpha = solve(label_ref[...])
    error = dot(cross, alpha, 0, 0) - onehot_ref[...]
    loss_ref[...] = jnp.broadcast_to(0.5 * jnp.sum(error * error), loss_ref.shape)
    gamma = solve(dot(cross, error))
    intersection = jnp.sum(gamma * alpha)
    row_ref[0] = alpha
    row_ref[1] = gamma
    row_ref[2] = error
    mine = pl.multiple_of((row_index * col_count + col_index) * own, own)
    gamma_ref[...] = row_ref[1, pl.ds(mine, own), :]

    def rows_here(which):
        starts = [pl.multiple_of((r2 * col_count + col_index) * own, own) for r2 in range(row_count)]
        return jnp.concatenate([row_ref[which, pl.ds(start, own), :] for start in starts], axis=0)

    def columns_here(which):
        return row_ref[which, pl.ds(pl.multiple_of(row_index * block, block), block), :]

    left = jnp.concatenate([rows_here(1), rows_here(0)], axis=1)
    right = jnp.concatenate(
        [
            jnp.concatenate([-columns_here(0), -columns_here(1)], axis=1),
            jnp.concatenate([jnp.zeros((block, LANES), f32), columns_here(2)], axis=1),
        ],
        axis=0,
    )
    weights = dot(left, right, 1, 1)
    u = lax.broadcasted_iota(jnp.int32, weights.shape, 0)
    v = lax.broadcasted_iota(jnp.int32, weights.shape, 1)
    same = (u // own == row_index) & (v == col_index * own + u % own)
    weights = weights - jnp.where(same, intersection * (2.0 * ridge_scale / count), 0.0)
    weights = dot(weights, sorting, 1, 1)
    weight_ref[...] = pltpu.roll(weights, (LANES - 2 * own * col_index) % LANES, 1)


def solve_in_kernel(gathered, onehot, row_index, col_index, row_count, col_count, own):
    f32 = jnp.float32
    count = row_count * col_count * own
    vmem = pl.BlockSpec(memory_space=pltpu.VMEM)
    return pl.pallas_call(
        lambda *refs: solve_kernel(row_count, col_count, own, *refs),
        out_shape=[
            jax.ShapeDtypeStruct((row_count * own, LANES), f32),
            jax.ShapeDtypeStruct((own, LANES), f32),
            jax.ShapeDtypeStruct((SUBLANES, LANES), f32),
        ],
        in_specs=[pl.BlockSpec(memory_space=pltpu.SMEM), vmem, vmem],
        out_specs=[vmem] * 3,
        scratch_shapes=[
            pltpu.VMEM((row_count, count, LANES), f32),
            pltpu.VMEM((count, LANES), f32),
            pltpu.VMEM((count, count), f32),
            pltpu.VMEM((count, count), f32),
            pltpu.VMEM((3, count, LANES), f32),
        ],
        name="solve",
    )(jnp.stack([row_index, col_index]).astype(jnp.int32), gathered, onehot)


def solve_with(factor, rhs):
    halfway = lax.linalg.triangular_solve(factor, rhs, left_side=True, lower=True)
    return lax.linalg.triangular_solve(factor, halfway, left_side=True, lower=True, transpose_a=True)


def solve_plainly(gathered, onehot, row_index, col_index, row_count, col_count, own):
    count = row_count * col_count * own
    rows = row_count * own
    block = 2 * col_count * own
    labels = gathered[:, rows : rows + own].reshape(count, LANES)
    kernels = []
    for kind in range(2):
        picked = gathered[:, :rows, :block].reshape(-1, rows, col_count, 2 * own)
        picked = picked[..., kind * own : (kind + 1) * own]
        picked = picked.reshape(row_count, col_count, row_count, own, block // 2)
        picked = jnp.stack(
            [jnp.roll(picked[:, c], c * own, axis=-1) for c in range(col_count)], axis=1
        )
        kernels.append(jnp.transpose(picked, (2, 1, 3, 0, 4)).reshape(count, count))
    identity = jnp.eye(count, dtype=jnp.float32)
    ridge = jnp.trace(kernels[0]) * (ridge_scale / count)
    factor = jnp.linalg.cholesky(kernels[0] + ridge * identity)
    alpha = solve_with(factor, labels)
    error = jnp.dot(kernels[1].T, alpha, precision=highest) - onehot
    gamma = solve_with(factor, jnp.dot(kernels[1], error, precision=highest))
    intersection = jnp.sum(gamma * alpha)
    values = jnp.stack([alpha, gamma, error]).reshape(3, row_count, col_count, own, LANES)
    here = lax.dynamic_index_in_dim(values, col_index, 2, keepdims=False).reshape(3, rows, LANES)
    there = lax.dynamic_index_in_dim(values, row_index, 1, keepdims=False)
    there = lax.dynamic_slice_in_dim(
        jnp.concatenate([there, there], axis=1), col_index, col_count, 1
    ).reshape(3, -1, LANES)

    def outer(a, b):
        return jnp.dot(a, b.T, precision=highest)

    pair = -outer(here[1], there[0]) - outer(here[0], there[1])
    u, v = jnp.arange(rows)[:, None], jnp.arange(block // 2)[None, :]
    same = (u // own == row_index) & (v == u % own)
    pair = pair - jnp.where(same, intersection * (2.0 * ridge_scale / count), 0.0)
    weights = jnp.stack([pair, outer(here[0], there[2])]).reshape(2, rows, col_count, own)
    weights = jnp.transpose(weights, (1, 2, 0, 3)).reshape(rows, block)
    weights = jnp.pad(weights, ((0, 0), (0, LANES - block)))
    mine = (row_index * col_count + col_index) * own
    return (
        weights,
        lax.dynamic_slice_in_dim(gamma, mine, own, 0),
        jnp.full((SUBLANES, LANES), 0.5 * jnp.sum(error * error)),
    )


def body(support_views, support_pick, target_views, target_pick, support_labels, target_labels):
    own, _, channels, pixels = support_views.shape
    side = math.isqrt(pixels)
    classes = support_labels.shape[1]
    row_count = lax.axis_size("row")
    col_count = lax.axis_size("col")
    row_index = lax.axis_index("row")
    col_index = lax.axis_index("col")
    own_support = choose_view(support_views, support_pick)
    own_target = choose_view(target_views, target_pick)

    both = jnp.stack([own_support, own_target]).reshape(2 * own, channels, side, side)
    chunk = jnp.transpose(both, (1, 2, 0, 3)).reshape(channels, side, 2 * own * side)
    chunks = [chunk]
    for d in range(1, col_count):
        pairs = [((i + d) % col_count, i) for i in range(col_count)]
        chunks.append(lax.ppermute(chunk, "col", pairs))
    v_rows = []
    taken = 0
    for share in SHARES:
        width = share * col_count // sum(SHARES)
        part = jnp.concatenate(chunks[taken : taken + width], axis=-1) if width > 1 else chunks[taken]
        v_rows.append(part.reshape(channels, side, -1, LANES))
        taken += width

    row_images = lax.all_gather(own_support, "row", axis=0, tiled=True)
    groups = row_images.shape[0] // SUBLANES
    narrow = jnp.transpose(
        row_images.reshape(groups, SUBLANES, channels, side, side), (2, 3, 0, 1, 4)
    )
    rows, tile = narrow, None
    batches = []
    first = 0
    for columns in v_rows:
        rows, tile, angles, roots = pair_forward(rows, columns, first, tile)
        batches.append((angles, roots, columns))
        first += columns.shape[2]
    devices = row_count * col_count
    labels = jnp.pad(support_labels, ((0, 0), (0, LANES - classes)))
    parcel = jnp.concatenate([tile, labels], axis=0)
    gathered = lax.all_to_all(
        jnp.broadcast_to(parcel[None], (devices,) + parcel.shape), AXES, 0, 0, tiled=True
    )
    lanes = jnp.arange(LANES, dtype=jnp.int32)[None, :]
    onehot = jnp.where(
        lanes < classes, (target_labels[:, None] == lanes).astype(jnp.float32) - 1.0 / classes, 0.0
    )
    fits = own == SUBLANES and 2 * col_count * own == LANES and row_count % 2 == 0
    solve = solve_in_kernel if fits else solve_plainly
    weights, gamma_own, loss = solve(
        gathered, onehot, row_index, col_index, row_count, col_count, own
    )
    grads = pair_backward(weights, rows, batches)
    if own == SUBLANES:
        support_grad = lax.dynamic_index_in_dim(grads, row_index, 0, keepdims=False)
        for k in range(1, row_count):
            pairs = [(i, (i + k) % row_count) for i in range(row_count)]
            there = lax.dynamic_index_in_dim(grads, (row_index + k) % row_count, 0, keepdims=False)
            support_grad = support_grad + lax.ppermute(there, "row", pairs)
        support_grad = jnp.transpose(support_grad, (2, 1, 0, 3))
    else:
        grads = jnp.transpose(grads, (0, 3, 2, 1, 4)).reshape(row_count * own, channels, pixels)
        support_grad = lax.psum_scatter(grads, "row", scatter_dimension=0, tiled=True)
    support_grad = support_grad.reshape(own, channels, pixels)
    return (support_grad, gamma_own[:, :classes], loss[0, 0])


def solution(mesh):
    return jax.shard_map(
        body,
        mesh=mesh,
        in_specs=(
            P(AXES, None, None, None),
            P(AXES),
            P(AXES, None, None, None),
            P(AXES),
            P(AXES, None),
            P(),
        ),
        out_specs=(P(AXES, None, None), P(AXES, None), P()),
        check_vma=False,
    )
```

```python
import math

import jax
import jax.numpy as jnp
from jax import lax
from jax.experimental import pallas as pl
from jax.experimental.pallas import tpu as pltpu
from jax.sharding import PartitionSpec as P

LAYERS = 3
LANES = 128
SUBLANES = 8
PART = 8
FORWARD_PART = 7
BLOCK = 64
ROWS = 2
RING = 8

bias_variance = 0.1
ridge_scale = 0.1
highest = lax.Precision.HIGHEST
tiny = 1e-30
PI = math.pi

ACOS = (
    1.4142137164552202,
    0.11783707507052552,
    0.026725055357041356,
    0.00674552756719407,
    0.005608499939250727,
    -0.0026297111285195295,
    0.002296009448189848,
)
SINE = (
    0.31830981148327425,
    0.032252498831491,
    0.001158328114192081,
    2.2834735017183973e-05,
)
AXES = ("row", "col")


def horner(coefficients, x):
    total = coefficients[-1] * x + coefficients[-2]
    for coefficient in coefficients[-3::-1]:
        total = total * x + coefficient
    return total


def choose_view(views, picked):
    options = jnp.arange(views.shape[1], dtype=jnp.int32)
    selector = (picked[:, None] == options[None, :]).astype(jnp.float32)
    return jnp.sum(selector[:, :, None, None] * views, axis=1)


def edges(side, shape):
    x = lax.broadcasted_iota(jnp.int32, shape, len(shape) - 1) % side
    return x > 0, x < side - 1


def across(surface, masks):
    axis = surface.ndim - 1
    left = jnp.where(masks[0], pltpu.roll(surface, 1, axis), 0.0)
    right = jnp.where(masks[1], pltpu.roll(surface, LANES - 1, axis), 0.0)
    return surface + left + right


def map_scale(channels, layer):
    return 9.0 * channels if layer == 0 else 9.0


def forward_kernel(side, channels, groups, packs, first, *refs):
    if first == 0:
        narrow_ref, v_ref = refs[:2]
        u_ref, *u_map_refs = refs[2 : 3 + LAYERS]
        u_sums_ref = refs[-1]
        outs = refs[3 + LAYERS : -1]
    else:
        u_ref, v_ref = refs[:2]
        u_map_refs = refs[2 : 2 + LAYERS]
        past_ref = refs[2 + LAYERS]
        outs = refs[3 + LAYERS :]
    angle_refs = outs[:LAYERS]
    root_refs = outs[LAYERS : 2 * LAYERS]
    tile_ref = outs[2 * LAYERS]
    sums_ref, own_sums_ref, total_ref, inverse_ref = outs[2 * LAYERS + 1 :]
    step = pl.program_id(0)
    steps = side // ROWS
    masks = edges(side, (SUBLANES, LANES))
    own_masks = edges(side, (packs, LANES))
    width = packs if packs <= PART else FORWARD_PART
    blocks = [range(start, min(start + width, packs)) for start in range(0, packs, width)]

    def slot(row):
        return row & (RING - 1)

    def spread(line):
        return jnp.broadcast_to(line, (SUBLANES, LANES))

    if first == 0:

        @pl.when(step == 0)
        def _():
            for layer in range(LAYERS):
                u_sums_ref[layer, RING - 1] = jnp.zeros(u_sums_ref.shape[2:], jnp.float32)

        for layer in range(LAYERS):

            @pl.when(step == steps + layer)
            def _(layer=layer):
                u_sums_ref[layer, slot(side)] = jnp.zeros(u_sums_ref.shape[2:], jnp.float32)

        @pl.when(step < steps)
        def _():
            for r in range(ROWS):
                for g in range(groups):
                    energy = None
                    for c in range(channels):
                        plane = jnp.concatenate([narrow_ref[c, r, g]] * (LANES // side), axis=-1)
                        u_ref[c, r, g] = plane
                        energy = plane * plane if energy is None else energy + plane * plane
                    u_sums_ref[0, slot(step * ROWS + r), g] = across(energy, masks)

    def row_maps(layer):
        scale = map_scale(channels, layer)
        for r in range(ROWS):
            row = (step - 1 - layer) * ROWS + r
            for g in range(groups):
                total = (
                    u_sums_ref[layer, slot(row - 1), g]
                    + u_sums_ref[layer, slot(row), g]
                    + u_sums_ref[layer, slot(row + 1), g]
                )
                current = total * (1.0 / scale) + bias_variance
                inverse = lax.rsqrt(current)
                u_map_refs[layer][r, 0, g] = inverse * (1.0 / scale)
                u_map_refs[layer][r, 1, g] = current * inverse * (1.0 / PI)
                if layer + 1 < LAYERS:
                    u_sums_ref[layer + 1, slot(row), g] = across(current, masks)

    @pl.when(step == 0)
    def _():
        total_ref[...] = jnp.zeros(total_ref.shape, jnp.float32)
        for layer in range(LAYERS):
            sums_ref[layer, RING - 1] = jnp.zeros(sums_ref.shape[2:], jnp.float32)
            own_sums_ref[layer, RING - 1] = jnp.zeros(own_sums_ref.shape[2:], jnp.float32)

    for layer in range(LAYERS):

        @pl.when(step == steps + layer)
        def _(layer=layer):
            sums_ref[layer, slot(side)] = jnp.zeros(sums_ref.shape[2:], jnp.float32)
            own_sums_ref[layer, slot(side)] = jnp.zeros(own_sums_ref.shape[2:], jnp.float32)

    def product_stage(block):
        for r in range(ROWS):
            where = slot(step * ROWS + r)
            if block is blocks[0]:
                energy = None
                for c in range(channels):
                    plane = v_ref[c, r]
                    energy = plane * plane if energy is None else energy + plane * plane
                own_sums_ref[0, where] = across(energy, own_masks)
            for pack in block:
                lines = [spread(v_ref[c, r, pack : pack + 1, :]) for c in range(channels)]
                for g in range(groups):
                    product = None
                    for c in range(channels):
                        part = u_ref[c, r, g] * lines[c]
                        product = part if product is None else product + part
                    sums_ref[0, where, pack * groups + g] = across(product, masks)

    def arc_stage(layer, block):
        if first == 0:
            row_maps(layer)
        scale = map_scale(channels, layer)
        offset = scale * bias_variance
        rows = [(step - 1 - layer) * ROWS + r for r in range(ROWS)]
        near = [slot(rows[0] + r) for r in range(-1, ROWS + 1)]
        inverses, roots = [], []
        for r in range(ROWS if block is blocks[0] else 0):
            own_total = own_sums_ref[layer, near[r]] + own_sums_ref[layer, near[r + 1]] + own_sums_ref[layer, near[r + 2]]
            own_map = own_total * (1.0 / scale) + bias_variance
            inverse = lax.rsqrt(own_map)
            inverses.append(inverse)
            roots.append(own_map * inverse)
            root_refs[layer][r] = roots[r]
            inverse_ref[layer, r] = inverse
            if layer + 1 < LAYERS:
                own_sums_ref[layer + 1, near[r + 1]] = across(own_map, own_masks)
        if block is not blocks[0]:
            inverses = [inverse_ref.at[layer, r] for r in range(ROWS)]
            roots = [root_refs[layer].at[r] for r in range(ROWS)]
        for pack in block:
            for g in range(groups):
                at = pack * groups + g
                for r in range(0, ROWS, 2):
                    lines = [sums_ref[layer, near[r + k], at] for k in range(4)]
                    middle = (lines[1] + lines[2]) + offset
                    for k, summed in enumerate((lines[0] + middle, middle + lines[3])):
                        right_inverse = spread(inverses[r + k][pack : pack + 1, :])
                        right_root = spread(roots[r + k][pack : pack + 1, :])
                        cosine = summed * u_map_refs[layer][r + k, 0, g] * right_inverse
                        gap = 1.0 - (jnp.abs(cosine) if layer == 0 else cosine)
                        gap = jnp.maximum(gap, tiny)
                        theta = gap * lax.rsqrt(gap)
                        rest = 2.0 - gap
                        sine = theta * (rest * lax.rsqrt(rest))
                        theta = theta * horner(ACOS, gap)
                        angle = PI - theta
                        if layer == 0:
                            angle = jnp.where(cosine >= 0.0, angle, theta)
                        angle_refs[layer][r + k, at] = angle
                        value = (cosine * angle + sine) * u_map_refs[layer][r + k, 1, g] * right_root
                        if layer + 1 < LAYERS:
                            sums_ref[layer + 1, near[r + k + 1], at] = across(value, masks)
                        else:
                            total_ref[at] += value

    for block in blocks:
        pl.when(step < steps)(lambda block=block: product_stage(block))
    for layer in range(LAYERS):
        for block in blocks:
            pl.when((step > layer) & (step <= steps + layer))(
                lambda layer=layer, block=block: arc_stage(layer, block)
            )

    @pl.when(step == steps + LAYERS - 1)
    def _():
        lane = lax.broadcasted_iota(jnp.int32, (LANES, LANES), 1)
        from_lane = lax.broadcasted_iota(jnp.int32, (LANES, LANES), 0)
        copies = LANES // side
        folding = jnp.where(lane % copies == from_lane // side, 1.0 / (side * side), 0.0)
        means = jnp.dot(total_ref[...].reshape(-1, LANES), folding, precision=highest)
        place = lax.broadcasted_iota(jnp.int32, (SUBLANES, LANES), 1) // copies
        for g in range(groups):
            mine = slice(g * SUBLANES, (g + 1) * SUBLANES)
            line = jnp.zeros((SUBLANES, LANES), jnp.float32) if first == 0 else past_ref[mine, :]
            for pack in range(packs):
                at = (pack * groups + g) * SUBLANES
                line = jnp.where(place == first + pack, means[at : at + SUBLANES], line)
            tile_ref[mine, :] = line


def pair_forward(rows, v_rows, first, tile):
    channels, side, groups = (rows if first == 0 else rows[0]).shape[:3]
    packs = v_rows.shape[2]
    steps = side // ROWS
    count = packs * groups
    f32 = jnp.float32

    def lag(layer, trailing):
        return lambda i: (jnp.clip(i - 1 - layer, 0, steps - 1),) + (0,) * trailing

    def now(trailing):
        return lambda i: (0, jnp.minimum(i, steps - 1)) + (0,) * trailing

    image = pl.BlockSpec((channels, ROWS, groups, SUBLANES, LANES), now(3))
    maps = [pl.BlockSpec((ROWS, 2, groups, SUBLANES, LANES), lag(layer, 4)) for layer in range(LAYERS)]
    column = pl.BlockSpec((channels, ROWS, packs, LANES), now(2))
    whole = pl.BlockSpec((groups * SUBLANES, LANES), lambda i: (0, 0))
    out_shape = (
        [jax.ShapeDtypeStruct((side, count, SUBLANES, LANES), f32)] * LAYERS
        + [jax.ShapeDtypeStruct((side, packs, LANES), f32)] * LAYERS
        + [jax.ShapeDtypeStruct((groups * SUBLANES, LANES), f32)]
    )
    out_specs = (
        [pl.BlockSpec((ROWS, count, SUBLANES, LANES), lag(layer, 3)) for layer in range(LAYERS)]
        + [pl.BlockSpec((ROWS, packs, LANES), lag(layer, 2)) for layer in range(LAYERS)]
        + [whole]
    )
    scratch_shapes = [
        pltpu.VMEM((LAYERS, RING, count, SUBLANES, LANES), f32),
        pltpu.VMEM((LAYERS, RING, packs, LANES), f32),
        pltpu.VMEM((count, SUBLANES, LANES), f32),
        pltpu.VMEM((LAYERS, ROWS, packs, LANES), f32),
    ]
    if first == 0:
        operands = [rows, v_rows]
        in_specs = [pl.BlockSpec((channels, ROWS, groups, SUBLANES, side), now(3)), column]
        out_shape = (
            [jax.ShapeDtypeStruct((channels, side, groups, SUBLANES, LANES), f32)]
            + [jax.ShapeDtypeStruct((side, 2, groups, SUBLANES, LANES), f32)] * LAYERS
            + out_shape
        )
        out_specs = [image] + maps + out_specs
        scratch_shapes = scratch_shapes + [pltpu.VMEM((LAYERS, RING, groups, SUBLANES, LANES), f32)]
    else:
        operands = [rows[0], v_rows, *rows[1:], tile]
        in_specs = [image, column] + maps + [whole]
    results = pl.pallas_call(
        lambda *refs: forward_kernel(side, channels, groups, packs, first, *refs),
        out_shape=out_shape,
        grid=(steps + LAYERS,),
        in_specs=in_specs,
        out_specs=out_specs,
        scratch_shapes=scratch_shapes,
        name="pair_forward",
    )(*operands)
    if first == 0:
        rows, results = results[: 1 + LAYERS], results[1 + LAYERS :]
    return rows, results[-1], results[:LAYERS], results[LAYERS : 2 * LAYERS]


def backward_kernel(side, channels, groups, packs, *refs):
    weight_ref, u_ref = refs[0], refs[1]
    u_map_refs = refs[2 : 2 + LAYERS]
    taken = 2 + LAYERS
    angle_refs, root_refs, image_refs = [], [], []
    for batch in range(len(packs)):
        angle_refs.append(refs[taken : taken + LAYERS])
        root_refs.append(refs[taken + LAYERS : taken + 2 * LAYERS])
        image_refs.append(refs[taken + 2 * LAYERS])
        taken += 2 * LAYERS + 1
    grad_ref, sums_ref, own_sums_ref, wide_ref, total_ref = refs[taken:]
    parts = [(batch, pack) for batch in range(len(packs)) for pack in range(packs[batch])]
    blocks = [
        list(enumerate(parts))[start : start + PART] for start in range(0, len(parts), PART)
    ]
    step = pl.program_id(0)
    steps = side // ROWS
    masks = edges(side, (SUBLANES, LANES))
    shrink = 1.0 / (9.0 * PI)
    pixels = side * side

    def slot(row):
        return row & (RING - 1)

    def fold(total):
        total = total + pltpu.roll(total, 2 * side, 1)
        return total + pltpu.roll(total, side, 1)

    def spread(line):
        return jnp.broadcast_to(line, (SUBLANES, LANES))

    def summed(ref, depth, row, at):
        lines = [ref[depth, slot(row + k), at] for k in range(-1, ROWS + 1)]
        totals = []
        for r in range(0, ROWS, 2):
            middle = lines[r + 1] + lines[r + 2]
            totals += [lines[r] + middle, middle + lines[r + 3]]
        return totals

    def add(total, part):
        return part if total is None else total + part

    @pl.when(step == 0)
    def _():
        lane = lax.broadcasted_iota(jnp.int32, (SUBLANES, LANES), 1)
        for pack in range(len(parts)):
            index = lane // side + pack * (LANES // side)
            for g in range(groups):
                line = weight_ref[g * SUBLANES : (g + 1) * SUBLANES, :]
                wide_ref[pack * groups + g] = jnp.take_along_axis(line, index, axis=1)
        for depth in range(LAYERS):
            sums_ref[depth, RING - 1] = jnp.zeros(sums_ref.shape[2:], jnp.float32)
            own_sums_ref[depth, RING - 1] = jnp.zeros(own_sums_ref.shape[2:], jnp.float32)

    for depth in range(LAYERS):

        @pl.when(step == steps + depth)
        def _(depth=depth):
            sums_ref[depth, slot(side)] = jnp.zeros(sums_ref.shape[2:], jnp.float32)
            own_sums_ref[depth, slot(side)] = jnp.zeros(own_sums_ref.shape[2:], jnp.float32)

    def layer_block(depth, block):
        layer = LAYERS - 1 - depth
        row = (step - depth) * ROWS
        totals = [[None] * groups for _ in range(ROWS)]
        for part, (batch, pack) in blocks[block]:
            for g in range(groups):
                inner = pack * groups + g
                at = part * groups + g
                if depth == 0:
                    grads = [wide_ref[at]] * ROWS
                else:
                    grads = summed(sums_ref, depth - 1, row, at)
                for r, grad in enumerate(grads):
                    angle = angle_refs[batch][layer][r, inner]
                    sums_ref[depth, slot(row + r), at] = across(grad * angle, masks)
                    product = angle * (PI - angle)
                    root = spread(root_refs[batch][layer][r, pack : pack + 1, :])
                    totals[r][g] = add(totals[r][g], grad * root * (product * horner(SINE, product)))
        for r in range(ROWS):
            for g in range(groups):
                total = totals[r][g]
                total_ref[depth, r, g] = total if block == 0 else total_ref[depth, r, g] + total

    def layer_end(depth):
        layer = LAYERS - 1 - depth
        row = (step - depth) * ROWS
        factor = shrink**depth / (pixels * 2.0 * PI * PI)
        for g in range(groups):
            above = summed(own_sums_ref, depth - 1, row, g) if depth > 0 else None
            for r in range(ROWS):
                carry = fold(total_ref[depth, r, g]) * (factor / u_map_refs[layer][r, 1, g])
                if depth > 0:
                    carry = carry + above[r] * (1.0 / 9.0)
                own_sums_ref[depth, slot(row + r), g] = across(carry, masks)

    def image_block(block):
        row = (step - LAYERS) * ROWS
        totals = [[[None] * groups for _ in range(channels)] for _ in range(ROWS)]
        for part, (batch, pack) in blocks[block]:
            for g in range(groups):
                at = part * groups + g
                for r, grad in enumerate(summed(sums_ref, LAYERS - 1, row, at)):
                    for c in range(channels):
                        line = spread(image_refs[batch][c, r, pack : pack + 1, :])
                        totals[r][c][g] = add(totals[r][c][g], grad * line)
        for r in range(ROWS):
            for c in range(channels):
                for g in range(groups):
                    total, at = totals[r][c][g], LAYERS + c
                    total_ref[at, r, g] = total if block == 0 else total_ref[at, r, g] + total

    def image_end():
        row = (step - LAYERS) * ROWS
        copies = LANES // side
        lane = lax.broadcasted_iota(jnp.int32, (SUBLANES, LANES), 1)
        for g in range(groups):
            above = summed(own_sums_ref, LAYERS - 1, row, g)
            for r in range(ROWS):
                carry = above[r] * (2.0 / (9.0 * channels))
                for c in range(channels):
                    image = fold(total_ref[LAYERS + c, r, g]) * (shrink**LAYERS / (pixels * channels))
                    image = image + carry * u_ref[c, r, g]
                    lines = grad_ref[g, 0, c]
                    grad_ref[g, 0, c] = jnp.where(lane // side == (row + r) % copies, image, lines)

    for depth in range(LAYERS):
        for block in range(len(blocks)):
            pl.when((step >= depth) & (step < steps + depth))(
                lambda depth=depth, block=block: layer_block(depth, block)
            )
        pl.when((step >= depth) & (step < steps + depth))(lambda depth=depth: layer_end(depth))
    for block in range(len(blocks)):
        pl.when(step >= LAYERS)(lambda block=block: image_block(block))
    pl.when(step >= LAYERS)(image_end)


def pair_backward(weights, rows, batches):
    channels, side, groups = rows[0].shape[:3]
    packs = [images.shape[2] for _, _, images in batches]
    steps = side // ROWS
    copies = LANES // side
    f32 = jnp.float32

    def at_lag(lag, trailing):
        return lambda i: (jnp.clip(i - lag, 0, steps - 1),) + (0,) * trailing

    def image_rows(trailing):
        return lambda i: (0, jnp.clip(i - LAYERS, 0, steps - 1)) + (0,) * trailing

    operands = [weights, *rows]
    in_specs = [
        pl.BlockSpec(weights.shape, lambda i: (0, 0)),
        pl.BlockSpec((channels, ROWS, groups, SUBLANES, LANES), image_rows(3)),
    ] + [
        pl.BlockSpec((ROWS, 2, groups, SUBLANES, LANES), at_lag(LAYERS - 1 - layer, 4))
        for layer in range(LAYERS)
    ]
    for (angles, roots, images), width in zip(batches, packs):
        for layer in range(LAYERS):
            operands.append(angles[layer])
            in_specs.append(
                pl.BlockSpec((ROWS, width * groups, SUBLANES, LANES), at_lag(LAYERS - 1 - layer, 3))
            )
        for layer in range(LAYERS):
            operands.append(roots[layer])
            in_specs.append(pl.BlockSpec((ROWS, width, LANES), at_lag(LAYERS - 1 - layer, 2)))
        operands.append(images)
        in_specs.append(pl.BlockSpec((channels, ROWS, width, LANES), image_rows(2)))
    count = sum(packs) * groups
    return pl.pallas_call(
        lambda *refs: backward_kernel(side, channels, groups, packs, *refs),
        out_shape=jax.ShapeDtypeStruct((groups, side // copies, channels, SUBLANES, LANES), f32),
        grid=(steps + LAYERS,),
        in_specs=in_specs,
        out_specs=pl.BlockSpec(
            (groups, 1, channels, SUBLANES, LANES),
            lambda i: (0, jnp.clip(i - LAYERS, 0, steps - 1) * ROWS // copies, 0, 0, 0),
        ),
        scratch_shapes=[
            pltpu.VMEM((LAYERS, RING, count, SUBLANES, LANES), f32),
            pltpu.VMEM((LAYERS, RING, groups, SUBLANES, LANES), f32),
            pltpu.VMEM((count, SUBLANES, LANES), f32),
            pltpu.VMEM((LAYERS + channels, ROWS, groups, SUBLANES, LANES), f32),
        ],
        name="pair_backward",
    )(*operands)


def eliminate(panel):
    height, width = panel.shape
    tiles = [panel[:, start : start + LANES] for start in range(0, width, LANES)]
    lane = lax.broadcasted_iota(jnp.int32, tiles[0].shape, 1)
    row = lax.broadcasted_iota(jnp.int32, tiles[0].shape, 0)
    for j in range(0, height, 2):
        k = j + 1
        first = jnp.broadcast_to(tiles[0][:, j : j + 1], tiles[0].shape)
        second = jnp.broadcast_to(tiles[0][:, k : k + 1], tiles[0].shape)
        a, b, d = first[j : j + 1], first[k : k + 1], second[k : k + 1]
        scale = 1.0 / (a * d - b * b)
        a, b, d = a * scale, b * scale, d * scale
        for t, tile in enumerate(tiles):
            upper, lower = tile[j : j + 1], tile[k : k + 1]
            if t == 0:
                upper = jnp.where(lane[:1] == j, 1.0, jnp.where(lane[:1] == k, 0.0, upper))
                lower = jnp.where(lane[:1] == k, 1.0, jnp.where(lane[:1] == j, 0.0, lower))
                tile = jnp.where((lane == j) | (lane == k), 0.0, tile)
            upper, lower = d * upper - b * lower, a * lower - b * upper
            rest = tile - first * upper - second * lower
            tiles[t] = jnp.where(row == j, upper, jnp.where(row == k, lower, rest))
    return jnp.concatenate(tiles, axis=1)


def lane_of(kind, d, k, col_count, own, near):
    far = 2 * near * own + (kind * (col_count - near) + d - near) * own + k
    return jnp.where(d < near, (2 * d + kind) * own + k, far)


def sorting(kind, col_count, own, near):
    i = lax.broadcasted_iota(jnp.int32, (LANES, LANES), 0)
    j = lax.broadcasted_iota(jnp.int32, (LANES, LANES), 1) % (LANES // 2)
    return (i == lane_of(kind, j // own, j % own, col_count, own, near)).astype(jnp.float32)


def exact_dot(a, b, da=1, db=0):
    return lax.dot_general(
        a, b, (((da,), (db,)), ((), ())), precision=highest, preferred_element_type=jnp.float32
    )


def whole_matrix(kind, row_count, col_count, own, near, gathered_ref, big_ref):
    count = row_count * col_count * own
    rows = row_count * own
    half = LANES // 2
    for r in range(row_count):
        for c in range(col_count):
            tile = gathered_ref[r * col_count + c, :rows, :]
            for r2 in range(row_count):
                at = (c * row_count + r2) * own
                big_ref[r, at : at + own, :] = tile[r2 * own : (r2 + 1) * own]
    parts = exact_dot(
        big_ref[...].reshape(row_count * count, LANES), sorting(kind, col_count, own, near)
    ).reshape(row_count, count, LANES)
    lane = lax.broadcasted_iota(jnp.int32, (rows, LANES), 1)
    for c in range(col_count):
        for t in range(row_count // 2):
            even, odd = (
                pltpu.roll(part, own * c, 1) if c else part
                for part in (parts[2 * t, c * rows : (c + 1) * rows], parts[2 * t + 1, c * rows : (c + 1) * rows])
            )
            joined = jnp.where(lane < half, even, odd)
            for r2 in range(row_count):
                at = (r2 * col_count + c) * own
                big_ref[t, at : at + own, :] = joined[r2 * own : (r2 + 1) * own]
    return jnp.concatenate([big_ref[t] for t in range(row_count // 2)], axis=1)


def solve_from(inverse_ref, system_ref, right):
    first = exact_dot(inverse_ref[...], right)
    return first + exact_dot(inverse_ref[...], right - exact_dot(system_ref[...], first))


def invert_kernel(row_count, col_count, own, near, gathered_ref, *refs):
    system_ref, inverse_ref, alpha_ref, big_ref, label_ref = refs
    count = row_count * col_count * own
    rows = row_count * own
    support = whole_matrix(0, row_count, col_count, own, near, gathered_ref, big_ref)
    for source in range(row_count * col_count):
        label_ref[source * own : (source + 1) * own, :] = gathered_ref[source, rows : rows + own, :]
    wide_lane = lax.broadcasted_iota(jnp.int32, (count, count), 1)
    wide_row = lax.broadcasted_iota(jnp.int32, (count, count), 0)
    ridge = jnp.sum(jnp.where(wide_lane == wide_row, support, 0.0)) * (ridge_scale / count)
    system = support + jnp.where(wide_lane == wide_row, ridge, 0.0)
    system_ref[...] = system
    inverse_ref[...] = system
    rest_lane = lax.broadcasted_iota(jnp.int32, (count - BLOCK, count), 1)

    def one_block(step, carry):
        reduced = eliminate(inverse_ref[:BLOCK, :])
        below = inverse_ref[BLOCK:, :]
        below = jnp.where(rest_lane < BLOCK, 0.0, below) - exact_dot(below[:, :BLOCK], reduced)
        inverse_ref[: count - BLOCK, :] = pltpu.roll(below, count - BLOCK, 1)
        inverse_ref[count - BLOCK :, :] = pltpu.roll(reduced, count - BLOCK, 1)
        return carry

    lax.fori_loop(0, count // BLOCK, one_block, 0)
    alpha_ref[...] = solve_from(inverse_ref, system_ref, label_ref[...])


def weights_kernel(row_count, col_count, own, near, place_ref, gathered_ref, onehot_ref, *refs):
    system_ref, inverse_ref, alpha_ref, weight_ref, gamma_ref, loss_ref, big_ref, row_ref = refs
    row_index, col_index = place_ref[0], place_ref[1]
    count = row_count * col_count * own
    block = col_count * own
    cross = whole_matrix(1, row_count, col_count, own, near, gathered_ref, big_ref)
    alpha = alpha_ref[...]
    error = exact_dot(cross, alpha, 0, 0) - onehot_ref[...]
    loss_ref[...] = jnp.broadcast_to(0.5 * jnp.sum(error * error), loss_ref.shape)
    gamma = solve_from(inverse_ref, system_ref, exact_dot(cross, error))
    intersection = jnp.sum(gamma * alpha)
    row_ref[0] = alpha
    row_ref[1] = gamma
    row_ref[2] = error
    mine = pl.multiple_of((row_index * col_count + col_index) * own, own)
    gamma_ref[...] = row_ref[1, pl.ds(mine, own), :]

    def rows_here(which):
        starts = [pl.multiple_of((r2 * col_count + col_index) * own, own) for r2 in range(row_count)]
        return jnp.concatenate([row_ref[which, pl.ds(start, own), :] for start in starts], axis=0)

    def columns_here(which):
        here = row_ref[which, pl.ds(pl.multiple_of(row_index * block, block), block), :]
        return jnp.concatenate([here, here], axis=0)

    alpha_rows, gamma_rows = rows_here(0), rows_here(1)
    pair = -exact_dot(gamma_rows, columns_here(0), 1, 1) - exact_dot(alpha_rows, columns_here(1), 1, 1)
    target = exact_dot(alpha_rows, columns_here(2), 1, 1)
    u = lax.broadcasted_iota(jnp.int32, pair.shape, 0)
    v = lax.broadcasted_iota(jnp.int32, pair.shape, 1)
    same = (u // own == row_index) & (v % block == col_index * own + u % own)
    pair = pair - jnp.where(same, intersection * (2.0 * ridge_scale / count), 0.0)
    total = None
    for kind, part in enumerate((pair, target)):
        turned = pltpu.roll(part, (LANES - own * col_index) % LANES, 1)
        turned = jnp.where(v < block, turned, 0.0)
        back = exact_dot(turned, sorting(kind, col_count, own, near), 1, 1)
        total = back if total is None else total + back
    weight_ref[...] = total


def invert_in_kernel(gathered, row_count, col_count, own, near):
    f32 = jnp.float32
    count = row_count * col_count * own
    vmem = pl.BlockSpec(memory_space=pltpu.VMEM)
    square = jax.ShapeDtypeStruct((count, count), f32)
    return pl.pallas_call(
        lambda *refs: invert_kernel(row_count, col_count, own, near, *refs),
        out_shape=[square, square, jax.ShapeDtypeStruct((count, LANES), f32)],
        in_specs=[vmem],
        out_specs=[vmem] * 3,
        scratch_shapes=[
            pltpu.VMEM((row_count, count, LANES), f32),
            pltpu.VMEM((count, LANES), f32),
        ],
        name="invert",
    )(gathered)


def weights_in_kernel(gathered, onehot, solved, row_index, col_index, row_count, col_count, own, near):
    f32 = jnp.float32
    count = row_count * col_count * own
    vmem = pl.BlockSpec(memory_space=pltpu.VMEM)
    return pl.pallas_call(
        lambda *refs: weights_kernel(row_count, col_count, own, near, *refs),
        out_shape=[
            jax.ShapeDtypeStruct((row_count * own, LANES), f32),
            jax.ShapeDtypeStruct((own, LANES), f32),
            jax.ShapeDtypeStruct((SUBLANES, LANES), f32),
        ],
        in_specs=[pl.BlockSpec(memory_space=pltpu.SMEM)] + [vmem] * 5,
        out_specs=[vmem] * 3,
        scratch_shapes=[
            pltpu.VMEM((row_count, count, LANES), f32),
            pltpu.VMEM((3, count, LANES), f32),
        ],
        name="weights",
    )(jnp.stack([row_index, col_index]).astype(jnp.int32), gathered, onehot, *solved)


def solve_with(factor, rhs):
    halfway = lax.linalg.triangular_solve(factor, rhs, left_side=True, lower=True)
    return lax.linalg.triangular_solve(factor, halfway, left_side=True, lower=True, transpose_a=True)


def solve_plainly(gathered, onehot, row_index, col_index, row_count, col_count, own, near):
    count = row_count * col_count * own
    rows = row_count * own
    block = 2 * col_count * own
    labels = gathered[:, rows : rows + own].reshape(count, LANES)
    kernels, sorts = [], []
    for kind in range(2):
        j = jnp.arange(block // 2, dtype=jnp.int32)[None, :]
        lanes = lane_of(kind, j // own, j % own, col_count, own, near)
        sort = (jnp.arange(LANES, dtype=jnp.int32)[:, None] == lanes).astype(jnp.float32)
        sorts.append(sort)
        picked = jnp.dot(gathered[:, :rows].reshape(-1, LANES), sort, precision=highest)
        picked = picked.reshape(row_count, col_count, row_count, own, block // 2)
        picked = jnp.stack(
            [jnp.roll(picked[:, c], c * own, axis=-1) for c in range(col_count)], axis=1
        )
        kernels.append(jnp.transpose(picked, (2, 1, 3, 0, 4)).reshape(count, count))
    identity = jnp.eye(count, dtype=jnp.float32)
    ridge = jnp.trace(kernels[0]) * (ridge_scale / count)
    factor = jnp.linalg.cholesky(kernels[0] + ridge * identity)
    alpha = solve_with(factor, labels)
    error = jnp.dot(kernels[1].T, alpha, precision=highest) - onehot
    gamma = solve_with(factor, jnp.dot(kernels[1], error, precision=highest))
    intersection = jnp.sum(gamma * alpha)
    values = jnp.stack([alpha, gamma, error]).reshape(3, row_count, col_count, own, LANES)
    here = lax.dynamic_index_in_dim(values, col_index, 2, keepdims=False).reshape(3, rows, LANES)
    there = lax.dynamic_index_in_dim(values, row_index, 1, keepdims=False)
    there = lax.dynamic_slice_in_dim(
        jnp.concatenate([there, there], axis=1), col_index, col_count, 1
    ).reshape(3, -1, LANES)

    def outer(a, b):
        return jnp.dot(a, b.T, precision=highest)

    pair = -outer(here[1], there[0]) - outer(here[0], there[1])
    u, v = jnp.arange(rows)[:, None], jnp.arange(block // 2)[None, :]
    same = (u // own == row_index) & (v == u % own)
    pair = pair - jnp.where(same, intersection * (2.0 * ridge_scale / count), 0.0)
    weights = outer(pair, sorts[0]) + outer(outer(here[0], there[2]), sorts[1])
    mine = (row_index * col_count + col_index) * own
    return (
        weights,
        lax.dynamic_slice_in_dim(gamma, mine, own, 0),
        jnp.full((SUBLANES, LANES), 0.5 * jnp.sum(error * error)),
    )


def body(support_views, support_pick, target_views, target_pick, support_labels, target_labels):
    own, _, channels, pixels = support_views.shape
    side = math.isqrt(pixels)
    classes = support_labels.shape[1]
    row_count = lax.axis_size("row")
    col_count = lax.axis_size("col")
    row_index = lax.axis_index("row")
    col_index = lax.axis_index("col")
    own_support = choose_view(support_views, support_pick)
    own_target = choose_view(target_views, target_pick)

    both = jnp.stack([own_support, own_target]).reshape(2 * own, channels, side, side)
    chunk = jnp.transpose(both, (1, 2, 0, 3)).reshape(channels, side, 2 * own * side)
    chunks = [chunk]
    for d in range(1, col_count):
        pairs = [((i + d) % col_count, i) for i in range(col_count)]
        chunks.append(lax.ppermute(chunk, "col", pairs))
    near = 1 if own % (LANES // side) == 0 else LANES // side
    middle = own * side
    v_rows = [
        jnp.concatenate(chunks[:near], axis=-1) if near > 1 else chunk,
        jnp.concatenate([part[..., :middle] for part in chunks[near:]], axis=-1),
        jnp.concatenate([part[..., middle:] for part in chunks[near:]], axis=-1),
    ]
    v_rows = [part.reshape(channels, side, -1, LANES) for part in v_rows]

    row_images = lax.all_gather(own_support, "row", axis=0, tiled=True)
    groups = row_images.shape[0] // SUBLANES
    narrow = jnp.transpose(
        row_images.reshape(groups, SUBLANES, channels, side, side), (2, 3, 0, 1, 4)
    )
    devices = row_count * col_count
    labels = jnp.pad(support_labels, ((0, 0), (0, LANES - classes)))
    lanes = jnp.arange(LANES, dtype=jnp.int32)[None, :]
    onehot = jnp.where(
        lanes < classes, (target_labels[:, None] == lanes).astype(jnp.float32) - 1.0 / classes, 0.0
    )

    def to_all(parcel):
        copies = jnp.broadcast_to(parcel[None], (devices,) + parcel.shape)
        return lax.all_to_all(copies, AXES, 0, 0, tiled=True)

    rows, tile = narrow, None
    batches, tiles = [], []
    first = 0
    for columns in v_rows:
        rows, tile, angles, roots = pair_forward(rows, columns, first, tile)
        batches.append((angles, roots, columns))
        tiles.append(tile)
        first += columns.shape[2]
    sizes = (row_count, col_count, own, near)
    if own == SUBLANES and 2 * col_count * own == LANES and row_count % 2 == 0:
        support_tiles = to_all(jnp.concatenate([tiles[1], labels], axis=0))
        target_tiles = to_all(tiles[2])
        solved = invert_in_kernel(support_tiles, *sizes)
        weights, gamma_own, loss = weights_in_kernel(
            target_tiles, onehot, solved, row_index, col_index, *sizes
        )
    else:
        gathered = to_all(jnp.concatenate([tiles[2], labels], axis=0))
        weights, gamma_own, loss = solve_plainly(gathered, onehot, row_index, col_index, *sizes)
    grads = pair_backward(weights, rows, batches)
    if own == SUBLANES:
        support_grad = lax.dynamic_index_in_dim(grads, row_index, 0, keepdims=False)
        for k in range(1, row_count):
            pairs = [(i, (i + k) % row_count) for i in range(row_count)]
            there = lax.dynamic_index_in_dim(grads, (row_index + k) % row_count, 0, keepdims=False)
            support_grad = support_grad + lax.ppermute(there, "row", pairs)
        support_grad = jnp.transpose(support_grad, (2, 1, 0, 3))
    else:
        grads = jnp.transpose(grads, (0, 3, 2, 1, 4)).reshape(row_count * own, channels, pixels)
        support_grad = lax.psum_scatter(grads, "row", scatter_dimension=0, tiled=True)
    support_grad = support_grad.reshape(own, channels, pixels)
    return (support_grad, gamma_own[:, :classes], loss[0, 0])


def solution(mesh):
    return jax.shard_map(
        body,
        mesh=mesh,
        in_specs=(
            P(AXES, None, None, None),
            P(AXES),
            P(AXES, None, None, None),
            P(AXES),
            P(AXES, None),
            P(),
        ),
        out_specs=(P(AXES, None, None), P(AXES, None), P()),
        check_vma=False,
    )
```

```python
import math

import jax
import jax.numpy as jnp
from jax import lax
from jax.experimental import pallas as pl
from jax.experimental.pallas import tpu as pltpu
from jax.sharding import PartitionSpec as P

LAYERS = 3
LANES = 128
SUBLANES = 8
PART = 8
FORWARD_PART = 7
BLOCK = 64
ROWS = 2
RING = 8

bias_variance = 0.1
ridge_scale = 0.1
highest = lax.Precision.HIGHEST
tiny = 1e-30
PI = math.pi

ACOS = (
    2.20239957601501,
    -0.9079020788090617,
    0.36298714579028,
    -0.09949097018131615,
    0.012802548128944304,
)
SINE = (
    0.31830981148327425,
    0.032252498831491,
    0.001158328114192081,
    2.2834735017183973e-05,
)
AXES = ("row", "col")


def horner(coefficients, x):
    total = coefficients[-1] * x + coefficients[-2]
    for coefficient in coefficients[-3::-1]:
        total = total * x + coefficient
    return total


def choose_view(views, picked):
    options = jnp.arange(views.shape[1], dtype=jnp.int32)
    selector = (picked[:, None] == options[None, :]).astype(jnp.float32)
    return jnp.sum(selector[:, :, None, None] * views, axis=1)


def edges(side, shape):
    x = lax.broadcasted_iota(jnp.int32, shape, len(shape) - 1) % side
    return x > 0, x < side - 1


def across(surface, masks):
    axis = surface.ndim - 1
    left = jnp.where(masks[0], pltpu.roll(surface, 1, axis), 0.0)
    right = jnp.where(masks[1], pltpu.roll(surface, LANES - 1, axis), 0.0)
    return surface + left + right


def map_scale(channels, layer):
    return 9.0 * channels if layer == 0 else 9.0


def forward_kernel(side, channels, groups, packs, first, *refs):
    if first == 0:
        narrow_ref, v_ref = refs[:2]
        u_ref, *u_map_refs = refs[2 : 3 + LAYERS]
        u_sums_ref = refs[-1]
        outs = refs[3 + LAYERS : -1]
    else:
        u_ref, v_ref = refs[:2]
        u_map_refs = refs[2 : 2 + LAYERS]
        past_ref = refs[2 + LAYERS]
        outs = refs[3 + LAYERS :]
    angle_refs = outs[:LAYERS]
    root_refs = outs[LAYERS : 2 * LAYERS]
    tile_ref = outs[2 * LAYERS]
    sums_ref, own_sums_ref, total_ref, inverse_ref = outs[2 * LAYERS + 1 :]
    step = pl.program_id(0)
    steps = side // ROWS
    masks = edges(side, (SUBLANES, LANES))
    own_masks = edges(side, (packs, LANES))
    width = packs if packs <= PART else FORWARD_PART
    blocks = [range(start, min(start + width, packs)) for start in range(0, packs, width)]

    def slot(row):
        return row & (RING - 1)

    def spread(line):
        return jnp.broadcast_to(line, (SUBLANES, LANES))

    if first == 0:

        @pl.when(step == 0)
        def _():
            for layer in range(LAYERS):
                u_sums_ref[layer, RING - 1] = jnp.zeros(u_sums_ref.shape[2:], jnp.float32)

        for layer in range(LAYERS):

            @pl.when(step == steps + layer)
            def _(layer=layer):
                u_sums_ref[layer, slot(side)] = jnp.zeros(u_sums_ref.shape[2:], jnp.float32)

        @pl.when(step < steps)
        def _():
            for r in range(ROWS):
                for g in range(groups):
                    energy = None
                    for c in range(channels):
                        plane = jnp.concatenate([narrow_ref[c, r, g]] * (LANES // side), axis=-1)
                        u_ref[c, r, g] = plane
                        energy = plane * plane if energy is None else energy + plane * plane
                    u_sums_ref[0, slot(step * ROWS + r), g] = across(energy, masks)

    def row_maps(layer):
        scale = map_scale(channels, layer)
        for r in range(ROWS):
            row = (step - 1 - layer) * ROWS + r
            for g in range(groups):
                total = (
                    u_sums_ref[layer, slot(row - 1), g]
                    + u_sums_ref[layer, slot(row), g]
                    + u_sums_ref[layer, slot(row + 1), g]
                )
                current = total * (1.0 / scale) + bias_variance
                inverse = lax.rsqrt(current)
                u_map_refs[layer][r, 0, g] = inverse * (1.0 / scale)
                u_map_refs[layer][r, 1, g] = current * inverse * (1.0 / PI)
                if layer + 1 < LAYERS:
                    u_sums_ref[layer + 1, slot(row), g] = across(current, masks)

    @pl.when(step == 0)
    def _():
        total_ref[...] = jnp.zeros(total_ref.shape, jnp.float32)
        for layer in range(LAYERS):
            sums_ref[layer, RING - 1] = jnp.zeros(sums_ref.shape[2:], jnp.float32)
            own_sums_ref[layer, RING - 1] = jnp.zeros(own_sums_ref.shape[2:], jnp.float32)

    for layer in range(LAYERS):

        @pl.when(step == steps + layer)
        def _(layer=layer):
            sums_ref[layer, slot(side)] = jnp.zeros(sums_ref.shape[2:], jnp.float32)
            own_sums_ref[layer, slot(side)] = jnp.zeros(own_sums_ref.shape[2:], jnp.float32)

    def product_stage(block):
        for r in range(ROWS):
            where = slot(step * ROWS + r)
            if block is blocks[0]:
                energy = None
                for c in range(channels):
                    plane = v_ref[c, r]
                    energy = plane * plane if energy is None else energy + plane * plane
                own_sums_ref[0, where] = across(energy, own_masks)
            for pack in block:
                lines = [spread(v_ref[c, r, pack : pack + 1, :]) for c in range(channels)]
                for g in range(groups):
                    product = None
                    for c in range(channels):
                        part = u_ref[c, r, g] * lines[c]
                        product = part if product is None else product + part
                    sums_ref[0, where, pack * groups + g] = across(product, masks)

    def arc_stage(layer, block):
        if first == 0:
            row_maps(layer)
        scale = map_scale(channels, layer)
        offset = scale * bias_variance
        rows = [(step - 1 - layer) * ROWS + r for r in range(ROWS)]
        near = [slot(rows[0] + r) for r in range(-1, ROWS + 1)]
        inverses, roots = [], []
        for r in range(ROWS if block is blocks[0] else 0):
            own_total = own_sums_ref[layer, near[r]] + own_sums_ref[layer, near[r + 1]] + own_sums_ref[layer, near[r + 2]]
            own_map = own_total * (1.0 / scale) + bias_variance
            inverse = lax.rsqrt(own_map)
            inverses.append(inverse)
            roots.append(own_map * inverse)
            root_refs[layer][r] = roots[r]
            inverse_ref[layer, r] = inverse
            if layer + 1 < LAYERS:
                own_sums_ref[layer + 1, near[r + 1]] = across(own_map, own_masks)
        if block is not blocks[0]:
            inverses = [inverse_ref.at[layer, r] for r in range(ROWS)]
            roots = [root_refs[layer].at[r] for r in range(ROWS)]
        for pack in block:
            for g in range(groups):
                at = pack * groups + g
                for r in range(0, ROWS, 2):
                    lines = [sums_ref[layer, near[r + k], at] for k in range(4)]
                    middle = (lines[1] + lines[2]) + offset
                    for k, summed in enumerate((lines[0] + middle, middle + lines[3])):
                        right_inverse = spread(inverses[r + k][pack : pack + 1, :])
                        right_root = spread(roots[r + k][pack : pack + 1, :])
                        cosine = summed * u_map_refs[layer][r + k, 0, g] * right_inverse
                        gap = 1.0 - (jnp.abs(cosine) if layer == 0 else cosine)
                        gap = jnp.maximum(gap, tiny)
                        root = gap * lax.rsqrt(gap)
                        rest = 2.0 - gap
                        rest = rest * lax.rsqrt(rest)
                        sine = root * rest
                        theta = root * horner(ACOS, rest)
                        angle = PI - theta
                        if layer == 0:
                            angle = jnp.where(cosine >= 0.0, angle, theta)
                        angle_refs[layer][r + k, at] = angle
                        value = (cosine * angle + sine) * u_map_refs[layer][r + k, 1, g] * right_root
                        if layer + 1 < LAYERS:
                            sums_ref[layer + 1, near[r + k + 1], at] = across(value, masks)
                        else:
                            total_ref[at] += value

    for block in blocks:
        pl.when(step < steps)(lambda block=block: product_stage(block))
    for layer in range(LAYERS):
        for block in blocks:
            pl.when((step > layer) & (step <= steps + layer))(
                lambda layer=layer, block=block: arc_stage(layer, block)
            )

    @pl.when(step == steps + LAYERS - 1)
    def _():
        lane = lax.broadcasted_iota(jnp.int32, (LANES, LANES), 1)
        from_lane = lax.broadcasted_iota(jnp.int32, (LANES, LANES), 0)
        copies = LANES // side
        folding = jnp.where(lane % copies == from_lane // side, 1.0 / (side * side), 0.0)
        means = jnp.dot(total_ref[...].reshape(-1, LANES), folding, precision=highest)
        place = lax.broadcasted_iota(jnp.int32, (SUBLANES, LANES), 1) // copies
        for g in range(groups):
            mine = slice(g * SUBLANES, (g + 1) * SUBLANES)
            line = jnp.zeros((SUBLANES, LANES), jnp.float32) if first == 0 else past_ref[mine, :]
            for pack in range(packs):
                at = (pack * groups + g) * SUBLANES
                line = jnp.where(place == first + pack, means[at : at + SUBLANES], line)
            tile_ref[mine, :] = line


def pair_forward(rows, v_rows, first, tile):
    channels, side, groups = (rows if first == 0 else rows[0]).shape[:3]
    packs = v_rows.shape[2]
    steps = side // ROWS
    count = packs * groups
    f32 = jnp.float32

    def lag(layer, trailing):
        return lambda i: (jnp.clip(i - 1 - layer, 0, steps - 1),) + (0,) * trailing

    def now(trailing):
        return lambda i: (0, jnp.minimum(i, steps - 1)) + (0,) * trailing

    image = pl.BlockSpec((channels, ROWS, groups, SUBLANES, LANES), now(3))
    maps = [pl.BlockSpec((ROWS, 2, groups, SUBLANES, LANES), lag(layer, 4)) for layer in range(LAYERS)]
    column = pl.BlockSpec((channels, ROWS, packs, LANES), now(2))
    whole = pl.BlockSpec((groups * SUBLANES, LANES), lambda i: (0, 0))
    out_shape = (
        [jax.ShapeDtypeStruct((side, count, SUBLANES, LANES), f32)] * LAYERS
        + [jax.ShapeDtypeStruct((side, packs, LANES), f32)] * LAYERS
        + [jax.ShapeDtypeStruct((groups * SUBLANES, LANES), f32)]
    )
    out_specs = (
        [pl.BlockSpec((ROWS, count, SUBLANES, LANES), lag(layer, 3)) for layer in range(LAYERS)]
        + [pl.BlockSpec((ROWS, packs, LANES), lag(layer, 2)) for layer in range(LAYERS)]
        + [whole]
    )
    scratch_shapes = [
        pltpu.VMEM((LAYERS, RING, count, SUBLANES, LANES), f32),
        pltpu.VMEM((LAYERS, RING, packs, LANES), f32),
        pltpu.VMEM((count, SUBLANES, LANES), f32),
        pltpu.VMEM((LAYERS, ROWS, packs, LANES), f32),
    ]
    if first == 0:
        operands = [rows, v_rows]
        in_specs = [pl.BlockSpec((channels, ROWS, groups, SUBLANES, side), now(3)), column]
        out_shape = (
            [jax.ShapeDtypeStruct((channels, side, groups, SUBLANES, LANES), f32)]
            + [jax.ShapeDtypeStruct((side, 2, groups, SUBLANES, LANES), f32)] * LAYERS
            + out_shape
        )
        out_specs = [image] + maps + out_specs
        scratch_shapes = scratch_shapes + [pltpu.VMEM((LAYERS, RING, groups, SUBLANES, LANES), f32)]
    else:
        operands = [rows[0], v_rows, *rows[1:], tile]
        in_specs = [image, column] + maps + [whole]
    results = pl.pallas_call(
        lambda *refs: forward_kernel(side, channels, groups, packs, first, *refs),
        out_shape=out_shape,
        grid=(steps + LAYERS,),
        in_specs=in_specs,
        out_specs=out_specs,
        scratch_shapes=scratch_shapes,
        name="pair_forward",
    )(*operands)
    if first == 0:
        rows, results = results[: 1 + LAYERS], results[1 + LAYERS :]
    return rows, results[-1], results[:LAYERS], results[LAYERS : 2 * LAYERS]


def backward_kernel(side, channels, groups, packs, *refs):
    weight_ref, u_ref = refs[0], refs[1]
    u_map_refs = refs[2 : 2 + LAYERS]
    taken = 2 + LAYERS
    angle_refs, root_refs, image_refs = [], [], []
    for batch in range(len(packs)):
        angle_refs.append(refs[taken : taken + LAYERS])
        root_refs.append(refs[taken + LAYERS : taken + 2 * LAYERS])
        image_refs.append(refs[taken + 2 * LAYERS])
        taken += 2 * LAYERS + 1
    grad_ref, sums_ref, own_sums_ref, wide_ref, total_ref = refs[taken:]
    parts = [(batch, pack) for batch in range(len(packs)) for pack in range(packs[batch])]
    blocks = [
        list(enumerate(parts))[start : start + PART] for start in range(0, len(parts), PART)
    ]
    step = pl.program_id(0)
    steps = side // ROWS
    masks = edges(side, (SUBLANES, LANES))
    shrink = 1.0 / (9.0 * PI)
    pixels = side * side

    def slot(row):
        return row & (RING - 1)

    def fold(total):
        total = total + pltpu.roll(total, 2 * side, 1)
        return total + pltpu.roll(total, side, 1)

    def spread(line):
        return jnp.broadcast_to(line, (SUBLANES, LANES))

    def summed(ref, depth, row, at):
        lines = [ref[depth, slot(row + k), at] for k in range(-1, ROWS + 1)]
        totals = []
        for r in range(0, ROWS, 2):
            middle = lines[r + 1] + lines[r + 2]
            totals += [lines[r] + middle, middle + lines[r + 3]]
        return totals

    def add(total, part):
        return part if total is None else total + part

    @pl.when(step == 0)
    def _():
        lane = lax.broadcasted_iota(jnp.int32, (SUBLANES, LANES), 1)
        for pack in range(len(parts)):
            index = lane // side + pack * (LANES // side)
            for g in range(groups):
                line = weight_ref[g * SUBLANES : (g + 1) * SUBLANES, :]
                wide_ref[pack * groups + g] = jnp.take_along_axis(line, index, axis=1)
        for depth in range(LAYERS):
            sums_ref[depth, RING - 1] = jnp.zeros(sums_ref.shape[2:], jnp.float32)
            own_sums_ref[depth, RING - 1] = jnp.zeros(own_sums_ref.shape[2:], jnp.float32)

    for depth in range(LAYERS):

        @pl.when(step == steps + depth)
        def _(depth=depth):
            sums_ref[depth, slot(side)] = jnp.zeros(sums_ref.shape[2:], jnp.float32)
            own_sums_ref[depth, slot(side)] = jnp.zeros(own_sums_ref.shape[2:], jnp.float32)

    def layer_block(depth, block):
        layer = LAYERS - 1 - depth
        row = (step - depth) * ROWS
        totals = [[None] * groups for _ in range(ROWS)]
        for part, (batch, pack) in blocks[block]:
            for g in range(groups):
                inner = pack * groups + g
                at = part * groups + g
                if depth == 0:
                    grads = [wide_ref[at]] * ROWS
                else:
                    grads = summed(sums_ref, depth - 1, row, at)
                for r, grad in enumerate(grads):
                    angle = angle_refs[batch][layer][r, inner]
                    sums_ref[depth, slot(row + r), at] = across(grad * angle, masks)
                    product = angle * (PI - angle)
                    root = spread(root_refs[batch][layer][r, pack : pack + 1, :])
                    totals[r][g] = add(totals[r][g], grad * root * (product * horner(SINE, product)))
        for r in range(ROWS):
            for g in range(groups):
                total = totals[r][g]
                total_ref[depth, r, g] = total if block == 0 else total_ref[depth, r, g] + total

    def layer_end(depth):
        layer = LAYERS - 1 - depth
        row = (step - depth) * ROWS
        factor = shrink**depth / (pixels * 2.0 * PI * PI)
        for g in range(groups):
            above = summed(own_sums_ref, depth - 1, row, g) if depth > 0 else None
            for r in range(ROWS):
                carry = fold(total_ref[depth, r, g]) * (factor / u_map_refs[layer][r, 1, g])
                if depth > 0:
                    carry = carry + above[r] * (1.0 / 9.0)
                own_sums_ref[depth, slot(row + r), g] = across(carry, masks)

    def image_block(block):
        row = (step - LAYERS) * ROWS
        totals = [[[None] * groups for _ in range(channels)] for _ in range(ROWS)]
        for part, (batch, pack) in blocks[block]:
            for g in range(groups):
                at = part * groups + g
                for r, grad in enumerate(summed(sums_ref, LAYERS - 1, row, at)):
                    for c in range(channels):
                        line = spread(image_refs[batch][c, r, pack : pack + 1, :])
                        totals[r][c][g] = add(totals[r][c][g], grad * line)
        for r in range(ROWS):
            for c in range(channels):
                for g in range(groups):
                    total, at = totals[r][c][g], LAYERS + c
                    total_ref[at, r, g] = total if block == 0 else total_ref[at, r, g] + total

    def image_end():
        row = (step - LAYERS) * ROWS
        copies = LANES // side
        lane = lax.broadcasted_iota(jnp.int32, (SUBLANES, LANES), 1)
        for g in range(groups):
            above = summed(own_sums_ref, LAYERS - 1, row, g)
            for r in range(ROWS):
                carry = above[r] * (2.0 / (9.0 * channels))
                for c in range(channels):
                    image = fold(total_ref[LAYERS + c, r, g]) * (shrink**LAYERS / (pixels * channels))
                    image = image + carry * u_ref[c, r, g]
                    lines = grad_ref[g, 0, c]
                    grad_ref[g, 0, c] = jnp.where(lane // side == (row + r) % copies, image, lines)

    for depth in range(LAYERS):
        for block in range(len(blocks)):
            pl.when((step >= depth) & (step < steps + depth))(
                lambda depth=depth, block=block: layer_block(depth, block)
            )
        pl.when((step >= depth) & (step < steps + depth))(lambda depth=depth: layer_end(depth))
    for block in range(len(blocks)):
        pl.when(step >= LAYERS)(lambda block=block: image_block(block))
    pl.when(step >= LAYERS)(image_end)


def pair_backward(weights, rows, batches):
    channels, side, groups = rows[0].shape[:3]
    packs = [images.shape[2] for _, _, images in batches]
    steps = side // ROWS
    copies = LANES // side
    f32 = jnp.float32

    def at_lag(lag, trailing):
        return lambda i: (jnp.clip(i - lag, 0, steps - 1),) + (0,) * trailing

    def image_rows(trailing):
        return lambda i: (0, jnp.clip(i - LAYERS, 0, steps - 1)) + (0,) * trailing

    operands = [weights, *rows]
    in_specs = [
        pl.BlockSpec(weights.shape, lambda i: (0, 0)),
        pl.BlockSpec((channels, ROWS, groups, SUBLANES, LANES), image_rows(3)),
    ] + [
        pl.BlockSpec((ROWS, 2, groups, SUBLANES, LANES), at_lag(LAYERS - 1 - layer, 4))
        for layer in range(LAYERS)
    ]
    for (angles, roots, images), width in zip(batches, packs):
        for layer in range(LAYERS):
            operands.append(angles[layer])
            in_specs.append(
                pl.BlockSpec((ROWS, width * groups, SUBLANES, LANES), at_lag(LAYERS - 1 - layer, 3))
            )
        for layer in range(LAYERS):
            operands.append(roots[layer])
            in_specs.append(pl.BlockSpec((ROWS, width, LANES), at_lag(LAYERS - 1 - layer, 2)))
        operands.append(images)
        in_specs.append(pl.BlockSpec((channels, ROWS, width, LANES), image_rows(2)))
    count = sum(packs) * groups
    return pl.pallas_call(
        lambda *refs: backward_kernel(side, channels, groups, packs, *refs),
        out_shape=jax.ShapeDtypeStruct((groups, side // copies, channels, SUBLANES, LANES), f32),
        grid=(steps + LAYERS,),
        in_specs=in_specs,
        out_specs=pl.BlockSpec(
            (groups, 1, channels, SUBLANES, LANES),
            lambda i: (0, jnp.clip(i - LAYERS, 0, steps - 1) * ROWS // copies, 0, 0, 0),
        ),
        scratch_shapes=[
            pltpu.VMEM((LAYERS, RING, count, SUBLANES, LANES), f32),
            pltpu.VMEM((LAYERS, RING, groups, SUBLANES, LANES), f32),
            pltpu.VMEM((count, SUBLANES, LANES), f32),
            pltpu.VMEM((LAYERS + channels, ROWS, groups, SUBLANES, LANES), f32),
        ],
        name="pair_backward",
    )(*operands)


def eliminate(panel):
    height, width = panel.shape
    tiles = [panel[:, start : start + LANES] for start in range(0, width, LANES)]
    lane = lax.broadcasted_iota(jnp.int32, tiles[0].shape, 1)
    row = lax.broadcasted_iota(jnp.int32, tiles[0].shape, 0)
    for j in range(0, height, 2):
        k = j + 1
        first = jnp.broadcast_to(tiles[0][:, j : j + 1], tiles[0].shape)
        second = jnp.broadcast_to(tiles[0][:, k : k + 1], tiles[0].shape)
        a, b, d = first[j : j + 1], first[k : k + 1], second[k : k + 1]
        scale = 1.0 / (a * d - b * b)
        a, b, d = a * scale, b * scale, d * scale
        for t, tile in enumerate(tiles):
            upper, lower = tile[j : j + 1], tile[k : k + 1]
            if t == 0:
                upper = jnp.where(lane[:1] == j, 1.0, jnp.where(lane[:1] == k, 0.0, upper))
                lower = jnp.where(lane[:1] == k, 1.0, jnp.where(lane[:1] == j, 0.0, lower))
                tile = jnp.where((lane == j) | (lane == k), 0.0, tile)
            upper, lower = d * upper - b * lower, a * lower - b * upper
            rest = tile - first * upper - second * lower
            tiles[t] = jnp.where(row == j, upper, jnp.where(row == k, lower, rest))
    return jnp.concatenate(tiles, axis=1)


def lane_of(kind, d, k, col_count, own, near):
    far = 2 * near * own + (kind * (col_count - near) + d - near) * own + k
    return jnp.where(d < near, (2 * d + kind) * own + k, far)


def sorting(kind, col_count, own, near):
    i = lax.broadcasted_iota(jnp.int32, (LANES, LANES), 0)
    j = lax.broadcasted_iota(jnp.int32, (LANES, LANES), 1) % (LANES // 2)
    return (i == lane_of(kind, j // own, j % own, col_count, own, near)).astype(jnp.float32)


def exact_dot(a, b, da=1, db=0):
    return lax.dot_general(
        a, b, (((da,), (db,)), ((), ())), precision=highest, preferred_element_type=jnp.float32
    )


def whole_matrix(kind, row_count, col_count, own, near, gathered_ref, big_ref):
    count = row_count * col_count * own
    rows = row_count * own
    half = LANES // 2
    for r in range(row_count):
        for c in range(col_count):
            tile = gathered_ref[r * col_count + c, :rows, :]
            for r2 in range(row_count):
                at = (c * row_count + r2) * own
                big_ref[r, at : at + own, :] = tile[r2 * own : (r2 + 1) * own]
    parts = exact_dot(
        big_ref[...].reshape(row_count * count, LANES), sorting(kind, col_count, own, near)
    ).reshape(row_count, count, LANES)
    lane = lax.broadcasted_iota(jnp.int32, (rows, LANES), 1)
    for c in range(col_count):
        for t in range(row_count // 2):
            even, odd = (
                pltpu.roll(part, own * c, 1) if c else part
                for part in (parts[2 * t, c * rows : (c + 1) * rows], parts[2 * t + 1, c * rows : (c + 1) * rows])
            )
            joined = jnp.where(lane < half, even, odd)
            for r2 in range(row_count):
                at = (r2 * col_count + c) * own
                big_ref[t, at : at + own, :] = joined[r2 * own : (r2 + 1) * own]
    return jnp.concatenate([big_ref[t] for t in range(row_count // 2)], axis=1)


def solve_from(inverse_ref, system_ref, right):
    first = exact_dot(inverse_ref[...], right)
    return first + exact_dot(inverse_ref[...], right - exact_dot(system_ref[...], first))


def invert_kernel(row_count, col_count, own, near, gathered_ref, *refs):
    system_ref, inverse_ref, alpha_ref, big_ref, label_ref = refs
    count = row_count * col_count * own
    rows = row_count * own
    support = whole_matrix(0, row_count, col_count, own, near, gathered_ref, big_ref)
    for source in range(row_count * col_count):
        label_ref[source * own : (source + 1) * own, :] = gathered_ref[source, rows : rows + own, :]
    wide_lane = lax.broadcasted_iota(jnp.int32, (count, count), 1)
    wide_row = lax.broadcasted_iota(jnp.int32, (count, count), 0)
    ridge = jnp.sum(jnp.where(wide_lane == wide_row, support, 0.0)) * (ridge_scale / count)
    system = support + jnp.where(wide_lane == wide_row, ridge, 0.0)
    system_ref[...] = system
    inverse_ref[...] = system
    rest_lane = lax.broadcasted_iota(jnp.int32, (count - BLOCK, count), 1)

    def one_block(step, carry):
        reduced = eliminate(inverse_ref[:BLOCK, :])
        below = inverse_ref[BLOCK:, :]
        below = jnp.where(rest_lane < BLOCK, 0.0, below) - exact_dot(below[:, :BLOCK], reduced)
        inverse_ref[: count - BLOCK, :] = pltpu.roll(below, count - BLOCK, 1)
        inverse_ref[count - BLOCK :, :] = pltpu.roll(reduced, count - BLOCK, 1)
        return carry

    lax.fori_loop(0, count // BLOCK, one_block, 0)
    alpha_ref[...] = solve_from(inverse_ref, system_ref, label_ref[...])


def weights_kernel(row_count, col_count, own, near, place_ref, gathered_ref, onehot_ref, *refs):
    system_ref, inverse_ref, alpha_ref, weight_ref, gamma_ref, loss_ref, big_ref, row_ref = refs
    row_index, col_index = place_ref[0], place_ref[1]
    count = row_count * col_count * own
    block = col_count * own
    cross = whole_matrix(1, row_count, col_count, own, near, gathered_ref, big_ref)
    alpha = alpha_ref[...]
    error = exact_dot(cross, alpha, 0, 0) - onehot_ref[...]
    loss_ref[...] = jnp.broadcast_to(0.5 * jnp.sum(error * error), loss_ref.shape)
    gamma = solve_from(inverse_ref, system_ref, exact_dot(cross, error))
    intersection = jnp.sum(gamma * alpha)
    row_ref[0] = alpha
    row_ref[1] = gamma
    row_ref[2] = error
    mine = pl.multiple_of((row_index * col_count + col_index) * own, own)
    gamma_ref[...] = row_ref[1, pl.ds(mine, own), :]

    def rows_here(which):
        starts = [pl.multiple_of((r2 * col_count + col_index) * own, own) for r2 in range(row_count)]
        return jnp.concatenate([row_ref[which, pl.ds(start, own), :] for start in starts], axis=0)

    def columns_here(which):
        here = row_ref[which, pl.ds(pl.multiple_of(row_index * block, block), block), :]
        return jnp.concatenate([here, here], axis=0)

    alpha_rows, gamma_rows = rows_here(0), rows_here(1)
    pair = -exact_dot(gamma_rows, columns_here(0), 1, 1) - exact_dot(alpha_rows, columns_here(1), 1, 1)
    target = exact_dot(alpha_rows, columns_here(2), 1, 1)
    u = lax.broadcasted_iota(jnp.int32, pair.shape, 0)
    v = lax.broadcasted_iota(jnp.int32, pair.shape, 1)
    same = (u // own == row_index) & (v % block == col_index * own + u % own)
    pair = pair - jnp.where(same, intersection * (2.0 * ridge_scale / count), 0.0)
    total = None
    for kind, part in enumerate((pair, target)):
        turned = pltpu.roll(part, (LANES - own * col_index) % LANES, 1)
        turned = jnp.where(v < block, turned, 0.0)
        back = exact_dot(turned, sorting(kind, col_count, own, near), 1, 1)
        total = back if total is None else total + back
    weight_ref[...] = total


def invert_in_kernel(gathered, row_count, col_count, own, near):
    f32 = jnp.float32
    count = row_count * col_count * own
    vmem = pl.BlockSpec(memory_space=pltpu.VMEM)
    square = jax.ShapeDtypeStruct((count, count), f32)
    return pl.pallas_call(
        lambda *refs: invert_kernel(row_count, col_count, own, near, *refs),
        out_shape=[square, square, jax.ShapeDtypeStruct((count, LANES), f32)],
        in_specs=[vmem],
        out_specs=[vmem] * 3,
        scratch_shapes=[
            pltpu.VMEM((row_count, count, LANES), f32),
            pltpu.VMEM((count, LANES), f32),
        ],
        name="invert",
    )(gathered)


def weights_in_kernel(gathered, onehot, solved, row_index, col_index, row_count, col_count, own, near):
    f32 = jnp.float32
    count = row_count * col_count * own
    vmem = pl.BlockSpec(memory_space=pltpu.VMEM)
    return pl.pallas_call(
        lambda *refs: weights_kernel(row_count, col_count, own, near, *refs),
        out_shape=[
            jax.ShapeDtypeStruct((row_count * own, LANES), f32),
            jax.ShapeDtypeStruct((own, LANES), f32),
            jax.ShapeDtypeStruct((SUBLANES, LANES), f32),
        ],
        in_specs=[pl.BlockSpec(memory_space=pltpu.SMEM)] + [vmem] * 5,
        out_specs=[vmem] * 3,
        scratch_shapes=[
            pltpu.VMEM((row_count, count, LANES), f32),
            pltpu.VMEM((3, count, LANES), f32),
        ],
        name="weights",
    )(jnp.stack([row_index, col_index]).astype(jnp.int32), gathered, onehot, *solved)


def solve_with(factor, rhs):
    halfway = lax.linalg.triangular_solve(factor, rhs, left_side=True, lower=True)
    return lax.linalg.triangular_solve(factor, halfway, left_side=True, lower=True, transpose_a=True)


def solve_plainly(gathered, onehot, row_index, col_index, row_count, col_count, own, near):
    count = row_count * col_count * own
    rows = row_count * own
    block = 2 * col_count * own
    labels = gathered[:, rows : rows + own].reshape(count, LANES)
    kernels, sorts = [], []
    for kind in range(2):
        j = jnp.arange(block // 2, dtype=jnp.int32)[None, :]
        lanes = lane_of(kind, j // own, j % own, col_count, own, near)
        sort = (jnp.arange(LANES, dtype=jnp.int32)[:, None] == lanes).astype(jnp.float32)
        sorts.append(sort)
        picked = jnp.dot(gathered[:, :rows].reshape(-1, LANES), sort, precision=highest)
        picked = picked.reshape(row_count, col_count, row_count, own, block // 2)
        picked = jnp.stack(
            [jnp.roll(picked[:, c], c * own, axis=-1) for c in range(col_count)], axis=1
        )
        kernels.append(jnp.transpose(picked, (2, 1, 3, 0, 4)).reshape(count, count))
    identity = jnp.eye(count, dtype=jnp.float32)
    ridge = jnp.trace(kernels[0]) * (ridge_scale / count)
    factor = jnp.linalg.cholesky(kernels[0] + ridge * identity)
    alpha = solve_with(factor, labels)
    error = jnp.dot(kernels[1].T, alpha, precision=highest) - onehot
    gamma = solve_with(factor, jnp.dot(kernels[1], error, precision=highest))
    intersection = jnp.sum(gamma * alpha)
    values = jnp.stack([alpha, gamma, error]).reshape(3, row_count, col_count, own, LANES)
    here = lax.dynamic_index_in_dim(values, col_index, 2, keepdims=False).reshape(3, rows, LANES)
    there = lax.dynamic_index_in_dim(values, row_index, 1, keepdims=False)
    there = lax.dynamic_slice_in_dim(
        jnp.concatenate([there, there], axis=1), col_index, col_count, 1
    ).reshape(3, -1, LANES)

    def outer(a, b):
        return jnp.dot(a, b.T, precision=highest)

    pair = -outer(here[1], there[0]) - outer(here[0], there[1])
    u, v = jnp.arange(rows)[:, None], jnp.arange(block // 2)[None, :]
    same = (u // own == row_index) & (v == u % own)
    pair = pair - jnp.where(same, intersection * (2.0 * ridge_scale / count), 0.0)
    weights = outer(pair, sorts[0]) + outer(outer(here[0], there[2]), sorts[1])
    mine = (row_index * col_count + col_index) * own
    return (
        weights,
        lax.dynamic_slice_in_dim(gamma, mine, own, 0),
        jnp.full((SUBLANES, LANES), 0.5 * jnp.sum(error * error)),
    )


def body(support_views, support_pick, target_views, target_pick, support_labels, target_labels):
    own, _, channels, pixels = support_views.shape
    side = math.isqrt(pixels)
    classes = support_labels.shape[1]
    row_count = lax.axis_size("row")
    col_count = lax.axis_size("col")
    row_index = lax.axis_index("row")
    col_index = lax.axis_index("col")
    own_support = choose_view(support_views, support_pick)
    own_target = choose_view(target_views, target_pick)

    both = jnp.stack([own_support, own_target]).reshape(2 * own, channels, side, side)
    chunk = jnp.transpose(both, (1, 2, 0, 3)).reshape(channels, side, 2 * own * side)
    chunks = [chunk]
    for d in range(1, col_count):
        pairs = [((i + d) % col_count, i) for i in range(col_count)]
        chunks.append(lax.ppermute(chunk, "col", pairs))
    near = 1 if own % (LANES // side) == 0 else LANES // side
    middle = own * side
    v_rows = [
        jnp.concatenate(chunks[:near], axis=-1) if near > 1 else chunk,
        jnp.concatenate([part[..., :middle] for part in chunks[near:]], axis=-1),
        jnp.concatenate([part[..., middle:] for part in chunks[near:]], axis=-1),
    ]
    v_rows = [part.reshape(channels, side, -1, LANES) for part in v_rows]

    row_images = lax.all_gather(own_support, "row", axis=0, tiled=True)
    groups = row_images.shape[0] // SUBLANES
    narrow = jnp.transpose(
        row_images.reshape(groups, SUBLANES, channels, side, side), (2, 3, 0, 1, 4)
    )
    devices = row_count * col_count
    labels = jnp.pad(support_labels, ((0, 0), (0, LANES - classes)))
    lanes = jnp.arange(LANES, dtype=jnp.int32)[None, :]
    onehot = jnp.where(
        lanes < classes, (target_labels[:, None] == lanes).astype(jnp.float32) - 1.0 / classes, 0.0
    )

    def to_all(parcel):
        copies = jnp.broadcast_to(parcel[None], (devices,) + parcel.shape)
        return lax.all_to_all(copies, AXES, 0, 0, tiled=True)

    rows, tile = narrow, None
    batches, tiles = [], []
    first = 0
    for columns in v_rows:
        rows, tile, angles, roots = pair_forward(rows, columns, first, tile)
        batches.append((angles, roots, columns))
        tiles.append(tile)
        first += columns.shape[2]
    sizes = (row_count, col_count, own, near)
    if own == SUBLANES and 2 * col_count * own == LANES and row_count % 2 == 0:
        support_tiles = to_all(jnp.concatenate([tiles[1], labels], axis=0))
        target_tiles = to_all(tiles[2])
        solved = invert_in_kernel(support_tiles, *sizes)
        weights, gamma_own, loss = weights_in_kernel(
            target_tiles, onehot, solved, row_index, col_index, *sizes
        )
    else:
        gathered = to_all(jnp.concatenate([tiles[2], labels], axis=0))
        weights, gamma_own, loss = solve_plainly(gathered, onehot, row_index, col_index, *sizes)
    grads = pair_backward(weights, rows, batches)
    if own == SUBLANES:
        support_grad = lax.dynamic_index_in_dim(grads, row_index, 0, keepdims=False)
        for k in range(1, row_count):
            pairs = [(i, (i + k) % row_count) for i in range(row_count)]
            there = lax.dynamic_index_in_dim(grads, (row_index + k) % row_count, 0, keepdims=False)
            support_grad = support_grad + lax.ppermute(there, "row", pairs)
        support_grad = jnp.transpose(support_grad, (2, 1, 0, 3))
    else:
        grads = jnp.transpose(grads, (0, 3, 2, 1, 4)).reshape(row_count * own, channels, pixels)
        support_grad = lax.psum_scatter(grads, "row", scatter_dimension=0, tiled=True)
    support_grad = support_grad.reshape(own, channels, pixels)
    return (support_grad, gamma_own[:, :classes], loss[0, 0])


def solution(mesh):
    return jax.shard_map(
        body,
        mesh=mesh,
        in_specs=(
            P(AXES, None, None, None),
            P(AXES),
            P(AXES, None, None, None),
            P(AXES),
            P(AXES, None),
            P(),
        ),
        out_specs=(P(AXES, None, None), P(AXES, None), P()),
        check_vma=False,
    )
```

```python
import math

import jax
import jax.numpy as jnp
from jax import lax
from jax.experimental import pallas as pl
from jax.experimental.pallas import tpu as pltpu
from jax.sharding import PartitionSpec as P

LAYERS = 3
LANES = 128
SUBLANES = 8
PART = 8
FORWARD_PART = 7
BLOCK = 64
ROWS = 2
RING = 8

bias_variance = 0.1
ridge_scale = 0.1
highest = lax.Precision.HIGHEST
tiny = 1e-30
PI = math.pi

ACOS = (
    2.20239957601501,
    -0.9079020788090617,
    0.36298714579028,
    -0.09949097018131615,
    0.012802548128944304,
)
SINE = (
    0.31830981148327425,
    0.032252498831491,
    0.001158328114192081,
    2.2834735017183973e-05,
)
AXES = ("row", "col")


def horner(coefficients, x):
    total = coefficients[-1] * x + coefficients[-2]
    for coefficient in coefficients[-3::-1]:
        total = total * x + coefficient
    return total


def choose_view(views, picked):
    options = jnp.arange(views.shape[1], dtype=jnp.int32)
    selector = (picked[:, None] == options[None, :]).astype(jnp.float32)
    return jnp.sum(selector[:, :, None, None] * views, axis=1)


def edges(side, shape):
    x = lax.broadcasted_iota(jnp.int32, shape, len(shape) - 1) % side
    return x > 0, x < side - 1


def across(surface, masks):
    axis = surface.ndim - 1
    left = jnp.where(masks[0], pltpu.roll(surface, 1, axis), 0.0)
    right = jnp.where(masks[1], pltpu.roll(surface, LANES - 1, axis), 0.0)
    return surface + left + right


def map_scale(channels, layer):
    return 9.0 * channels if layer == 0 else 9.0


class PerLayer:
    def __init__(self, refs):
        self.refs = refs
        self.shape = (len(refs),) + refs[0].shape

    def __getitem__(self, at):
        return self.refs[at[0]][at[1:]]

    def __setitem__(self, at, value):
        self.refs[at[0]][at[1:]] = value


def forward_kernel(side, channels, groups, packs, first, *refs):
    if first == 0:
        narrow_ref, v_ref = refs[:2]
        u_ref, *u_map_refs = refs[2 : 3 + LAYERS]
        u_sums_ref = refs[-1]
        outs = refs[3 + LAYERS : -1]
    else:
        u_ref, v_ref = refs[:2]
        u_map_refs = refs[2 : 2 + LAYERS]
        past_ref = refs[2 + LAYERS]
        outs = refs[3 + LAYERS :]
    angle_refs = outs[:LAYERS]
    root_refs = outs[LAYERS : 2 * LAYERS]
    tile_ref = outs[2 * LAYERS]
    own_sums_ref, total_ref, inverse_ref = outs[2 * LAYERS + 1 : 2 * LAYERS + 4]
    sums_ref = PerLayer(outs[2 * LAYERS + 4 : 3 * LAYERS + 4])
    step = pl.program_id(0)
    steps = side // ROWS
    masks = edges(side, (SUBLANES, LANES))
    own_masks = edges(side, (packs, LANES))
    width = packs if packs <= PART else FORWARD_PART
    blocks = [range(start, min(start + width, packs)) for start in range(0, packs, width)]

    def slot(row):
        return row & (RING - 1)

    def spread(line):
        return jnp.broadcast_to(line, (SUBLANES, LANES))

    if first == 0:

        @pl.when(step == 0)
        def _():
            for layer in range(LAYERS):
                u_sums_ref[layer, RING - 1] = jnp.zeros(u_sums_ref.shape[2:], jnp.float32)

        for layer in range(LAYERS):

            @pl.when(step == steps + layer)
            def _(layer=layer):
                u_sums_ref[layer, slot(side)] = jnp.zeros(u_sums_ref.shape[2:], jnp.float32)

        @pl.when(step < steps)
        def _():
            for r in range(ROWS):
                for g in range(groups):
                    energy = None
                    for c in range(channels):
                        plane = jnp.concatenate([narrow_ref[c, r, g]] * (LANES // side), axis=-1)
                        u_ref[c, r, g] = plane
                        energy = plane * plane if energy is None else energy + plane * plane
                    u_sums_ref[0, slot(step * ROWS + r), g] = across(energy, masks)

    def row_maps(layer):
        scale = map_scale(channels, layer)
        for r in range(ROWS):
            row = (step - 1 - layer) * ROWS + r
            for g in range(groups):
                total = (
                    u_sums_ref[layer, slot(row - 1), g]
                    + u_sums_ref[layer, slot(row), g]
                    + u_sums_ref[layer, slot(row + 1), g]
                )
                current = total * (1.0 / scale) + bias_variance
                inverse = lax.rsqrt(current)
                u_map_refs[layer][r, 0, g] = inverse * (1.0 / scale)
                u_map_refs[layer][r, 1, g] = current * inverse * (1.0 / PI)
                if layer + 1 < LAYERS:
                    u_sums_ref[layer + 1, slot(row), g] = across(current, masks)

    @pl.when(step == 0)
    def _():
        total_ref[...] = jnp.zeros(total_ref.shape, jnp.float32)
        for layer in range(LAYERS):
            sums_ref[layer, RING - 1] = jnp.zeros(sums_ref.shape[2:], jnp.float32)
            own_sums_ref[layer, RING - 1] = jnp.zeros(own_sums_ref.shape[2:], jnp.float32)

    for layer in range(LAYERS):

        @pl.when(step == steps + layer)
        def _(layer=layer):
            sums_ref[layer, slot(side)] = jnp.zeros(sums_ref.shape[2:], jnp.float32)
            own_sums_ref[layer, slot(side)] = jnp.zeros(own_sums_ref.shape[2:], jnp.float32)

    def product_stage(block):
        for r in range(ROWS):
            where = slot(step * ROWS + r)
            if block is blocks[0]:
                energy = None
                for c in range(channels):
                    plane = v_ref[c, r]
                    energy = plane * plane if energy is None else energy + plane * plane
                own_sums_ref[0, where] = across(energy, own_masks)
            for pack in block:
                lines = [spread(v_ref[c, r, pack : pack + 1, :]) for c in range(channels)]
                for g in range(groups):
                    product = None
                    for c in range(channels):
                        part = u_ref[c, r, g] * lines[c]
                        product = part if product is None else product + part
                    sums_ref[0, where, pack * groups + g] = across(product, masks)

    def arc_stage(layer, block):
        if first == 0:
            row_maps(layer)
        scale = map_scale(channels, layer)
        offset = scale * bias_variance
        rows = [(step - 1 - layer) * ROWS + r for r in range(ROWS)]
        near = [slot(rows[0] + r) for r in range(-1, ROWS + 1)]
        inverses, roots = [], []
        for r in range(ROWS if block is blocks[0] else 0):
            own_total = own_sums_ref[layer, near[r]] + own_sums_ref[layer, near[r + 1]] + own_sums_ref[layer, near[r + 2]]
            own_map = own_total * (1.0 / scale) + bias_variance
            inverse = lax.rsqrt(own_map)
            inverses.append(inverse)
            roots.append(own_map * inverse)
            root_refs[layer][r] = roots[r]
            inverse_ref[layer, r] = inverse
            if layer + 1 < LAYERS:
                own_sums_ref[layer + 1, near[r + 1]] = across(own_map, own_masks)
        if block is not blocks[0]:
            inverses = [inverse_ref.at[layer, r] for r in range(ROWS)]
            roots = [root_refs[layer].at[r] for r in range(ROWS)]
        for pack in block:
            for g in range(groups):
                at = pack * groups + g
                for r in range(0, ROWS, 2):
                    lines = [sums_ref[layer, near[r + k], at] for k in range(4)]
                    middle = (lines[1] + lines[2]) + offset
                    for k, summed in enumerate((lines[0] + middle, middle + lines[3])):
                        right_inverse = spread(inverses[r + k][pack : pack + 1, :])
                        right_root = spread(roots[r + k][pack : pack + 1, :])
                        cosine = summed * u_map_refs[layer][r + k, 0, g] * right_inverse
                        gap = 1.0 - (jnp.abs(cosine) if layer == 0 else cosine)
                        gap = jnp.maximum(gap, tiny)
                        root = gap * lax.rsqrt(gap)
                        rest = 2.0 - gap
                        rest = rest * lax.rsqrt(rest)
                        sine = root * rest
                        theta = root * horner(ACOS, rest)
                        angle = PI - theta
                        if layer == 0:
                            angle = jnp.where(cosine >= 0.0, angle, theta)
                        angle_refs[layer][r + k, at] = angle
                        value = (cosine * angle + sine) * u_map_refs[layer][r + k, 1, g] * right_root
                        if layer + 1 < LAYERS:
                            sums_ref[layer + 1, near[r + k + 1], at] = across(value, masks)
                        else:
                            total_ref[at] += value

    for block in blocks:
        pl.when(step < steps)(lambda block=block: product_stage(block))
    for layer in range(LAYERS):
        for block in blocks:
            pl.when((step > layer) & (step <= steps + layer))(
                lambda layer=layer, block=block: arc_stage(layer, block)
            )

    @pl.when(step == steps + LAYERS - 1)
    def _():
        lane = lax.broadcasted_iota(jnp.int32, (LANES, LANES), 1)
        from_lane = lax.broadcasted_iota(jnp.int32, (LANES, LANES), 0)
        copies = LANES // side
        folding = jnp.where(lane % copies == from_lane // side, 1.0 / (side * side), 0.0)
        means = jnp.dot(total_ref[...].reshape(-1, LANES), folding, precision=highest)
        place = lax.broadcasted_iota(jnp.int32, (SUBLANES, LANES), 1) // copies
        for g in range(groups):
            mine = slice(g * SUBLANES, (g + 1) * SUBLANES)
            line = jnp.zeros((SUBLANES, LANES), jnp.float32) if first == 0 else past_ref[mine, :]
            for pack in range(packs):
                at = (pack * groups + g) * SUBLANES
                line = jnp.where(place == first + pack, means[at : at + SUBLANES], line)
            tile_ref[mine, :] = line


def pair_forward(rows, v_rows, first, tile):
    channels, side, groups = (rows if first == 0 else rows[0]).shape[:3]
    packs = v_rows.shape[2]
    steps = side // ROWS
    count = packs * groups
    f32 = jnp.float32

    def lag(layer, trailing):
        return lambda i: (jnp.clip(i - 1 - layer, 0, steps - 1),) + (0,) * trailing

    def now(trailing):
        return lambda i: (0, jnp.minimum(i, steps - 1)) + (0,) * trailing

    image = pl.BlockSpec((channels, ROWS, groups, SUBLANES, LANES), now(3))
    maps = [pl.BlockSpec((ROWS, 2, groups, SUBLANES, LANES), lag(layer, 4)) for layer in range(LAYERS)]
    column = pl.BlockSpec((channels, ROWS, packs, LANES), now(2))
    whole = pl.BlockSpec((groups * SUBLANES, LANES), lambda i: (0, 0))
    out_shape = (
        [jax.ShapeDtypeStruct((side, count, SUBLANES, LANES), f32)] * LAYERS
        + [jax.ShapeDtypeStruct((side, packs, LANES), f32)] * LAYERS
        + [jax.ShapeDtypeStruct((groups * SUBLANES, LANES), f32)]
    )
    out_specs = (
        [pl.BlockSpec((ROWS, count, SUBLANES, LANES), lag(layer, 3)) for layer in range(LAYERS)]
        + [pl.BlockSpec((ROWS, packs, LANES), lag(layer, 2)) for layer in range(LAYERS)]
        + [whole]
    )
    scratch_shapes = [
        pltpu.VMEM((LAYERS, RING, packs, LANES), f32),
        pltpu.VMEM((count, SUBLANES, LANES), f32),
        pltpu.VMEM((LAYERS, ROWS, packs, LANES), f32),
    ] + [pltpu.VMEM((RING, count, SUBLANES, LANES), f32)] * LAYERS
    if first == 0:
        operands = [rows, v_rows]
        in_specs = [pl.BlockSpec((channels, ROWS, groups, SUBLANES, side), now(3)), column]
        out_shape = (
            [jax.ShapeDtypeStruct((channels, side, groups, SUBLANES, LANES), f32)]
            + [jax.ShapeDtypeStruct((side, 2, groups, SUBLANES, LANES), f32)] * LAYERS
            + out_shape
        )
        out_specs = [image] + maps + out_specs
        scratch_shapes = scratch_shapes + [pltpu.VMEM((LAYERS, RING, groups, SUBLANES, LANES), f32)]
    else:
        operands = [rows[0], v_rows, *rows[1:], tile]
        in_specs = [image, column] + maps + [whole]
    results = pl.pallas_call(
        lambda *refs: forward_kernel(side, channels, groups, packs, first, *refs),
        out_shape=out_shape,
        grid=(steps + LAYERS,),
        in_specs=in_specs,
        out_specs=out_specs,
        scratch_shapes=scratch_shapes,
        name="pair_forward",
    )(*operands)
    if first == 0:
        rows, results = results[: 1 + LAYERS], results[1 + LAYERS :]
    return rows, results[-1], results[:LAYERS], results[LAYERS : 2 * LAYERS]


def backward_kernel(side, channels, groups, packs, *refs):
    turn_ref, weight_ref, u_ref = refs[:3]
    u_map_refs = refs[3 : 3 + LAYERS]
    taken = 3 + LAYERS
    angle_refs, root_refs, image_refs = [], [], []
    for batch in range(len(packs)):
        angle_refs.append(refs[taken : taken + LAYERS])
        root_refs.append(refs[taken + LAYERS : taken + 2 * LAYERS])
        image_refs.append(refs[taken + 2 * LAYERS])
        taken += 2 * LAYERS + 1
    grad_refs = refs[taken : taken + groups]
    own_sums_ref, wide_ref, total_ref = refs[taken + groups : taken + groups + 3]
    sums_ref = PerLayer(refs[taken + groups + 3 :])
    parts = [(batch, pack) for batch in range(len(packs)) for pack in range(packs[batch])]
    blocks = [
        list(enumerate(parts))[start : start + PART] for start in range(0, len(parts), PART)
    ]
    step = pl.program_id(0)
    steps = side // ROWS
    masks = edges(side, (SUBLANES, LANES))
    shrink = 1.0 / (9.0 * PI)
    pixels = side * side

    def slot(row):
        return row & (RING - 1)

    def fold(total):
        total = total + pltpu.roll(total, 2 * side, 1)
        return total + pltpu.roll(total, side, 1)

    def spread(line):
        return jnp.broadcast_to(line, (SUBLANES, LANES))

    def summed(ref, depth, row, at):
        lines = [ref[depth, slot(row + k), at] for k in range(-1, ROWS + 1)]
        totals = []
        for r in range(0, ROWS, 2):
            middle = lines[r + 1] + lines[r + 2]
            totals += [lines[r] + middle, middle + lines[r + 3]]
        return totals

    def add(total, part):
        return part if total is None else total + part

    @pl.when(step == 0)
    def _():
        lane = lax.broadcasted_iota(jnp.int32, (SUBLANES, LANES), 1)
        for pack in range(len(parts)):
            index = lane // side + pack * (LANES // side)
            for g in range(groups):
                line = weight_ref[g * SUBLANES : (g + 1) * SUBLANES, :]
                wide_ref[pack * groups + g] = jnp.take_along_axis(line, index, axis=1)
        for depth in range(LAYERS):
            sums_ref[depth, RING - 1] = jnp.zeros(sums_ref.shape[2:], jnp.float32)
            own_sums_ref[depth, RING - 1] = jnp.zeros(own_sums_ref.shape[2:], jnp.float32)

    for depth in range(LAYERS):

        @pl.when(step == steps + depth)
        def _(depth=depth):
            sums_ref[depth, slot(side)] = jnp.zeros(sums_ref.shape[2:], jnp.float32)
            own_sums_ref[depth, slot(side)] = jnp.zeros(own_sums_ref.shape[2:], jnp.float32)

    def layer_block(depth, block):
        layer = LAYERS - 1 - depth
        row = (step - depth) * ROWS
        totals = [[None] * groups for _ in range(ROWS)]
        for part, (batch, pack) in blocks[block]:
            for g in range(groups):
                inner = pack * groups + g
                at = part * groups + g
                if depth == 0:
                    grads = [wide_ref[at]] * ROWS
                else:
                    grads = summed(sums_ref, depth - 1, row, at)
                for r, grad in enumerate(grads):
                    angle = angle_refs[batch][layer][r, inner]
                    sums_ref[depth, slot(row + r), at] = across(grad * angle, masks)
                    product = angle * (PI - angle)
                    root = spread(root_refs[batch][layer][r, pack : pack + 1, :])
                    totals[r][g] = add(totals[r][g], grad * root * (product * horner(SINE, product)))
        for r in range(ROWS):
            for g in range(groups):
                total = totals[r][g]
                total_ref[depth, r, g] = total if block == 0 else total_ref[depth, r, g] + total

    def layer_end(depth):
        layer = LAYERS - 1 - depth
        row = (step - depth) * ROWS
        factor = shrink**depth / (pixels * 2.0 * PI * PI)
        for g in range(groups):
            above = summed(own_sums_ref, depth - 1, row, g) if depth > 0 else None
            for r in range(ROWS):
                carry = fold(total_ref[depth, r, g]) * (factor / u_map_refs[layer][r, 1, g])
                if depth > 0:
                    carry = carry + above[r] * (1.0 / 9.0)
                own_sums_ref[depth, slot(row + r), g] = across(carry, masks)

    def image_block(block):
        row = (step - LAYERS) * ROWS
        totals = [[[None] * groups for _ in range(channels)] for _ in range(ROWS)]
        for part, (batch, pack) in blocks[block]:
            for g in range(groups):
                at = part * groups + g
                for r, grad in enumerate(summed(sums_ref, LAYERS - 1, row, at)):
                    for c in range(channels):
                        line = spread(image_refs[batch][c, r, pack : pack + 1, :])
                        totals[r][c][g] = add(totals[r][c][g], grad * line)
        for r in range(ROWS):
            for c in range(channels):
                for g in range(groups):
                    total, at = totals[r][c][g], LAYERS + c
                    total_ref[at, r, g] = total if block == 0 else total_ref[at, r, g] + total

    def image_end():
        row = (step - LAYERS) * ROWS
        copies = LANES // side
        lane = lax.broadcasted_iota(jnp.int32, (SUBLANES, LANES), 1)
        for k in range(groups):
            g = lax.rem(turn_ref[0] + k, groups)
            above = summed(own_sums_ref, LAYERS - 1, row, g)
            for r in range(ROWS):
                carry = above[r] * (2.0 / (9.0 * channels))
                for c in range(channels):
                    image = fold(total_ref[LAYERS + c, r, g]) * (shrink**LAYERS / (pixels * channels))
                    image = image + carry * u_ref[c, r, g]
                    lines = grad_refs[k][0, c]
                    grad_refs[k][0, c] = jnp.where(lane // side == (row + r) % copies, image, lines)

    for depth in range(LAYERS):
        for block in range(len(blocks)):
            pl.when((step >= depth) & (step < steps + depth))(
                lambda depth=depth, block=block: layer_block(depth, block)
            )
        pl.when((step >= depth) & (step < steps + depth))(lambda depth=depth: layer_end(depth))
    for block in range(len(blocks)):
        pl.when(step >= LAYERS)(lambda block=block: image_block(block))
    pl.when(step >= LAYERS)(image_end)


def pair_backward(turn, weights, rows, batches):
    channels, side, groups = rows[0].shape[:3]
    packs = [images.shape[2] for _, _, images in batches]
    steps = side // ROWS
    copies = LANES // side
    f32 = jnp.float32

    def at_lag(lag, trailing):
        return lambda i: (jnp.clip(i - lag, 0, steps - 1),) + (0,) * trailing

    def image_rows(trailing):
        return lambda i: (0, jnp.clip(i - LAYERS, 0, steps - 1)) + (0,) * trailing

    operands = [turn.astype(jnp.int32).reshape(1), weights, *rows]
    in_specs = [
        pl.BlockSpec(memory_space=pltpu.SMEM),
        pl.BlockSpec(weights.shape, lambda i: (0, 0)),
        pl.BlockSpec((channels, ROWS, groups, SUBLANES, LANES), image_rows(3)),
    ] + [
        pl.BlockSpec((ROWS, 2, groups, SUBLANES, LANES), at_lag(LAYERS - 1 - layer, 4))
        for layer in range(LAYERS)
    ]
    for (angles, roots, images), width in zip(batches, packs):
        for layer in range(LAYERS):
            operands.append(angles[layer])
            in_specs.append(
                pl.BlockSpec((ROWS, width * groups, SUBLANES, LANES), at_lag(LAYERS - 1 - layer, 3))
            )
        for layer in range(LAYERS):
            operands.append(roots[layer])
            in_specs.append(pl.BlockSpec((ROWS, width, LANES), at_lag(LAYERS - 1 - layer, 2)))
        operands.append(images)
        in_specs.append(pl.BlockSpec((channels, ROWS, width, LANES), image_rows(2)))
    count = sum(packs) * groups
    return pl.pallas_call(
        lambda *refs: backward_kernel(side, channels, groups, packs, *refs),
        out_shape=[jax.ShapeDtypeStruct((side // copies, channels, SUBLANES, LANES), f32)] * groups,
        grid=(steps + LAYERS,),
        in_specs=in_specs,
        out_specs=[
            pl.BlockSpec(
                (1, channels, SUBLANES, LANES),
                lambda i: (jnp.clip(i - LAYERS, 0, steps - 1) * ROWS // copies, 0, 0, 0),
            )
        ]
        * groups,
        scratch_shapes=[
            pltpu.VMEM((LAYERS, RING, groups, SUBLANES, LANES), f32),
            pltpu.VMEM((count, SUBLANES, LANES), f32),
            pltpu.VMEM((LAYERS + channels, ROWS, groups, SUBLANES, LANES), f32),
        ]
        + [pltpu.VMEM((RING, count, SUBLANES, LANES), f32)] * LAYERS,
        name="pair_backward",
    )(*operands)


def eliminate(panel):
    height, width = panel.shape
    tiles = [panel[:, start : start + LANES] for start in range(0, width, LANES)]
    lane = lax.broadcasted_iota(jnp.int32, tiles[0].shape, 1)
    row = lax.broadcasted_iota(jnp.int32, tiles[0].shape, 0)
    for j in range(0, height, 2):
        k = j + 1
        first = jnp.broadcast_to(tiles[0][:, j : j + 1], tiles[0].shape)
        second = jnp.broadcast_to(tiles[0][:, k : k + 1], tiles[0].shape)
        a, b, d = first[j : j + 1], first[k : k + 1], second[k : k + 1]
        scale = 1.0 / (a * d - b * b)
        a, b, d = a * scale, b * scale, d * scale
        for t, tile in enumerate(tiles):
            upper, lower = tile[j : j + 1], tile[k : k + 1]
            if t == 0:
                upper = jnp.where(lane[:1] == j, 1.0, jnp.where(lane[:1] == k, 0.0, upper))
                lower = jnp.where(lane[:1] == k, 1.0, jnp.where(lane[:1] == j, 0.0, lower))
                tile = jnp.where((lane == j) | (lane == k), 0.0, tile)
            upper, lower = d * upper - b * lower, a * lower - b * upper
            rest = tile - first * upper - second * lower
            tiles[t] = jnp.where(row == j, upper, jnp.where(row == k, lower, rest))
    return jnp.concatenate(tiles, axis=1)


def lane_of(kind, d, k, col_count, own, near):
    far = 2 * near * own + (kind * (col_count - near) + d - near) * own + k
    return jnp.where(d < near, (2 * d + kind) * own + k, far)


def sorting(kind, col_count, own, near):
    i = lax.broadcasted_iota(jnp.int32, (LANES, LANES), 0)
    j = lax.broadcasted_iota(jnp.int32, (LANES, LANES), 1) % (LANES // 2)
    return (i == lane_of(kind, j // own, j % own, col_count, own, near)).astype(jnp.float32)


def exact_dot(a, b, da=1, db=0):
    return lax.dot_general(
        a, b, (((da,), (db,)), ((), ())), precision=highest, preferred_element_type=jnp.float32
    )


def whole_matrix(kind, row_count, col_count, own, near, gathered_ref, big_ref):
    count = row_count * col_count * own
    rows = row_count * own
    half = LANES // 2
    for r in range(row_count):
        for c in range(col_count):
            tile = gathered_ref[r * col_count + c, :rows, :]
            for r2 in range(row_count):
                at = (c * row_count + r2) * own
                big_ref[r, at : at + own, :] = tile[r2 * own : (r2 + 1) * own]
    parts = exact_dot(
        big_ref[...].reshape(row_count * count, LANES), sorting(kind, col_count, own, near)
    ).reshape(row_count, count, LANES)
    lane = lax.broadcasted_iota(jnp.int32, (rows, LANES), 1)
    for c in range(col_count):
        for t in range(row_count // 2):
            even, odd = (
                pltpu.roll(part, own * c, 1) if c else part
                for part in (parts[2 * t, c * rows : (c + 1) * rows], parts[2 * t + 1, c * rows : (c + 1) * rows])
            )
            joined = jnp.where(lane < half, even, odd)
            for r2 in range(row_count):
                at = (r2 * col_count + c) * own
                big_ref[t, at : at + own, :] = joined[r2 * own : (r2 + 1) * own]
    return jnp.concatenate([big_ref[t] for t in range(row_count // 2)], axis=1)


def solve_from(inverse_ref, system_ref, right):
    first = exact_dot(inverse_ref[...], right)
    return first + exact_dot(inverse_ref[...], right - exact_dot(system_ref[...], first))


def invert_kernel(row_count, col_count, own, near, gathered_ref, *refs):
    system_ref, inverse_ref, alpha_ref, big_ref, label_ref = refs
    count = row_count * col_count * own
    rows = row_count * own
    support = whole_matrix(0, row_count, col_count, own, near, gathered_ref, big_ref)
    for source in range(row_count * col_count):
        label_ref[source * own : (source + 1) * own, :] = gathered_ref[source, rows : rows + own, :]
    wide_lane = lax.broadcasted_iota(jnp.int32, (count, count), 1)
    wide_row = lax.broadcasted_iota(jnp.int32, (count, count), 0)
    ridge = jnp.sum(jnp.where(wide_lane == wide_row, support, 0.0)) * (ridge_scale / count)
    system = support + jnp.where(wide_lane == wide_row, ridge, 0.0)
    system_ref[...] = system
    inverse_ref[...] = system
    rest_lane = lax.broadcasted_iota(jnp.int32, (count - BLOCK, count), 1)

    def one_block(step, carry):
        reduced = eliminate(inverse_ref[:BLOCK, :])
        below = inverse_ref[BLOCK:, :]
        below = jnp.where(rest_lane < BLOCK, 0.0, below) - exact_dot(below[:, :BLOCK], reduced)
        inverse_ref[: count - BLOCK, :] = pltpu.roll(below, count - BLOCK, 1)
        inverse_ref[count - BLOCK :, :] = pltpu.roll(reduced, count - BLOCK, 1)
        return carry

    lax.fori_loop(0, count // BLOCK, one_block, 0)
    alpha_ref[...] = solve_from(inverse_ref, system_ref, label_ref[...])


def weights_kernel(row_count, col_count, own, near, place_ref, gathered_ref, onehot_ref, *refs):
    system_ref, inverse_ref, alpha_ref, weight_ref, gamma_ref, loss_ref, big_ref, row_ref = refs
    row_index, col_index = place_ref[0], place_ref[1]
    count = row_count * col_count * own
    block = col_count * own
    cross = whole_matrix(1, row_count, col_count, own, near, gathered_ref, big_ref)
    alpha = alpha_ref[...]
    error = exact_dot(cross, alpha, 0, 0) - onehot_ref[...]
    loss_ref[...] = jnp.broadcast_to(0.5 * jnp.sum(error * error), loss_ref.shape)
    gamma = solve_from(inverse_ref, system_ref, exact_dot(cross, error))
    intersection = jnp.sum(gamma * alpha)
    row_ref[0] = alpha
    row_ref[1] = gamma
    row_ref[2] = error
    mine = pl.multiple_of((row_index * col_count + col_index) * own, own)
    gamma_ref[...] = row_ref[1, pl.ds(mine, own), :]

    def rows_here(which):
        starts = [pl.multiple_of((r2 * col_count + col_index) * own, own) for r2 in range(row_count)]
        return jnp.concatenate([row_ref[which, pl.ds(start, own), :] for start in starts], axis=0)

    def columns_here(which):
        here = row_ref[which, pl.ds(pl.multiple_of(row_index * block, block), block), :]
        return jnp.concatenate([here, here], axis=0)

    alpha_rows, gamma_rows = rows_here(0), rows_here(1)
    pair = -exact_dot(gamma_rows, columns_here(0), 1, 1) - exact_dot(alpha_rows, columns_here(1), 1, 1)
    target = exact_dot(alpha_rows, columns_here(2), 1, 1)
    u = lax.broadcasted_iota(jnp.int32, pair.shape, 0)
    v = lax.broadcasted_iota(jnp.int32, pair.shape, 1)
    same = (u // own == row_index) & (v % block == col_index * own + u % own)
    pair = pair - jnp.where(same, intersection * (2.0 * ridge_scale / count), 0.0)
    total = None
    for kind, part in enumerate((pair, target)):
        turned = pltpu.roll(part, (LANES - own * col_index) % LANES, 1)
        turned = jnp.where(v < block, turned, 0.0)
        back = exact_dot(turned, sorting(kind, col_count, own, near), 1, 1)
        total = back if total is None else total + back
    weight_ref[...] = total


def invert_in_kernel(gathered, row_count, col_count, own, near):
    f32 = jnp.float32
    count = row_count * col_count * own
    vmem = pl.BlockSpec(memory_space=pltpu.VMEM)
    square = jax.ShapeDtypeStruct((count, count), f32)
    return pl.pallas_call(
        lambda *refs: invert_kernel(row_count, col_count, own, near, *refs),
        out_shape=[square, square, jax.ShapeDtypeStruct((count, LANES), f32)],
        in_specs=[vmem],
        out_specs=[vmem] * 3,
        scratch_shapes=[
            pltpu.VMEM((row_count, count, LANES), f32),
            pltpu.VMEM((count, LANES), f32),
        ],
        name="invert",
    )(gathered)


def weights_in_kernel(gathered, onehot, solved, row_index, col_index, row_count, col_count, own, near):
    f32 = jnp.float32
    count = row_count * col_count * own
    vmem = pl.BlockSpec(memory_space=pltpu.VMEM)
    return pl.pallas_call(
        lambda *refs: weights_kernel(row_count, col_count, own, near, *refs),
        out_shape=[
            jax.ShapeDtypeStruct((row_count * own, LANES), f32),
            jax.ShapeDtypeStruct((own, LANES), f32),
            jax.ShapeDtypeStruct((SUBLANES, LANES), f32),
        ],
        in_specs=[pl.BlockSpec(memory_space=pltpu.SMEM)] + [vmem] * 5,
        out_specs=[vmem] * 3,
        scratch_shapes=[
            pltpu.VMEM((row_count, count, LANES), f32),
            pltpu.VMEM((3, count, LANES), f32),
        ],
        name="weights",
    )(jnp.stack([row_index, col_index]).astype(jnp.int32), gathered, onehot, *solved)


def solve_with(factor, rhs):
    halfway = lax.linalg.triangular_solve(factor, rhs, left_side=True, lower=True)
    return lax.linalg.triangular_solve(factor, halfway, left_side=True, lower=True, transpose_a=True)


def solve_plainly(gathered, onehot, row_index, col_index, row_count, col_count, own, near):
    count = row_count * col_count * own
    rows = row_count * own
    block = 2 * col_count * own
    labels = gathered[:, rows : rows + own].reshape(count, LANES)
    kernels, sorts = [], []
    for kind in range(2):
        j = jnp.arange(block // 2, dtype=jnp.int32)[None, :]
        lanes = lane_of(kind, j // own, j % own, col_count, own, near)
        sort = (jnp.arange(LANES, dtype=jnp.int32)[:, None] == lanes).astype(jnp.float32)
        sorts.append(sort)
        picked = jnp.dot(gathered[:, :rows].reshape(-1, LANES), sort, precision=highest)
        picked = picked.reshape(row_count, col_count, row_count, own, block // 2)
        picked = jnp.stack(
            [jnp.roll(picked[:, c], c * own, axis=-1) for c in range(col_count)], axis=1
        )
        kernels.append(jnp.transpose(picked, (2, 1, 3, 0, 4)).reshape(count, count))
    identity = jnp.eye(count, dtype=jnp.float32)
    ridge = jnp.trace(kernels[0]) * (ridge_scale / count)
    factor = jnp.linalg.cholesky(kernels[0] + ridge * identity)
    alpha = solve_with(factor, labels)
    error = jnp.dot(kernels[1].T, alpha, precision=highest) - onehot
    gamma = solve_with(factor, jnp.dot(kernels[1], error, precision=highest))
    intersection = jnp.sum(gamma * alpha)
    values = jnp.stack([alpha, gamma, error]).reshape(3, row_count, col_count, own, LANES)
    here = lax.dynamic_index_in_dim(values, col_index, 2, keepdims=False).reshape(3, rows, LANES)
    there = lax.dynamic_index_in_dim(values, row_index, 1, keepdims=False)
    there = lax.dynamic_slice_in_dim(
        jnp.concatenate([there, there], axis=1), col_index, col_count, 1
    ).reshape(3, -1, LANES)

    def outer(a, b):
        return jnp.dot(a, b.T, precision=highest)

    pair = -outer(here[1], there[0]) - outer(here[0], there[1])
    u, v = jnp.arange(rows)[:, None], jnp.arange(block // 2)[None, :]
    same = (u // own == row_index) & (v == u % own)
    pair = pair - jnp.where(same, intersection * (2.0 * ridge_scale / count), 0.0)
    weights = outer(pair, sorts[0]) + outer(outer(here[0], there[2]), sorts[1])
    mine = (row_index * col_count + col_index) * own
    return (
        weights,
        lax.dynamic_slice_in_dim(gamma, mine, own, 0),
        jnp.full((SUBLANES, LANES), 0.5 * jnp.sum(error * error)),
    )


def body(support_views, support_pick, target_views, target_pick, support_labels, target_labels):
    own, _, channels, pixels = support_views.shape
    side = math.isqrt(pixels)
    classes = support_labels.shape[1]
    row_count = lax.axis_size("row")
    col_count = lax.axis_size("col")
    row_index = lax.axis_index("row")
    col_index = lax.axis_index("col")
    own_support = choose_view(support_views, support_pick)
    own_target = choose_view(target_views, target_pick)

    both = jnp.stack([own_support, own_target]).reshape(2 * own, channels, side, side)
    chunk = jnp.transpose(both, (1, 2, 0, 3)).reshape(channels, side, 2 * own * side)
    chunks = [chunk]
    for d in range(1, col_count):
        pairs = [((i + d) % col_count, i) for i in range(col_count)]
        chunks.append(lax.ppermute(chunk, "col", pairs))
    near = 1 if own % (LANES // side) == 0 else LANES // side
    middle = own * side
    v_rows = [
        jnp.concatenate(chunks[:near], axis=-1) if near > 1 else chunk,
        jnp.concatenate([part[..., :middle] for part in chunks[near:]], axis=-1),
        jnp.concatenate([part[..., middle:] for part in chunks[near:]], axis=-1),
    ]
    v_rows = [part.reshape(channels, side, -1, LANES) for part in v_rows]

    row_images = lax.all_gather(own_support, "row", axis=0, tiled=True)
    groups = row_images.shape[0] // SUBLANES
    narrow = jnp.transpose(
        row_images.reshape(groups, SUBLANES, channels, side, side), (2, 3, 0, 1, 4)
    )
    devices = row_count * col_count
    labels = jnp.pad(support_labels, ((0, 0), (0, LANES - classes)))
    lanes = jnp.arange(LANES, dtype=jnp.int32)[None, :]
    onehot = jnp.where(
        lanes < classes, (target_labels[:, None] == lanes).astype(jnp.float32) - 1.0 / classes, 0.0
    )

    def to_all(parcel):
        copies = jnp.broadcast_to(parcel[None], (devices,) + parcel.shape)
        return lax.all_to_all(copies, AXES, 0, 0, tiled=True)

    rows, tile = narrow, None
    batches, tiles = [], []
    first = 0
    for columns in v_rows:
        rows, tile, angles, roots = pair_forward(rows, columns, first, tile)
        batches.append((angles, roots, columns))
        tiles.append(tile)
        first += columns.shape[2]
    sizes = (row_count, col_count, own, near)
    if own == SUBLANES and 2 * col_count * own == LANES and row_count % 2 == 0:
        support_tiles = to_all(jnp.concatenate([tiles[1], labels], axis=0))
        target_tiles = to_all(tiles[2])
        solved = invert_in_kernel(support_tiles, *sizes)
        weights, gamma_own, loss = weights_in_kernel(
            target_tiles, onehot, solved, row_index, col_index, *sizes
        )
    else:
        gathered = to_all(jnp.concatenate([tiles[2], labels], axis=0))
        weights, gamma_own, loss = solve_plainly(gathered, onehot, row_index, col_index, *sizes)
    if own == SUBLANES:
        support_grad, *others = pair_backward(row_index, weights, rows, batches)
        for k, there in enumerate(others, 1):
            pairs = [(i, (i + k) % row_count) for i in range(row_count)]
            support_grad = support_grad + lax.ppermute(there, "row", pairs)
        support_grad = jnp.transpose(support_grad, (2, 1, 0, 3))
    else:
        grads = jnp.stack(pair_backward(jnp.zeros(1, jnp.int32), weights, rows, batches))
        grads = jnp.transpose(grads, (0, 3, 2, 1, 4)).reshape(row_count * own, channels, pixels)
        support_grad = lax.psum_scatter(grads, "row", scatter_dimension=0, tiled=True)
    support_grad = support_grad.reshape(own, channels, pixels)
    return (support_grad, gamma_own[:, :classes], loss[0, 0])


def solution(mesh):
    return jax.shard_map(
        body,
        mesh=mesh,
        in_specs=(
            P(AXES, None, None, None),
            P(AXES),
            P(AXES, None, None, None),
            P(AXES),
            P(AXES, None),
            P(),
        ),
        out_specs=(P(AXES, None, None), P(AXES, None), P()),
        check_vma=False,
    )
```

```python
import math

import jax
import jax.numpy as jnp
from jax import lax
from jax.experimental import pallas as pl
from jax.experimental.pallas import tpu as pltpu
from jax.sharding import PartitionSpec as P

LAYERS = 3
LANES = 128
SUBLANES = 8
PART = 8
FORWARD_PART = 7
BLOCK = 64
ROWS = 2
RING = 8

bias_variance = 0.1
ridge_scale = 0.1
highest = lax.Precision.HIGHEST
tiny = 1e-30
PI = math.pi

ACOS = (
    2.20239957601501,
    -0.9079020788090617,
    0.36298714579028,
    -0.09949097018131615,
    0.012802548128944304,
)
SINE = (
    0.31830981148327425,
    0.032252498831491,
    0.001158328114192081,
    2.2834735017183973e-05,
)
AXES = ("row", "col")


def horner(coefficients, x):
    total = coefficients[-1] * x + coefficients[-2]
    for coefficient in coefficients[-3::-1]:
        total = total * x + coefficient
    return total


def choose_view(views, picked):
    options = jnp.arange(views.shape[1], dtype=jnp.int32)
    selector = (picked[:, None] == options[None, :]).astype(jnp.float32)
    return jnp.sum(selector[:, :, None, None] * views, axis=1)


def edges(side, shape):
    x = lax.broadcasted_iota(jnp.int32, shape, len(shape) - 1) % side
    return x > 0, x < side - 1


def across(surface, masks):
    axis = surface.ndim - 1
    left = jnp.where(masks[0], pltpu.roll(surface, 1, axis), 0.0)
    right = jnp.where(masks[1], pltpu.roll(surface, LANES - 1, axis), 0.0)
    return surface + left + right


def map_scale(channels, layer):
    return 9.0 * channels if layer == 0 else 9.0


class PerLayer:
    def __init__(self, refs):
        self.refs = refs
        self.shape = (len(refs),) + refs[0].shape

    def __getitem__(self, at):
        return self.refs[at[0]][at[1:]]

    def __setitem__(self, at, value):
        self.refs[at[0]][at[1:]] = value


def forward_kernel(side, channels, groups, packs, first, *refs):
    if first == 0:
        narrow_ref, v_ref = refs[:2]
        u_ref, *u_map_refs = refs[2 : 3 + LAYERS]
        u_sums_ref = PerLayer(refs[-LAYERS:])
        outs = refs[3 + LAYERS : -LAYERS]
    else:
        u_ref, v_ref = refs[:2]
        u_map_refs = refs[2 : 2 + LAYERS]
        past_ref = refs[2 + LAYERS]
        outs = refs[3 + LAYERS :]
    angle_refs = outs[:LAYERS]
    root_refs = outs[LAYERS : 2 * LAYERS]
    tile_ref = outs[2 * LAYERS]
    total_ref, inverse_ref = outs[2 * LAYERS + 1 : 2 * LAYERS + 3]
    sums_ref = PerLayer(outs[2 * LAYERS + 3 : 3 * LAYERS + 3])
    own_sums_ref = PerLayer(outs[3 * LAYERS + 3 : 4 * LAYERS + 3])
    step = pl.program_id(0)
    steps = side // ROWS
    masks = edges(side, (SUBLANES, LANES))
    own_masks = edges(side, (packs, LANES))
    width = packs if packs <= PART else FORWARD_PART
    blocks = [range(start, min(start + width, packs)) for start in range(0, packs, width)]

    def slot(row):
        return row & (RING - 1)

    def spread(line):
        return jnp.broadcast_to(line, (SUBLANES, LANES))

    if first == 0:

        @pl.when(step == 0)
        def _():
            for layer in range(LAYERS):
                u_sums_ref[layer, RING - 1] = jnp.zeros(u_sums_ref.shape[2:], jnp.float32)

        for layer in range(LAYERS):

            @pl.when(step == steps + layer)
            def _(layer=layer):
                u_sums_ref[layer, slot(side)] = jnp.zeros(u_sums_ref.shape[2:], jnp.float32)

        @pl.when(step < steps)
        def _():
            for r in range(ROWS):
                for g in range(groups):
                    energy = None
                    for c in range(channels):
                        plane = jnp.concatenate([narrow_ref[c, r, g]] * (LANES // side), axis=-1)
                        u_ref[c, r, g] = plane
                        energy = plane * plane if energy is None else energy + plane * plane
                    u_sums_ref[0, slot(step * ROWS + r), g] = across(energy, masks)

    def row_maps(layer):
        scale = map_scale(channels, layer)
        for r in range(ROWS):
            row = (step - 1 - layer) * ROWS + r
            for g in range(groups):
                total = (
                    u_sums_ref[layer, slot(row - 1), g]
                    + u_sums_ref[layer, slot(row), g]
                    + u_sums_ref[layer, slot(row + 1), g]
                )
                current = total * (1.0 / scale) + bias_variance
                inverse = lax.rsqrt(current)
                u_map_refs[layer][r, 0, g] = inverse * (1.0 / scale)
                u_map_refs[layer][r, 1, g] = current * inverse * (1.0 / PI)
                if layer + 1 < LAYERS:
                    u_sums_ref[layer + 1, slot(row), g] = across(current, masks)

    @pl.when(step == 0)
    def _():
        total_ref[...] = jnp.zeros(total_ref.shape, jnp.float32)
        for layer in range(LAYERS):
            sums_ref[layer, RING - 1] = jnp.zeros(sums_ref.shape[2:], jnp.float32)
            own_sums_ref[layer, RING - 1] = jnp.zeros(own_sums_ref.shape[2:], jnp.float32)

    for layer in range(LAYERS):

        @pl.when(step == steps + layer)
        def _(layer=layer):
            sums_ref[layer, slot(side)] = jnp.zeros(sums_ref.shape[2:], jnp.float32)
            own_sums_ref[layer, slot(side)] = jnp.zeros(own_sums_ref.shape[2:], jnp.float32)

    def product_stage(block):
        for r in range(ROWS):
            where = slot(step * ROWS + r)
            if block is blocks[0]:
                energy = None
                for c in range(channels):
                    plane = v_ref[c, r]
                    energy = plane * plane if energy is None else energy + plane * plane
                own_sums_ref[0, where] = across(energy, own_masks)
            for pack in block:
                lines = [spread(v_ref[c, r, pack : pack + 1, :]) for c in range(channels)]
                for g in range(groups):
                    product = None
                    for c in range(channels):
                        part = u_ref[c, r, g] * lines[c]
                        product = part if product is None else product + part
                    sums_ref[0, where, pack * groups + g] = across(product, masks)

    def arc_stage(layer, block):
        if first == 0:
            row_maps(layer)
        scale = map_scale(channels, layer)
        offset = scale * bias_variance
        rows = [(step - 1 - layer) * ROWS + r for r in range(ROWS)]
        near = [slot(rows[0] + r) for r in range(-1, ROWS + 1)]
        inverses, roots = [], []
        for r in range(ROWS if block is blocks[0] else 0):
            own_total = own_sums_ref[layer, near[r]] + own_sums_ref[layer, near[r + 1]] + own_sums_ref[layer, near[r + 2]]
            own_map = own_total * (1.0 / scale) + bias_variance
            inverse = lax.rsqrt(own_map)
            inverses.append(inverse)
            roots.append(own_map * inverse)
            root_refs[layer][r] = roots[r]
            inverse_ref[layer, r] = inverse
            if layer + 1 < LAYERS:
                own_sums_ref[layer + 1, near[r + 1]] = across(own_map, own_masks)
        if block is not blocks[0]:
            inverses = [inverse_ref.at[layer, r] for r in range(ROWS)]
            roots = [root_refs[layer].at[r] for r in range(ROWS)]
        for pack in block:
            for g in range(groups):
                at = pack * groups + g
                for r in range(0, ROWS, 2):
                    lines = [sums_ref[layer, near[r + k], at] for k in range(4)]
                    middle = (lines[1] + lines[2]) + offset
                    for k, summed in enumerate((lines[0] + middle, middle + lines[3])):
                        right_inverse = spread(inverses[r + k][pack : pack + 1, :])
                        right_root = spread(roots[r + k][pack : pack + 1, :])
                        cosine = summed * u_map_refs[layer][r + k, 0, g] * right_inverse
                        gap = 1.0 - (jnp.abs(cosine) if layer == 0 else cosine)
                        gap = jnp.maximum(gap, tiny)
                        root = gap * lax.rsqrt(gap)
                        rest = 2.0 - gap
                        rest = rest * lax.rsqrt(rest)
                        sine = root * rest
                        theta = root * horner(ACOS, rest)
                        angle = PI - theta
                        if layer == 0:
                            angle = jnp.where(cosine >= 0.0, angle, theta)
                        angle_refs[layer][r + k, at] = angle
                        value = (cosine * angle + sine) * u_map_refs[layer][r + k, 1, g] * right_root
                        if layer + 1 < LAYERS:
                            sums_ref[layer + 1, near[r + k + 1], at] = across(value, masks)
                        else:
                            total_ref[at] += value

    for block in blocks:
        pl.when(step < steps)(lambda block=block: product_stage(block))
    for layer in range(LAYERS):
        for block in blocks:
            pl.when((step > layer) & (step <= steps + layer))(
                lambda layer=layer, block=block: arc_stage(layer, block)
            )

    @pl.when(step == steps + LAYERS - 1)
    def _():
        lane = lax.broadcasted_iota(jnp.int32, (LANES, LANES), 1)
        from_lane = lax.broadcasted_iota(jnp.int32, (LANES, LANES), 0)
        copies = LANES // side
        folding = jnp.where(lane % copies == from_lane // side, 1.0 / (side * side), 0.0)
        means = jnp.dot(total_ref[...].reshape(-1, LANES), folding, precision=highest)
        place = lax.broadcasted_iota(jnp.int32, (SUBLANES, LANES), 1) // copies
        for g in range(groups):
            mine = slice(g * SUBLANES, (g + 1) * SUBLANES)
            line = jnp.zeros((SUBLANES, LANES), jnp.float32) if first == 0 else past_ref[mine, :]
            for pack in range(packs):
                at = (pack * groups + g) * SUBLANES
                line = jnp.where(place == first + pack, means[at : at + SUBLANES], line)
            tile_ref[mine, :] = line


def pair_forward(rows, v_rows, first, tile):
    channels, side, groups = (rows if first == 0 else rows[0]).shape[:3]
    packs = v_rows.shape[2]
    steps = side // ROWS
    count = packs * groups
    f32 = jnp.float32

    def lag(layer, trailing):
        return lambda i: (jnp.clip(i - 1 - layer, 0, steps - 1),) + (0,) * trailing

    def now(trailing):
        return lambda i: (0, jnp.minimum(i, steps - 1)) + (0,) * trailing

    image = pl.BlockSpec((channels, ROWS, groups, SUBLANES, LANES), now(3))
    maps = [pl.BlockSpec((ROWS, 2, groups, SUBLANES, LANES), lag(layer, 4)) for layer in range(LAYERS)]
    column = pl.BlockSpec((channels, ROWS, packs, LANES), now(2))
    whole = pl.BlockSpec((groups * SUBLANES, LANES), lambda i: (0, 0))
    out_shape = (
        [jax.ShapeDtypeStruct((side, count, SUBLANES, LANES), f32)] * LAYERS
        + [jax.ShapeDtypeStruct((side, packs, LANES), f32)] * LAYERS
        + [jax.ShapeDtypeStruct((groups * SUBLANES, LANES), f32)]
    )
    out_specs = (
        [pl.BlockSpec((ROWS, count, SUBLANES, LANES), lag(layer, 3)) for layer in range(LAYERS)]
        + [pl.BlockSpec((ROWS, packs, LANES), lag(layer, 2)) for layer in range(LAYERS)]
        + [whole]
    )
    scratch_shapes = [
        pltpu.VMEM((count, SUBLANES, LANES), f32),
        pltpu.VMEM((LAYERS, ROWS, packs, LANES), f32),
    ]
    scratch_shapes += [pltpu.VMEM((RING, count, SUBLANES, LANES), f32)] * LAYERS
    scratch_shapes += [pltpu.VMEM((RING, packs, LANES), f32)] * LAYERS
    if first == 0:
        operands = [rows, v_rows]
        in_specs = [pl.BlockSpec((channels, ROWS, groups, SUBLANES, side), now(3)), column]
        out_shape = (
            [jax.ShapeDtypeStruct((channels, side, groups, SUBLANES, LANES), f32)]
            + [jax.ShapeDtypeStruct((side, 2, groups, SUBLANES, LANES), f32)] * LAYERS
            + out_shape
        )
        out_specs = [image] + maps + out_specs
        scratch_shapes += [pltpu.VMEM((RING, groups, SUBLANES, LANES), f32)] * LAYERS
    else:
        operands = [rows[0], v_rows, *rows[1:], tile]
        in_specs = [image, column] + maps + [whole]
    results = pl.pallas_call(
        lambda *refs: forward_kernel(side, channels, groups, packs, first, *refs),
        out_shape=out_shape,
        grid=(steps + LAYERS,),
        in_specs=in_specs,
        out_specs=out_specs,
        scratch_shapes=scratch_shapes,
        name="pair_forward",
    )(*operands)
    if first == 0:
        rows, results = results[: 1 + LAYERS], results[1 + LAYERS :]
    return rows, results[-1], results[:LAYERS], results[LAYERS : 2 * LAYERS]


def backward_kernel(side, channels, groups, packs, *refs):
    turn_ref, weight_ref, u_ref = refs[:3]
    u_map_refs = refs[3 : 3 + LAYERS]
    taken = 3 + LAYERS
    angle_refs, root_refs, image_refs = [], [], []
    for batch in range(len(packs)):
        angle_refs.append(refs[taken : taken + LAYERS])
        root_refs.append(refs[taken + LAYERS : taken + 2 * LAYERS])
        image_refs.append(refs[taken + 2 * LAYERS])
        taken += 2 * LAYERS + 1
    grad_refs = refs[taken : taken + groups]
    wide_ref, total_ref = refs[taken + groups : taken + groups + 2]
    taken += groups + 2
    sums_ref = PerLayer(refs[taken : taken + LAYERS])
    own_sums_ref = PerLayer(refs[taken + LAYERS :])
    parts = [(batch, pack) for batch in range(len(packs)) for pack in range(packs[batch])]
    blocks = [
        list(enumerate(parts))[start : start + PART] for start in range(0, len(parts), PART)
    ]
    step = pl.program_id(0)
    steps = side // ROWS
    masks = edges(side, (SUBLANES, LANES))
    shrink = 1.0 / (9.0 * PI)
    pixels = side * side

    def slot(row):
        return row & (RING - 1)

    def fold(total):
        total = total + pltpu.roll(total, 2 * side, 1)
        return total + pltpu.roll(total, side, 1)

    def spread(line):
        return jnp.broadcast_to(line, (SUBLANES, LANES))

    def summed(ref, depth, row, at):
        lines = [ref[depth, slot(row + k), at] for k in range(-1, ROWS + 1)]
        totals = []
        for r in range(0, ROWS, 2):
            middle = lines[r + 1] + lines[r + 2]
            totals += [lines[r] + middle, middle + lines[r + 3]]
        return totals

    def add(total, part):
        return part if total is None else total + part

    @pl.when(step == 0)
    def _():
        lane = lax.broadcasted_iota(jnp.int32, (SUBLANES, LANES), 1)
        for pack in range(len(parts)):
            index = lane // side + pack * (LANES // side)
            for g in range(groups):
                line = weight_ref[g * SUBLANES : (g + 1) * SUBLANES, :]
                wide_ref[pack * groups + g] = jnp.take_along_axis(line, index, axis=1)
        for depth in range(LAYERS):
            sums_ref[depth, RING - 1] = jnp.zeros(sums_ref.shape[2:], jnp.float32)
            own_sums_ref[depth, RING - 1] = jnp.zeros(own_sums_ref.shape[2:], jnp.float32)

    for depth in range(LAYERS):

        @pl.when(step == steps + depth)
        def _(depth=depth):
            sums_ref[depth, slot(side)] = jnp.zeros(sums_ref.shape[2:], jnp.float32)
            own_sums_ref[depth, slot(side)] = jnp.zeros(own_sums_ref.shape[2:], jnp.float32)

    def layer_block(depth, block):
        layer = LAYERS - 1 - depth
        row = (step - depth) * ROWS
        totals = [[None] * groups for _ in range(ROWS)]
        for part, (batch, pack) in blocks[block]:
            for g in range(groups):
                inner = pack * groups + g
                at = part * groups + g
                if depth == 0:
                    grads = [wide_ref[at]] * ROWS
                else:
                    grads = summed(sums_ref, depth - 1, row, at)
                for r, grad in enumerate(grads):
                    angle = angle_refs[batch][layer][r, inner]
                    sums_ref[depth, slot(row + r), at] = across(grad * angle, masks)
                    product = angle * (PI - angle)
                    root = spread(root_refs[batch][layer][r, pack : pack + 1, :])
                    totals[r][g] = add(totals[r][g], grad * root * (product * horner(SINE, product)))
        for r in range(ROWS):
            for g in range(groups):
                total = totals[r][g]
                total_ref[depth, r, g] = total if block == 0 else total_ref[depth, r, g] + total

    def layer_end(depth):
        layer = LAYERS - 1 - depth
        row = (step - depth) * ROWS
        factor = shrink**depth / (pixels * 2.0 * PI * PI)
        for g in range(groups):
            above = summed(own_sums_ref, depth - 1, row, g) if depth > 0 else None
            for r in range(ROWS):
                carry = fold(total_ref[depth, r, g]) * (factor / u_map_refs[layer][r, 1, g])
                if depth > 0:
                    carry = carry + above[r] * (1.0 / 9.0)
                own_sums_ref[depth, slot(row + r), g] = across(carry, masks)

    def image_block(block):
        row = (step - LAYERS) * ROWS
        totals = [[[None] * groups for _ in range(channels)] for _ in range(ROWS)]
        for part, (batch, pack) in blocks[block]:
            for g in range(groups):
                at = part * groups + g
                for r, grad in enumerate(summed(sums_ref, LAYERS - 1, row, at)):
                    for c in range(channels):
                        line = spread(image_refs[batch][c, r, pack : pack + 1, :])
                        totals[r][c][g] = add(totals[r][c][g], grad * line)
        for r in range(ROWS):
            for c in range(channels):
                for g in range(groups):
                    total, at = totals[r][c][g], LAYERS + c
                    total_ref[at, r, g] = total if block == 0 else total_ref[at, r, g] + total

    def image_end():
        row = (step - LAYERS) * ROWS
        copies = LANES // side
        lane = lax.broadcasted_iota(jnp.int32, (SUBLANES, LANES), 1)
        for k in range(groups):
            g = lax.rem(turn_ref[0] + k, groups)
            above = summed(own_sums_ref, LAYERS - 1, row, g)
            for r in range(ROWS):
                carry = above[r] * (2.0 / (9.0 * channels))
                for c in range(channels):
                    image = fold(total_ref[LAYERS + c, r, g]) * (shrink**LAYERS / (pixels * channels))
                    image = image + carry * u_ref[c, r, g]
                    lines = grad_refs[k][0, c]
                    grad_refs[k][0, c] = jnp.where(lane // side == (row + r) % copies, image, lines)

    for depth in range(LAYERS):
        for block in range(len(blocks)):
            pl.when((step >= depth) & (step < steps + depth))(
                lambda depth=depth, block=block: layer_block(depth, block)
            )
        pl.when((step >= depth) & (step < steps + depth))(lambda depth=depth: layer_end(depth))
    for block in range(len(blocks)):
        pl.when(step >= LAYERS)(lambda block=block: image_block(block))
    pl.when(step >= LAYERS)(image_end)


def pair_backward(turn, weights, rows, batches):
    channels, side, groups = rows[0].shape[:3]
    packs = [images.shape[2] for _, _, images in batches]
    steps = side // ROWS
    copies = LANES // side
    f32 = jnp.float32

    def at_lag(lag, trailing):
        return lambda i: (jnp.clip(i - lag, 0, steps - 1),) + (0,) * trailing

    def image_rows(trailing):
        return lambda i: (0, jnp.clip(i - LAYERS, 0, steps - 1)) + (0,) * trailing

    operands = [turn.astype(jnp.int32).reshape(1), weights, *rows]
    in_specs = [
        pl.BlockSpec(memory_space=pltpu.SMEM),
        pl.BlockSpec(weights.shape, lambda i: (0, 0)),
        pl.BlockSpec((channels, ROWS, groups, SUBLANES, LANES), image_rows(3)),
    ] + [
        pl.BlockSpec((ROWS, 2, groups, SUBLANES, LANES), at_lag(LAYERS - 1 - layer, 4))
        for layer in range(LAYERS)
    ]
    for (angles, roots, images), width in zip(batches, packs):
        for layer in range(LAYERS):
            operands.append(angles[layer])
            in_specs.append(
                pl.BlockSpec((ROWS, width * groups, SUBLANES, LANES), at_lag(LAYERS - 1 - layer, 3))
            )
        for layer in range(LAYERS):
            operands.append(roots[layer])
            in_specs.append(pl.BlockSpec((ROWS, width, LANES), at_lag(LAYERS - 1 - layer, 2)))
        operands.append(images)
        in_specs.append(pl.BlockSpec((channels, ROWS, width, LANES), image_rows(2)))
    count = sum(packs) * groups
    return pl.pallas_call(
        lambda *refs: backward_kernel(side, channels, groups, packs, *refs),
        out_shape=[jax.ShapeDtypeStruct((side // copies, channels, SUBLANES, LANES), f32)] * groups,
        grid=(steps + LAYERS,),
        in_specs=in_specs,
        out_specs=[
            pl.BlockSpec(
                (1, channels, SUBLANES, LANES),
                lambda i: (jnp.clip(i - LAYERS, 0, steps - 1) * ROWS // copies, 0, 0, 0),
            )
        ]
        * groups,
        scratch_shapes=[
            pltpu.VMEM((count, SUBLANES, LANES), f32),
            pltpu.VMEM((LAYERS + channels, ROWS, groups, SUBLANES, LANES), f32),
        ]
        + [pltpu.VMEM((RING, count, SUBLANES, LANES), f32)] * LAYERS
        + [pltpu.VMEM((RING, groups, SUBLANES, LANES), f32)] * LAYERS,
        name="pair_backward",
    )(*operands)


def eliminate(panel):
    height, width = panel.shape
    tiles = [panel[:, start : start + LANES] for start in range(0, width, LANES)]
    lane = lax.broadcasted_iota(jnp.int32, tiles[0].shape, 1)
    row = lax.broadcasted_iota(jnp.int32, tiles[0].shape, 0)
    for j in range(0, height, 2):
        k = j + 1
        first = jnp.broadcast_to(tiles[0][:, j : j + 1], tiles[0].shape)
        second = jnp.broadcast_to(tiles[0][:, k : k + 1], tiles[0].shape)
        a, b, d = first[j : j + 1], first[k : k + 1], second[k : k + 1]
        scale = 1.0 / (a * d - b * b)
        a, b, d = a * scale, b * scale, d * scale
        for t, tile in enumerate(tiles):
            upper, lower = tile[j : j + 1], tile[k : k + 1]
            if t == 0:
                upper = jnp.where(lane[:1] == j, 1.0, jnp.where(lane[:1] == k, 0.0, upper))
                lower = jnp.where(lane[:1] == k, 1.0, jnp.where(lane[:1] == j, 0.0, lower))
                tile = jnp.where((lane == j) | (lane == k), 0.0, tile)
            upper, lower = d * upper - b * lower, a * lower - b * upper
            rest = tile - first * upper - second * lower
            tiles[t] = jnp.where(row == j, upper, jnp.where(row == k, lower, rest))
    return jnp.concatenate(tiles, axis=1)


def lane_of(kind, d, k, col_count, own, near):
    far = 2 * near * own + (kind * (col_count - near) + d - near) * own + k
    return jnp.where(d < near, (2 * d + kind) * own + k, far)


def sorting(kind, col_count, own, near):
    i = lax.broadcasted_iota(jnp.int32, (LANES, LANES), 0)
    j = lax.broadcasted_iota(jnp.int32, (LANES, LANES), 1) % (LANES // 2)
    return (i == lane_of(kind, j // own, j % own, col_count, own, near)).astype(jnp.float32)


def exact_dot(a, b, da=1, db=0):
    return lax.dot_general(
        a, b, (((da,), (db,)), ((), ())), precision=highest, preferred_element_type=jnp.float32
    )


def whole_matrix(kind, row_count, col_count, own, near, gathered_ref, big_ref):
    count = row_count * col_count * own
    rows = row_count * own
    half = LANES // 2
    for r in range(row_count):
        for c in range(col_count):
            tile = gathered_ref[r * col_count + c, :rows, :]
            for r2 in range(row_count):
                at = (c * row_count + r2) * own
                big_ref[r, at : at + own, :] = tile[r2 * own : (r2 + 1) * own]
    parts = exact_dot(
        big_ref[...].reshape(row_count * count, LANES), sorting(kind, col_count, own, near)
    ).reshape(row_count, count, LANES)
    lane = lax.broadcasted_iota(jnp.int32, (rows, LANES), 1)
    for c in range(col_count):
        for t in range(row_count // 2):
            even, odd = (
                pltpu.roll(part, own * c, 1) if c else part
                for part in (parts[2 * t, c * rows : (c + 1) * rows], parts[2 * t + 1, c * rows : (c + 1) * rows])
            )
            joined = jnp.where(lane < half, even, odd)
            for r2 in range(row_count):
                at = (r2 * col_count + c) * own
                big_ref[t, at : at + own, :] = joined[r2 * own : (r2 + 1) * own]
    return jnp.concatenate([big_ref[t] for t in range(row_count // 2)], axis=1)


def solve_from(inverse_ref, system_ref, right):
    first = exact_dot(inverse_ref[...], right)
    return first + exact_dot(inverse_ref[...], right - exact_dot(system_ref[...], first))


def invert_kernel(row_count, col_count, own, near, gathered_ref, *refs):
    system_ref, inverse_ref, alpha_ref, big_ref, label_ref = refs
    count = row_count * col_count * own
    rows = row_count * own
    support = whole_matrix(0, row_count, col_count, own, near, gathered_ref, big_ref)
    for source in range(row_count * col_count):
        label_ref[source * own : (source + 1) * own, :] = gathered_ref[source, rows : rows + own, :]
    wide_lane = lax.broadcasted_iota(jnp.int32, (count, count), 1)
    wide_row = lax.broadcasted_iota(jnp.int32, (count, count), 0)
    ridge = jnp.sum(jnp.where(wide_lane == wide_row, support, 0.0)) * (ridge_scale / count)
    system = support + jnp.where(wide_lane == wide_row, ridge, 0.0)
    system_ref[...] = system
    inverse_ref[...] = system
    rest_lane = lax.broadcasted_iota(jnp.int32, (count - BLOCK, count), 1)

    def one_block(step, carry):
        reduced = eliminate(inverse_ref[:BLOCK, :])
        below = inverse_ref[BLOCK:, :]
        below = jnp.where(rest_lane < BLOCK, 0.0, below) - exact_dot(below[:, :BLOCK], reduced)
        inverse_ref[: count - BLOCK, :] = pltpu.roll(below, count - BLOCK, 1)
        inverse_ref[count - BLOCK :, :] = pltpu.roll(reduced, count - BLOCK, 1)
        return carry

    lax.fori_loop(0, count // BLOCK, one_block, 0)
    alpha_ref[...] = solve_from(inverse_ref, system_ref, label_ref[...])


def weights_kernel(row_count, col_count, own, near, place_ref, gathered_ref, onehot_ref, *refs):
    system_ref, inverse_ref, alpha_ref, weight_ref, gamma_ref, loss_ref, big_ref, row_ref = refs
    row_index, col_index = place_ref[0], place_ref[1]
    count = row_count * col_count * own
    block = col_count * own
    cross = whole_matrix(1, row_count, col_count, own, near, gathered_ref, big_ref)
    alpha = alpha_ref[...]
    error = exact_dot(cross, alpha, 0, 0) - onehot_ref[...]
    loss_ref[...] = jnp.broadcast_to(0.5 * jnp.sum(error * error), loss_ref.shape)
    gamma = solve_from(inverse_ref, system_ref, exact_dot(cross, error))
    intersection = jnp.sum(gamma * alpha)
    row_ref[0] = alpha
    row_ref[1] = gamma
    row_ref[2] = error
    mine = pl.multiple_of((row_index * col_count + col_index) * own, own)
    gamma_ref[...] = row_ref[1, pl.ds(mine, own), :]

    def rows_here(which):
        starts = [pl.multiple_of((r2 * col_count + col_index) * own, own) for r2 in range(row_count)]
        return jnp.concatenate([row_ref[which, pl.ds(start, own), :] for start in starts], axis=0)

    def columns_here(which):
        here = row_ref[which, pl.ds(pl.multiple_of(row_index * block, block), block), :]
        return jnp.concatenate([here, here], axis=0)

    alpha_rows, gamma_rows = rows_here(0), rows_here(1)
    pair = -exact_dot(gamma_rows, columns_here(0), 1, 1) - exact_dot(alpha_rows, columns_here(1), 1, 1)
    target = exact_dot(alpha_rows, columns_here(2), 1, 1)
    u = lax.broadcasted_iota(jnp.int32, pair.shape, 0)
    v = lax.broadcasted_iota(jnp.int32, pair.shape, 1)
    same = (u // own == row_index) & (v % block == col_index * own + u % own)
    pair = pair - jnp.where(same, intersection * (2.0 * ridge_scale / count), 0.0)
    total = None
    for kind, part in enumerate((pair, target)):
        turned = pltpu.roll(part, (LANES - own * col_index) % LANES, 1)
        turned = jnp.where(v < block, turned, 0.0)
        back = exact_dot(turned, sorting(kind, col_count, own, near), 1, 1)
        total = back if total is None else total + back
    weight_ref[...] = total


def invert_in_kernel(gathered, row_count, col_count, own, near):
    f32 = jnp.float32
    count = row_count * col_count * own
    vmem = pl.BlockSpec(memory_space=pltpu.VMEM)
    square = jax.ShapeDtypeStruct((count, count), f32)
    return pl.pallas_call(
        lambda *refs: invert_kernel(row_count, col_count, own, near, *refs),
        out_shape=[square, square, jax.ShapeDtypeStruct((count, LANES), f32)],
        in_specs=[vmem],
        out_specs=[vmem] * 3,
        scratch_shapes=[
            pltpu.VMEM((row_count, count, LANES), f32),
            pltpu.VMEM((count, LANES), f32),
        ],
        name="invert",
    )(gathered)


def weights_in_kernel(gathered, onehot, solved, row_index, col_index, row_count, col_count, own, near):
    f32 = jnp.float32
    count = row_count * col_count * own
    vmem = pl.BlockSpec(memory_space=pltpu.VMEM)
    return pl.pallas_call(
        lambda *refs: weights_kernel(row_count, col_count, own, near, *refs),
        out_shape=[
            jax.ShapeDtypeStruct((row_count * own, LANES), f32),
            jax.ShapeDtypeStruct((own, LANES), f32),
            jax.ShapeDtypeStruct((SUBLANES, LANES), f32),
        ],
        in_specs=[pl.BlockSpec(memory_space=pltpu.SMEM)] + [vmem] * 5,
        out_specs=[vmem] * 3,
        scratch_shapes=[
            pltpu.VMEM((row_count, count, LANES), f32),
            pltpu.VMEM((3, count, LANES), f32),
        ],
        name="weights",
    )(jnp.stack([row_index, col_index]).astype(jnp.int32), gathered, onehot, *solved)


def solve_with(factor, rhs):
    halfway = lax.linalg.triangular_solve(factor, rhs, left_side=True, lower=True)
    return lax.linalg.triangular_solve(factor, halfway, left_side=True, lower=True, transpose_a=True)


def solve_plainly(gathered, onehot, row_index, col_index, row_count, col_count, own, near):
    count = row_count * col_count * own
    rows = row_count * own
    block = 2 * col_count * own
    labels = gathered[:, rows : rows + own].reshape(count, LANES)
    kernels, sorts = [], []
    for kind in range(2):
        j = jnp.arange(block // 2, dtype=jnp.int32)[None, :]
        lanes = lane_of(kind, j // own, j % own, col_count, own, near)
        sort = (jnp.arange(LANES, dtype=jnp.int32)[:, None] == lanes).astype(jnp.float32)
        sorts.append(sort)
        picked = jnp.dot(gathered[:, :rows].reshape(-1, LANES), sort, precision=highest)
        picked = picked.reshape(row_count, col_count, row_count, own, block // 2)
        picked = jnp.stack(
            [jnp.roll(picked[:, c], c * own, axis=-1) for c in range(col_count)], axis=1
        )
        kernels.append(jnp.transpose(picked, (2, 1, 3, 0, 4)).reshape(count, count))
    identity = jnp.eye(count, dtype=jnp.float32)
    ridge = jnp.trace(kernels[0]) * (ridge_scale / count)
    factor = jnp.linalg.cholesky(kernels[0] + ridge * identity)
    alpha = solve_with(factor, labels)
    error = jnp.dot(kernels[1].T, alpha, precision=highest) - onehot
    gamma = solve_with(factor, jnp.dot(kernels[1], error, precision=highest))
    intersection = jnp.sum(gamma * alpha)
    values = jnp.stack([alpha, gamma, error]).reshape(3, row_count, col_count, own, LANES)
    here = lax.dynamic_index_in_dim(values, col_index, 2, keepdims=False).reshape(3, rows, LANES)
    there = lax.dynamic_index_in_dim(values, row_index, 1, keepdims=False)
    there = lax.dynamic_slice_in_dim(
        jnp.concatenate([there, there], axis=1), col_index, col_count, 1
    ).reshape(3, -1, LANES)

    def outer(a, b):
        return jnp.dot(a, b.T, precision=highest)

    pair = -outer(here[1], there[0]) - outer(here[0], there[1])
    u, v = jnp.arange(rows)[:, None], jnp.arange(block // 2)[None, :]
    same = (u // own == row_index) & (v == u % own)
    pair = pair - jnp.where(same, intersection * (2.0 * ridge_scale / count), 0.0)
    weights = outer(pair, sorts[0]) + outer(outer(here[0], there[2]), sorts[1])
    mine = (row_index * col_count + col_index) * own
    return (
        weights,
        lax.dynamic_slice_in_dim(gamma, mine, own, 0),
        jnp.full((SUBLANES, LANES), 0.5 * jnp.sum(error * error)),
    )


def body(support_views, support_pick, target_views, target_pick, support_labels, target_labels):
    own, _, channels, pixels = support_views.shape
    side = math.isqrt(pixels)
    classes = support_labels.shape[1]
    row_count = lax.axis_size("row")
    col_count = lax.axis_size("col")
    row_index = lax.axis_index("row")
    col_index = lax.axis_index("col")
    own_support = choose_view(support_views, support_pick)
    own_target = choose_view(target_views, target_pick)

    both = jnp.stack([own_support, own_target]).reshape(2 * own, channels, side, side)
    chunk = jnp.transpose(both, (1, 2, 0, 3)).reshape(channels, side, 2 * own * side)
    chunks = [chunk]
    for d in range(1, col_count):
        pairs = [((i + d) % col_count, i) for i in range(col_count)]
        chunks.append(lax.ppermute(chunk, "col", pairs))
    near = 1 if own % (LANES // side) == 0 else LANES // side
    middle = own * side
    v_rows = [
        jnp.concatenate(chunks[:near], axis=-1) if near > 1 else chunk,
        jnp.concatenate([part[..., :middle] for part in chunks[near:]], axis=-1),
        jnp.concatenate([part[..., middle:] for part in chunks[near:]], axis=-1),
    ]
    v_rows = [part.reshape(channels, side, -1, LANES) for part in v_rows]

    row_images = lax.all_gather(own_support, "row", axis=0, tiled=True)
    groups = row_images.shape[0] // SUBLANES
    narrow = jnp.transpose(
        row_images.reshape(groups, SUBLANES, channels, side, side), (2, 3, 0, 1, 4)
    )
    devices = row_count * col_count
    labels = jnp.pad(support_labels, ((0, 0), (0, LANES - classes)))
    lanes = jnp.arange(LANES, dtype=jnp.int32)[None, :]
    onehot = jnp.where(
        lanes < classes, (target_labels[:, None] == lanes).astype(jnp.float32) - 1.0 / classes, 0.0
    )

    def to_all(parcel):
        copies = jnp.broadcast_to(parcel[None], (devices,) + parcel.shape)
        return lax.all_to_all(copies, AXES, 0, 0, tiled=True)

    rows, tile = narrow, None
    batches, tiles = [], []
    first = 0
    for columns in v_rows:
        rows, tile, angles, roots = pair_forward(rows, columns, first, tile)
        batches.append((angles, roots, columns))
        tiles.append(tile)
        first += columns.shape[2]
    sizes = (row_count, col_count, own, near)
    if own == SUBLANES and 2 * col_count * own == LANES and row_count % 2 == 0:
        support_tiles = to_all(jnp.concatenate([tiles[1], labels], axis=0))
        target_tiles = to_all(tiles[2])
        solved = invert_in_kernel(support_tiles, *sizes)
        weights, gamma_own, loss = weights_in_kernel(
            target_tiles, onehot, solved, row_index, col_index, *sizes
        )
    else:
        gathered = to_all(jnp.concatenate([tiles[2], labels], axis=0))
        weights, gamma_own, loss = solve_plainly(gathered, onehot, row_index, col_index, *sizes)
    if own == SUBLANES:
        support_grad, *others = pair_backward(row_index, weights, rows, batches)
        for k, there in enumerate(others, 1):
            pairs = [(i, (i + k) % row_count) for i in range(row_count)]
            support_grad = support_grad + lax.ppermute(there, "row", pairs)
        support_grad = jnp.transpose(support_grad, (2, 1, 0, 3))
    else:
        grads = jnp.stack(pair_backward(jnp.zeros(1, jnp.int32), weights, rows, batches))
        grads = jnp.transpose(grads, (0, 3, 2, 1, 4)).reshape(row_count * own, channels, pixels)
        support_grad = lax.psum_scatter(grads, "row", scatter_dimension=0, tiled=True)
    support_grad = support_grad.reshape(own, channels, pixels)
    return (support_grad, gamma_own[:, :classes], loss[0, 0])


def solution(mesh):
    return jax.shard_map(
        body,
        mesh=mesh,
        in_specs=(
            P(AXES, None, None, None),
            P(AXES),
            P(AXES, None, None, None),
            P(AXES),
            P(AXES, None),
            P(),
        ),
        out_specs=(P(AXES, None, None), P(AXES, None), P()),
        check_vma=False,
    )
```
